256 devices in a mesh: feat: 64 (over x, z, core), node: 4 (over y).
Axes of the slice: x: 4, y: 4, z: 8, core: 2. Of those that a mesh axis runs over, the one named last changes fastest.
Arguments:
- features: bfloat16 [32768, 1024], P(None, 'feat'), may hold values from -6 to 6
- w_self: bfloat16 [1024, 256], P('feat'), may hold values from -0.1875 to 0.1875
- w_neigh: bfloat16 [1024, 256], P('feat'), may hold values from -0.75 to 0.75
- bias: float32 [256], replicated, may hold values from -3 to 3
- d_out: bfloat16 [32768, 256], P(('node', 'feat')), may hold values from -6 to 6
- nbr_ids: int32 [256, 16], P('node'), may hold values from 0 to 255, as said below
- nbr_count: int32 [256], P('node'), may hold values from 1 to 16, as said below
- tiles: int32 [256, 16, 8, 128], P('node'), may hold values from 0 to 65535, as said below
Outputs:
- activated: bfloat16 [32768, 256], P(('node', 'feat'))
- grad_features: float32 [32768, 1024], P('node', 'feat')
- grad_self: float32 [1024, 256], P('feat')
- grad_neigh: float32 [1024, 256], P('feat')
The draws below stay inside these ranges and needn't reach their ends.
Inputs may be any that keep to these rules, and one draw needn't show every extreme that they name: `nbr_ids`: the ids of one block row are distinct; only the first nbr_count slots of a row are live, the others hold ids and tiles that must be ignored. `nbr_count`: some block row of every draw has exactly 16 live slots. `tiles`: bits for destination rows 128 and above are zero; some destination nodes have no edges at all.
All inputs are finite; a program needn't handle non-finite values.
Results may differ from the reference program's by a relative error of at most 0.0075.
Values may be sent and summed in bfloat16 or wider, within the bound.
A program may use at most 64 MiB of HBM per device.

```python
import math
import jax
import jax.numpy as jnp
from jax import lax

F = 1024
H = 256
BLK = 128
WORDS = 8
NBMAX = 16
BLOCKS_G = 64
NODES = 32768
NBLOCKS = 256


def draw_nbr_ids(key, part):
    scores = jax.random.randint(jax.random.fold_in(key, 11), (NBLOCKS, NBLOCKS), 0, 65536)
    scores = scores * NBLOCKS + jnp.arange(NBLOCKS, dtype=jnp.int32)[None, :]
    ordering = jnp.argsort(scores, axis=1, stable=True)
    return ordering[:, :NBMAX].astype(jnp.int32)


def draw_nbr_count(key, part):
    key_heavy, key_high, key_low, key_row = jax.random.split(jax.random.fold_in(key, 23), 4)
    groups = NBLOCKS // BLOCKS_G
    heavy_group = jax.random.randint(key_heavy, (), 0, groups)
    row_index = jnp.arange(NBLOCKS, dtype=jnp.int32)
    row_group = row_index // BLOCKS_G
    high_count = NBMAX - jax.random.randint(key_high, (NBLOCKS,), 0, max(NBMAX // 4, 1))
    low_count = jax.random.randint(key_low, (NBLOCKS,), 1, NBMAX // 2 + 1)
    counts = jnp.where(row_group == heavy_group, high_count, low_count)
    chosen_row = heavy_group * BLOCKS_G + jax.random.randint(key_row, (), 0, BLOCKS_G)
    counts = jnp.where(row_index == chosen_row, NBMAX, counts)
    return counts.astype(jnp.int32)


def draw_tiles(key, part):
    key_one, key_two, key_three, key_rows = jax.random.split(jax.random.fold_in(key, 37), 4)
    tile_shape = (NBLOCKS, NBMAX, WORDS, BLK)
    packed = jax.random.randint(key_one, tile_shape, 0, 2 ** 16)
    packed = jnp.bitwise_and(packed, jax.random.randint(key_two, tile_shape, 0, 2 ** 16))
    packed = jnp.bitwise_and(packed, jax.random.randint(key_three, tile_shape, 0, 2 ** 16))
    active = (jax.random.randint(key_rows, (NBLOCKS, BLK), 0, 20) != 0).astype(jnp.int32)
    padded = jnp.pad(active, ((0, 0), (0, WORDS * 16 - BLK))).reshape(NBLOCKS, WORDS, 16)
    shifts = jnp.arange(16, dtype=jnp.int32)
    row_words = jnp.sum(jnp.left_shift(padded, shifts), axis=-1).astype(jnp.int32)
    return jnp.bitwise_and(packed, row_words[:, None, :, None]).astype(jnp.int32)


def block_scale(rng, extent, cuts, least, largest):
    level, own = 1.0, jax.random.fold_in(rng, 6)
    for dim, blocks in cuts:
        steps = jnp.exp(jax.random.uniform(jax.random.fold_in(own, dim), (blocks,), jnp.float32, least / len(cuts), largest / len(cuts)))
        level = level * jnp.repeat(steps, extent[dim] // blocks).reshape([-1 if axis == dim else 1 for axis in range(len(extent))])
    return level


def scatter_about(rng, extent, scale, limit, shards=(), kind=jnp.bfloat16):
    array = scale * jax.random.normal(rng, extent, jnp.float32)
    if shards:
        array = array * block_scale(rng, extent, shards, -0.22, 0.18)
    return jnp.clip(array, -limit, limit).astype(kind)


def setup_inputs(seed: int = 0) -> dict:
    arg_keys = jax.random.split(jax.random.key(seed), 9)
    return {
        "features": scatter_about(arg_keys[0], (NODES, F), 1.0, 6.0, ((1, 64),)),
        "w_self": scatter_about(arg_keys[1], (F, H), F ** -0.5, 0.1875, ((0, 64),)),
        "w_neigh": scatter_about(arg_keys[2], (F, H), (F // 16) ** -0.5, 0.75, ((0, 64),)),
        "bias": scatter_about(arg_keys[3], (H,), 0.5, 3.0, (), jnp.float32),
        "d_out": scatter_about(arg_keys[4], (NODES, H), 1.0, 6.0, ((0, 256),)),
        "nbr_ids": draw_nbr_ids(jax.random.fold_in(arg_keys[8], 71), 0),
        "nbr_count": draw_nbr_count(jax.random.fold_in(arg_keys[8], 71), 0),
        "tiles": draw_tiles(jax.random.fold_in(arg_keys[8], 71), 0),
    }


def unpack(packed):
    shifts = jnp.arange(16, dtype=jnp.int32)
    bit_planes = jnp.bitwise_and(jnp.right_shift(packed[..., :, None, :], shifts[:, None]), 1)
    flat_shape = packed.shape[:-2] + (packed.shape[-2] * 16, packed.shape[-1])
    return bit_planes.reshape(flat_shape)[..., :packed.shape[-1], :]

def reference(features, w_self, w_neigh, bias, d_out, nbr_ids, nbr_count, tiles):
    node_total = features.shape[0]
    blocked = features.reshape(NBLOCKS, BLK, F)
    slot_range = jnp.arange(NBMAX, dtype=jnp.int32)

    def live_tiles(live_count, packed):
        live_mask = (slot_range < live_count).astype(jnp.float32)
        return unpack(packed).astype(jnp.float32) * live_mask[:, None, None]

    def aggregate(row_args):
        block_ids, live_count, packed = row_args
        adjacency = live_tiles(live_count, packed)
        degree = lax.optimization_barrier(jnp.sum(adjacency, axis=(0, 2)))
        source = blocked[block_ids].astype(jnp.float32)
        neigh_sum = jnp.einsum('sij,sjc->ic', adjacency, source)
        return (neigh_sum, degree)
    neigh_sum, degree = lax.map(aggregate, (nbr_ids, nbr_count, tiles))
    denom = jnp.maximum(degree, 1.0)
    neigh_mean = (neigh_sum / denom[..., None]).astype(jnp.bfloat16).reshape(node_total, F)
    pre_act = jnp.dot(features, w_self, preferred_element_type=jnp.float32) + jnp.dot(neigh_mean, w_neigh, preferred_element_type=jnp.float32) + bias
    activated = jax.nn.elu(pre_act).astype(jnp.bfloat16)
    elu_slope = jnp.where(pre_act > 0, 1.0, jnp.exp(jnp.minimum(pre_act, 0.0)))
    dpre = (d_out.astype(jnp.float32) * elu_slope).astype(jnp.bfloat16)
    grad_scale = 1.0 / math.sqrt(node_total)
    grad_self = jnp.dot(features.T, dpre, preferred_element_type=jnp.float32) * grad_scale
    grad_neigh = jnp.dot(neigh_mean.T, dpre, preferred_element_type=jnp.float32) * grad_scale
    d_self = jnp.dot(dpre, w_self.T, preferred_element_type=jnp.float32).astype(jnp.bfloat16)
    d_neigh = jnp.dot(dpre, w_neigh.T, preferred_element_type=jnp.float32).astype(jnp.bfloat16)
    d_scaled = (d_neigh.astype(jnp.float32).reshape(NBLOCKS, BLK, F) / denom[..., None]).astype(jnp.bfloat16)

    def spread(grad_all, row_args):
        block_ids, live_count, packed, row_grad = row_args
        adjacency = live_tiles(live_count, packed)
        product = jnp.einsum('sij,ic->sjc', adjacency, row_grad.astype(jnp.float32))
        return (grad_all.at[block_ids].add(product), None)
    grad_all = lax.scan(spread, jnp.zeros((NBLOCKS, BLK, F), jnp.float32), (nbr_ids, nbr_count, tiles, d_scaled))[0]
    grad_features = d_self.astype(jnp.float32) + grad_all.reshape(node_total, F)
    return (activated, grad_features, grad_self, grad_neigh)
```

```python
import math

import jax
import jax.numpy as jnp
from jax import lax
from jax.experimental import pallas as pl
from jax.experimental.pallas import tpu as pltpu
from jax.sharding import PartitionSpec as P


def unpack_tile(words):
    nwords, width = words.shape
    shifts = lax.broadcasted_iota(jnp.int32, (16, width), 0)
    rows = [
        jnp.bitwise_and(jnp.right_shift(jnp.broadcast_to(words[w : w + 1, :], (16, width)), shifts), 1)
        for w in range(nwords)
    ]
    return jnp.concatenate(rows, axis=0).astype(jnp.float32).astype(jnp.bfloat16)


def forward_kernel(ids_ref, cnt_ref, feat_ref, tiles_ref, nm_ref, deg_ref):
    b = pl.program_id(0)
    slots = tiles_ref.shape[1]
    cols, width = feat_ref.shape[1], feat_ref.shape[2]
    ones = jnp.ones((16, width), jnp.bfloat16)

    def body(s, acc):
        adj = unpack_tile(tiles_ref[0, s])
        src = feat_ref[ids_ref[b * slots + s]]
        lhs = jnp.concatenate([src, ones], axis=0)
        return acc + lax.dot_general(
            lhs, adj, (((1,), (1,)), ((), ())), preferred_element_type=jnp.float32
        )

    acc = lax.fori_loop(0, cnt_ref[b], body, jnp.zeros((cols + 16, width), jnp.float32))
    deg = acc[cols : cols + 1, :]
    nm_ref[0] = (acc[:cols, :] / jnp.maximum(deg, 1.0)).astype(nm_ref.dtype)
    deg_ref[0] = deg


def backward_kernel(ids_ref, cnt_ref, ds_ref, tiles_ref, g_ref):
    b = pl.program_id(0)
    slots = tiles_ref.shape[1]

    @pl.when(b == 0)
    def _():
        g_ref[...] = jnp.zeros_like(g_ref)

    d = ds_ref[0]

    def body(s, carry):
        adj = unpack_tile(tiles_ref[0, s])
        prod = jnp.dot(d, adj, preferred_element_type=jnp.float32)
        t = ids_ref[b * slots + s]
        g_ref[t] = g_ref[t] + prod
        return carry

    lax.fori_loop(0, cnt_ref[b], body, 0)


def aggregate_forward(ids_flat, counts, feat_blocks, tiles):
    blocks_here, slots, nwords, width = tiles.shape
    all_blocks, cols, _ = feat_blocks.shape
    return pl.pallas_call(
        forward_kernel,
        grid_spec=pltpu.PrefetchScalarGridSpec(
            num_scalar_prefetch=2,
            grid=(blocks_here,),
            in_specs=[
                pl.BlockSpec((all_blocks, cols, width), lambda b, *_: (0, 0, 0)),
                pl.BlockSpec((1, slots, nwords, width), lambda b, *_: (b, 0, 0, 0)),
            ],
            out_specs=[
                pl.BlockSpec((1, cols, width), lambda b, *_: (b, 0, 0)),
                pl.BlockSpec((1, 1, width), lambda b, *_: (b, 0, 0)),
            ],
        ),
        out_shape=[
            jax.ShapeDtypeStruct((blocks_here, cols, width), jnp.bfloat16),
            jax.ShapeDtypeStruct((blocks_here, 1, width), jnp.float32),
        ],
        compiler_params=pltpu.CompilerParams(dimension_semantics=("arbitrary",)),
    )(ids_flat, counts, feat_blocks, tiles)


def aggregate_backward(ids_flat, counts, ds_blocks, tiles, all_blocks):
    blocks_here, slots, nwords, width = tiles.shape
    cols = ds_blocks.shape[1]
    return pl.pallas_call(
        backward_kernel,
        grid_spec=pltpu.PrefetchScalarGridSpec(
            num_scalar_prefetch=2,
            grid=(blocks_here,),
            in_specs=[
                pl.BlockSpec((1, cols, width), lambda b, *_: (b, 0, 0)),
                pl.BlockSpec((1, slots, nwords, width), lambda b, *_: (b, 0, 0, 0)),
            ],
            out_specs=pl.BlockSpec((all_blocks, cols, width), lambda b, *_: (0, 0, 0)),
        ),
        out_shape=jax.ShapeDtypeStruct((all_blocks, cols, width), jnp.float32),
        compiler_params=pltpu.CompilerParams(dimension_semantics=("arbitrary",)),
    )(ids_flat, counts, ds_blocks, tiles)


def shards(features, w_self, w_neigh, bias, d_out, nbr_ids, nbr_count, tiles):
    node_total, cols = features.shape
    block_size = tiles.shape[3]
    blocks_here = nbr_ids.shape[0]
    all_blocks = node_total // block_size
    node_group = lax.axis_index("node")
    feat_index = lax.axis_index("feat")

    feat_blocks = features.reshape(all_blocks, block_size, cols).transpose(0, 2, 1)
    ids_flat = nbr_ids.reshape(-1)

    nm_blocks, deg_blocks = aggregate_forward(ids_flat, nbr_count, feat_blocks, tiles)

    w_self_all = lax.all_gather(w_self, "feat", axis=0, tiled=True)
    w_neigh_all = lax.all_gather(w_neigh, "feat", axis=0, tiled=True)

    feat_parts = lax.axis_size("feat")
    per = blocks_here // feat_parts
    group_feat = lax.dynamic_slice_in_dim(feat_blocks, node_group * blocks_here, blocks_here, 0)
    sent = jnp.stack([group_feat, nm_blocks], axis=1).reshape(feat_parts, per, 2, cols, block_size)
    got = lax.all_to_all(sent, "feat", 0, 0, tiled=True)
    own_t = got.transpose(2, 0, 3, 1, 4).reshape(2, feat_parts * cols, per * block_size)
    own_feat_t = own_t[0]
    own_nm_t = own_t[1]

    contract_rows = (((0,), (0,)), ((), ()))
    pre_act = (
        lax.dot_general(own_feat_t, w_self_all, contract_rows, preferred_element_type=jnp.float32)
        + lax.dot_general(own_nm_t, w_neigh_all, contract_rows, preferred_element_type=jnp.float32)
        + bias
    )
    activated = jax.nn.elu(pre_act).astype(jnp.bfloat16)
    elu_slope = jnp.where(pre_act > 0, 1.0, jnp.exp(jnp.minimum(pre_act, 0.0)))
    dpre = (d_out.astype(jnp.float32) * elu_slope).astype(jnp.bfloat16)

    contract_cols = (((1,), (1,)), ((), ()))
    d_self_t = lax.dot_general(
        w_self_all, dpre, contract_cols, preferred_element_type=jnp.float32
    ).astype(jnp.bfloat16)
    d_neigh_t = lax.dot_general(
        w_neigh_all, dpre, contract_cols, preferred_element_type=jnp.float32
    ).astype(jnp.bfloat16)
    own_deg = lax.dynamic_slice_in_dim(deg_blocks, feat_index * per, per, 0).reshape(1, -1)
    d_scaled_t = (d_neigh_t.astype(jnp.float32) / jnp.maximum(own_deg, 1.0)).astype(jnp.bfloat16)

    back = (
        jnp.stack([d_self_t, d_scaled_t], axis=0)
        .reshape(2, feat_parts, cols, per, block_size)
        .transpose(1, 3, 0, 2, 4)
    )
    got_back = lax.all_to_all(back, "feat", 0, 0, tiled=True).reshape(blocks_here, 2, cols, block_size)
    d_self_blocks = got_back[:, 0]
    d_scaled_blocks = got_back[:, 1]

    part = jnp.concatenate(
        [
            jnp.dot(own_feat_t, dpre, preferred_element_type=jnp.float32),
            jnp.dot(own_nm_t, dpre, preferred_element_type=jnp.float32),
        ],
        axis=1,
    )
    grads = lax.psum(lax.psum_scatter(part, "feat", scatter_dimension=0, tiled=True), "node")
    grad_scale = 1.0 / math.sqrt(node_total)
    hidden = w_self.shape[1]
    grad_self = grads[:, :hidden] * grad_scale
    grad_neigh = grads[:, hidden:] * grad_scale

    grad_all = aggregate_backward(ids_flat, nbr_count, d_scaled_blocks, tiles, all_blocks)
    grad_group = lax.psum_scatter(grad_all, "node", scatter_dimension=0, tiled=True)
    grad_group = grad_group + d_self_blocks.astype(jnp.float32)
    grad_features = grad_group.transpose(0, 2, 1).reshape(-1, cols)
    return (activated, grad_features, grad_self, grad_neigh)


def solution(mesh):
    placed = (
        P(None, "feat"),
        P("feat", None),
        P("feat", None),
        P(),
        P(("node", "feat"), None),
        P("node", None),
        P("node"),
        P("node", None, None, None),
    )
    return jax.shard_map(
        shards,
        mesh=mesh,
        in_specs=placed,
        out_specs=(P(("node", "feat"), None), P("node", "feat"), P("feat", None), P("feat", None)),
        check_vma=False,
    )
```

```python
import math

import jax
import jax.numpy as jnp
from jax import lax
from jax.experimental import pallas as pl
from jax.experimental.pallas import tpu as pltpu
from jax.sharding import PartitionSpec as P

ROWS_PER_STEP = 8


def unpack_tile(words):
    nwords, width = words.shape
    shifts = lax.broadcasted_iota(jnp.int32, (16, width), 0)
    rows = [
        jnp.bitwise_and(jnp.right_shift(jnp.broadcast_to(words[w : w + 1, :], (16, width)), shifts), 1)
        for w in range(nwords)
    ]
    return jnp.concatenate(rows, axis=0).astype(jnp.float32).astype(jnp.bfloat16)


def forward_kernel(ids_ref, cnt_ref, feat_ref, tiles_ref, nm_ref, deg_ref):
    step = pl.program_id(0)
    rows_here, slots = tiles_ref.shape[0], tiles_ref.shape[1]
    cols = nm_ref.shape[2]

    def row(r, carry):
        b = step * rows_here + r
        cnt = cnt_ref[b]
        adjs, srcs = [], []
        for s in range(slots):
            live = jnp.where(s < cnt, 1.0, 0.0)
            adjs.append(unpack_tile(tiles_ref[r, s]))
            src = feat_ref[ids_ref[b * slots + s]]
            srcs.append((src.astype(jnp.float32) * live).astype(jnp.bfloat16))
        out = jnp.dot(
            jnp.concatenate(adjs, axis=1),
            jnp.concatenate(srcs, axis=0),
            preferred_element_type=jnp.float32,
        )
        deg = out[:, cols : cols + 1]
        nm_ref[r] = (out[:, :cols] / jnp.maximum(deg, 1.0)).astype(nm_ref.dtype)
        deg_ref[r] = deg
        return carry

    lax.fori_loop(0, rows_here, row, 0)


def backward_kernel(ids_ref, cnt_ref, ds_ref, tiles_ref, g_ref):
    step = pl.program_id(0)
    rows_here, slots = tiles_ref.shape[0], tiles_ref.shape[1]
    width = tiles_ref.shape[3]

    @pl.when(step == 0)
    def _():
        g_ref[...] = jnp.zeros_like(g_ref)

    def row(r, carry):
        b = step * rows_here + r
        cnt = cnt_ref[b]
        adjcat = jnp.concatenate([unpack_tile(tiles_ref[r, s]) for s in range(slots)], axis=1)
        res = jnp.dot(ds_ref[r], adjcat, preferred_element_type=jnp.float32)
        for s in range(slots):
            live = jnp.where(s < cnt, 1.0, 0.0)
            t = ids_ref[b * slots + s]
            g_ref[t] = g_ref[t] + res[:, s * width : (s + 1) * width] * live
        return carry

    lax.fori_loop(0, rows_here, row, 0)


def aggregate_forward(ids_flat, counts, feat_aug, tiles, cols):
    blocks_here, slots, nwords, width = tiles.shape
    all_blocks, block_size, aug = feat_aug.shape
    rows = ROWS_PER_STEP
    return pl.pallas_call(
        forward_kernel,
        grid_spec=pltpu.PrefetchScalarGridSpec(
            num_scalar_prefetch=2,
            grid=(blocks_here // rows,),
            in_specs=[
                pl.BlockSpec((all_blocks, block_size, aug), lambda i, *_: (0, 0, 0)),
                pl.BlockSpec((rows, slots, nwords, width), lambda i, *_: (i, 0, 0, 0)),
            ],
            out_specs=[
                pl.BlockSpec((rows, block_size, cols), lambda i, *_: (i, 0, 0)),
                pl.BlockSpec((rows, block_size, 1), lambda i, *_: (i, 0, 0)),
            ],
        ),
        out_shape=[
            jax.ShapeDtypeStruct((blocks_here, block_size, cols), jnp.bfloat16),
            jax.ShapeDtypeStruct((blocks_here, block_size, 1), jnp.float32),
        ],
        compiler_params=pltpu.CompilerParams(dimension_semantics=("arbitrary",)),
    )(ids_flat, counts, feat_aug, tiles)


def aggregate_backward(ids_flat, counts, ds_blocks, tiles, all_blocks):
    blocks_here, slots, nwords, width = tiles.shape
    cols = ds_blocks.shape[1]
    rows = ROWS_PER_STEP
    return pl.pallas_call(
        backward_kernel,
        grid_spec=pltpu.PrefetchScalarGridSpec(
            num_scalar_prefetch=2,
            grid=(blocks_here // rows,),
            in_specs=[
                pl.BlockSpec((rows, cols, width), lambda i, *_: (i, 0, 0)),
                pl.BlockSpec((rows, slots, nwords, width), lambda i, *_: (i, 0, 0, 0)),
            ],
            out_specs=pl.BlockSpec((all_blocks, cols, width), lambda i, *_: (0, 0, 0)),
        ),
        out_shape=jax.ShapeDtypeStruct((all_blocks, cols, width), jnp.float32),
        compiler_params=pltpu.CompilerParams(dimension_semantics=("arbitrary",)),
    )(ids_flat, counts, ds_blocks, tiles)


def shards(features, w_self, w_neigh, bias, d_out, nbr_ids, nbr_count, tiles):
    node_total, cols = features.shape
    hidden = w_self.shape[1]
    block_size = tiles.shape[3]
    blocks_here = nbr_ids.shape[0]
    all_blocks = node_total // block_size
    node_group = lax.axis_index("node")
    feat_index = lax.axis_index("feat")
    feat_parts = lax.axis_size("feat")
    per = blocks_here // feat_parts

    feat_nat = features.reshape(all_blocks, block_size, cols)
    feat_aug = jnp.concatenate([feat_nat, jnp.ones_like(feat_nat)], axis=2)
    ids_flat = nbr_ids.reshape(-1)

    nm_blocks, deg_blocks = aggregate_forward(ids_flat, nbr_count, feat_aug, tiles, cols)

    w_both = jnp.concatenate([w_self, w_neigh], axis=1)
    w_all = lax.all_to_all(
        jnp.broadcast_to(w_both[None], (feat_parts,) + w_both.shape), "feat", 0, 0, tiled=True
    ).reshape(feat_parts * cols, 2 * hidden)
    w_self_all = w_all[:, :hidden]
    w_neigh_all = w_all[:, hidden:]

    group_feat = lax.dynamic_slice_in_dim(feat_nat, node_group * blocks_here, blocks_here, 0)
    sent = jnp.stack([group_feat, nm_blocks], axis=1).reshape(feat_parts, per, 2, block_size, cols)
    got = lax.all_to_all(sent, "feat", 0, 0, tiled=True)
    own = got.transpose(2, 1, 3, 0, 4).reshape(2, per * block_size, feat_parts * cols)
    own_feat = own[0]
    own_nm = own[1]

    pre_act = (
        jnp.dot(own_feat, w_self_all, preferred_element_type=jnp.float32)
        + jnp.dot(own_nm, w_neigh_all, preferred_element_type=jnp.float32)
        + bias
    )
    activated = jax.nn.elu(pre_act).astype(jnp.bfloat16)
    elu_slope = jnp.where(pre_act > 0, 1.0, jnp.exp(jnp.minimum(pre_act, 0.0)))
    dpre = (d_out.astype(jnp.float32) * elu_slope).astype(jnp.bfloat16)

    contract_cols = (((1,), (1,)), ((), ()))
    d_self = lax.dot_general(
        dpre, w_self_all, contract_cols, preferred_element_type=jnp.float32
    ).astype(jnp.bfloat16)
    d_neigh = lax.dot_general(
        dpre, w_neigh_all, contract_cols, preferred_element_type=jnp.float32
    ).astype(jnp.bfloat16)
    own_deg = lax.dynamic_slice_in_dim(deg_blocks, feat_index * per, per, 0).reshape(-1, 1)
    d_scaled = (d_neigh.astype(jnp.float32) / jnp.maximum(own_deg, 1.0)).astype(jnp.bfloat16)

    contract_rows = (((0,), (0,)), ((), ()))
    part = jnp.concatenate(
        [
            lax.dot_general(own_feat, dpre, contract_rows, preferred_element_type=jnp.float32),
            lax.dot_general(own_nm, dpre, contract_rows, preferred_element_type=jnp.float32),
        ],
        axis=1,
    )
    part_got = lax.all_to_all(part.reshape(feat_parts, cols, 2 * hidden), "feat", 0, 0, tiled=True)
    grads = lax.psum(jnp.sum(part_got, axis=0), "node")
    grad_scale = 1.0 / math.sqrt(node_total)
    grad_self = grads[:, :hidden] * grad_scale
    grad_neigh = grads[:, hidden:] * grad_scale

    back = (
        jnp.stack([d_self, d_scaled], axis=0)
        .reshape(2, per, block_size, feat_parts, cols)
        .transpose(3, 1, 0, 2, 4)
    )
    got_back = lax.all_to_all(back, "feat", 0, 0, tiled=True).reshape(blocks_here, 2, block_size, cols)
    d_self_blocks = got_back[:, 0]
    d_scaled_t = got_back[:, 1].transpose(0, 2, 1)

    grad_all = aggregate_backward(ids_flat, nbr_count, d_scaled_t, tiles, all_blocks)
    grad_group = lax.psum_scatter(grad_all, "node", scatter_dimension=0, tiled=True)
    grad_features = (
        grad_group.transpose(0, 2, 1) + d_self_blocks.astype(jnp.float32)
    ).reshape(-1, cols)
    return (activated, grad_features, grad_self, grad_neigh)


def solution(mesh):
    placed = (
        P(None, "feat"),
        P("feat", None),
        P("feat", None),
        P(),
        P(("node", "feat"), None),
        P("node", None),
        P("node"),
        P("node", None, None, None),
    )
    return jax.shard_map(
        shards,
        mesh=mesh,
        in_specs=placed,
        out_specs=(P(("node", "feat"), None), P("node", "feat"), P("feat", None), P("feat", None)),
        check_vma=False,
    )
```

```python
import math

import jax
import jax.numpy as jnp
from jax import lax
from jax.experimental import pallas as pl
from jax.experimental.pallas import tpu as pltpu
from jax.sharding import PartitionSpec as P

ROWS_PER_STEP = 8


def unpack_tile(words):
    nwords, width = words.shape
    shifts = lax.broadcasted_iota(jnp.int32, (16, width), 0)
    rows = [
        jnp.bitwise_and(jnp.right_shift(jnp.broadcast_to(words[w : w + 1, :], (16, width)), shifts), 1)
        for w in range(nwords)
    ]
    return jnp.concatenate(rows, axis=0).astype(jnp.float32).astype(jnp.bfloat16)


def forward_kernel(ids_ref, cnt_ref, feat_ref, tiles_ref, nm_ref, deg_ref):
    step = pl.program_id(0)
    rows_here, slots = tiles_ref.shape[0], tiles_ref.shape[1]
    cols, width = feat_ref.shape[1], feat_ref.shape[2]

    def row(r, carry):
        b = step * rows_here + r
        cnt = cnt_ref[b]
        adjs, lhs = [], []
        for s in range(slots):
            live = jnp.where(s < cnt, 1.0, 0.0)
            adjs.append(unpack_tile(tiles_ref[r, s]))
            src = feat_ref[ids_ref[b * slots + s]].astype(jnp.float32) * live
            lhs.append(
                jnp.concatenate([src, jnp.full((cols, width), live, jnp.float32)], axis=0).astype(
                    jnp.bfloat16
                )
            )
        out = lax.dot_general(
            jnp.concatenate(lhs, axis=1),
            jnp.concatenate(adjs, axis=1),
            (((1,), (1,)), ((), ())),
            preferred_element_type=jnp.float32,
        )
        deg = out[cols : cols + 1, :]
        nm_ref[r] = (out[:cols, :] / jnp.maximum(deg, 1.0)).astype(nm_ref.dtype)
        deg_ref[r] = deg
        return carry

    lax.fori_loop(0, rows_here, row, 0)


def backward_kernel(ids_ref, cnt_ref, ds_ref, tiles_ref, g_ref):
    step = pl.program_id(0)
    rows_here, slots = tiles_ref.shape[0], tiles_ref.shape[1]
    width = tiles_ref.shape[3]

    @pl.when(step == 0)
    def _():
        g_ref[...] = jnp.zeros_like(g_ref)

    def row(r, carry):
        b = step * rows_here + r
        cnt = cnt_ref[b]
        adjcat = jnp.concatenate([unpack_tile(tiles_ref[r, s]) for s in range(slots)], axis=1)
        res = jnp.dot(ds_ref[r], adjcat, preferred_element_type=jnp.float32)
        for s in range(slots):
            live = jnp.where(s < cnt, 1.0, 0.0)
            t = ids_ref[b * slots + s]
            g_ref[t] = g_ref[t] + res[:, s * width : (s + 1) * width] * live
        return carry

    lax.fori_loop(0, rows_here, row, 0)


def aggregate_forward(ids_flat, counts, feat_t, tiles):
    blocks_here, slots, nwords, width = tiles.shape
    all_blocks, cols, _ = feat_t.shape
    rows = ROWS_PER_STEP
    return pl.pallas_call(
        forward_kernel,
        grid_spec=pltpu.PrefetchScalarGridSpec(
            num_scalar_prefetch=2,
            grid=(blocks_here // rows,),
            in_specs=[
                pl.BlockSpec((all_blocks, cols, width), lambda i, *_: (0, 0, 0)),
                pl.BlockSpec((rows, slots, nwords, width), lambda i, *_: (i, 0, 0, 0)),
            ],
            out_specs=[
                pl.BlockSpec((rows, cols, width), lambda i, *_: (i, 0, 0)),
                pl.BlockSpec((rows, 1, width), lambda i, *_: (i, 0, 0)),
            ],
        ),
        out_shape=[
            jax.ShapeDtypeStruct((blocks_here, cols, width), jnp.bfloat16),
            jax.ShapeDtypeStruct((blocks_here, 1, width), jnp.float32),
        ],
        compiler_params=pltpu.CompilerParams(dimension_semantics=("arbitrary",)),
    )(ids_flat, counts, feat_t, tiles)


def aggregate_backward(ids_flat, counts, ds_blocks, tiles, all_blocks):
    blocks_here, slots, nwords, width = tiles.shape
    cols = ds_blocks.shape[1]
    rows = ROWS_PER_STEP
    return pl.pallas_call(
        backward_kernel,
        grid_spec=pltpu.PrefetchScalarGridSpec(
            num_scalar_prefetch=2,
            grid=(blocks_here // rows,),
            in_specs=[
                pl.BlockSpec((rows, cols, width), lambda i, *_: (i, 0, 0)),
                pl.BlockSpec((rows, slots, nwords, width), lambda i, *_: (i, 0, 0, 0)),
            ],
            out_specs=pl.BlockSpec((all_blocks, cols, width), lambda i, *_: (0, 0, 0)),
        ),
        out_shape=jax.ShapeDtypeStruct((all_blocks, cols, width), jnp.float32),
        compiler_params=pltpu.CompilerParams(dimension_semantics=("arbitrary",)),
    )(ids_flat, counts, ds_blocks, tiles)


def shards(features, w_self, w_neigh, bias, d_out, nbr_ids, nbr_count, tiles):
    node_total, cols = features.shape
    hidden = w_self.shape[1]
    block_size = tiles.shape[3]
    blocks_here = nbr_ids.shape[0]
    all_blocks = node_total // block_size
    node_group = lax.axis_index("node")
    feat_index = lax.axis_index("feat")
    feat_parts = lax.axis_size("feat")
    per = blocks_here // feat_parts
    own_nodes = per * block_size

    feat_t = features.reshape(all_blocks, block_size, cols).transpose(0, 2, 1)
    ids_flat = nbr_ids.reshape(-1)

    nm_t, deg_blocks = aggregate_forward(ids_flat, nbr_count, feat_t, tiles)

    group_t = lax.dynamic_slice_in_dim(feat_t, node_group * blocks_here, blocks_here, 0)
    w_both = jnp.concatenate([w_self, w_neigh], axis=1).reshape(1, -1)
    sent = jnp.concatenate(
        [
            group_t.reshape(feat_parts, -1),
            nm_t.reshape(feat_parts, -1),
            jnp.broadcast_to(w_both, (feat_parts, w_both.shape[1])),
        ],
        axis=1,
    )
    got = lax.all_to_all(sent, "feat", 0, 0, tiled=True)
    span = own_nodes * cols
    own = (
        got[:, : 2 * span]
        .reshape(feat_parts, 2, per, cols, block_size)
        .transpose(1, 2, 4, 0, 3)
        .reshape(2, own_nodes, feat_parts * cols)
    )
    own_feat = own[0]
    own_nm = own[1]
    w_all = got[:, 2 * span :].reshape(feat_parts * cols, 2 * hidden)
    w_self_all = w_all[:, :hidden]
    w_neigh_all = w_all[:, hidden:]

    pre_act = (
        jnp.dot(own_feat, w_self_all, preferred_element_type=jnp.float32)
        + jnp.dot(own_nm, w_neigh_all, preferred_element_type=jnp.float32)
        + bias
    )
    activated = jax.nn.elu(pre_act).astype(jnp.bfloat16)
    elu_slope = jnp.where(pre_act > 0, 1.0, jnp.exp(jnp.minimum(pre_act, 0.0)))
    dpre = (d_out.astype(jnp.float32) * elu_slope).astype(jnp.bfloat16)

    contract_cols = (((1,), (1,)), ((), ()))
    d_self_t = lax.dot_general(
        w_self_all, dpre, contract_cols, preferred_element_type=jnp.float32
    ).astype(jnp.bfloat16)
    d_neigh_t = lax.dot_general(
        w_neigh_all, dpre, contract_cols, preferred_element_type=jnp.float32
    ).astype(jnp.bfloat16)
    own_deg = lax.dynamic_slice_in_dim(deg_blocks, feat_index * per, per, 0).reshape(1, -1)
    d_scaled_t = (d_neigh_t.astype(jnp.float32) / jnp.maximum(own_deg, 1.0)).astype(jnp.bfloat16)

    contract_rows = (((0,), (0,)), ((), ()))
    part = jnp.concatenate(
        [
            lax.dot_general(own_feat, dpre, contract_rows, preferred_element_type=jnp.float32),
            lax.dot_general(own_nm, dpre, contract_rows, preferred_element_type=jnp.float32),
        ],
        axis=1,
    )
    part_hi = part.astype(jnp.bfloat16)
    part_lo = (part - part_hi.astype(jnp.float32)).astype(jnp.bfloat16)

    def per_peer(x_t):
        return x_t.reshape(feat_parts, cols, per, block_size).transpose(0, 2, 1, 3).reshape(feat_parts, -1)

    back = jnp.concatenate(
        [
            per_peer(d_self_t),
            per_peer(d_scaled_t),
            part_hi.reshape(feat_parts, -1),
            part_lo.reshape(feat_parts, -1),
        ],
        axis=1,
    )
    got_back = lax.all_to_all(back, "feat", 0, 0, tiled=True)
    d_t = got_back[:, : 2 * span].reshape(feat_parts, 2, per, cols, block_size)
    d_self_blocks = d_t[:, 0].reshape(blocks_here, cols, block_size)
    d_scaled_blocks = d_t[:, 1].reshape(blocks_here, cols, block_size)
    halves = got_back[:, 2 * span :].reshape(feat_parts, 2, cols, 2 * hidden).astype(jnp.float32)
    grads = lax.psum(jnp.sum(halves[:, 0] + halves[:, 1], axis=0), "node")
    grad_scale = 1.0 / math.sqrt(node_total)
    grad_self = grads[:, :hidden] * grad_scale
    grad_neigh = grads[:, hidden:] * grad_scale

    grad_all = aggregate_backward(ids_flat, nbr_count, d_scaled_blocks, tiles, all_blocks)
    grad_group = lax.psum_scatter(grad_all, "node", scatter_dimension=0, tiled=True)
    grad_group = grad_group + d_self_blocks.astype(jnp.float32)
    grad_features = grad_group.transpose(0, 2, 1).reshape(-1, cols)
    return (activated, grad_features, grad_self, grad_neigh)


def solution(mesh):
    placed = (
        P(None, "feat"),
        P("feat", None),
        P("feat", None),
        P(),
        P(("node", "feat"), None),
        P("node", None),
        P("node"),
        P("node", None, None, None),
    )
    return jax.shard_map(
        shards,
        mesh=mesh,
        in_specs=placed,
        out_specs=(P(("node", "feat"), None), P("node", "feat"), P("feat", None), P("feat", None)),
        check_vma=False,
    )
```

```python
import math

import jax
import jax.numpy as jnp
from jax import lax
from jax.experimental import pallas as pl
from jax.experimental.pallas import tpu as pltpu
from jax.sharding import PartitionSpec as P

ROWS_PER_STEP = 8


def unpack_tile(words):
    nwords, width = words.shape
    shifts = lax.broadcasted_iota(jnp.int32, (16, width), 0)
    rows = [
        jnp.bitwise_and(jnp.right_shift(jnp.broadcast_to(words[w : w + 1, :], (16, width)), shifts), 1)
        for w in range(nwords)
    ]
    return jnp.concatenate(rows, axis=0).astype(jnp.float32).astype(jnp.bfloat16)


def forward_kernel(ids_ref, cnt_ref, feat_ref, tiles_ref, nm_ref, deg_ref):
    step = pl.program_id(0)
    rows_here, slots = tiles_ref.shape[0], tiles_ref.shape[1]
    cols, width = feat_ref.shape[1], feat_ref.shape[2]

    def row(r, carry):
        b = step * rows_here + r
        cnt = cnt_ref[b]
        adjs, lhs = [], []
        for s in range(slots):
            live = jnp.where(s < cnt, 1.0, 0.0)
            adjs.append(unpack_tile(tiles_ref[r, s]))
            src = feat_ref[ids_ref[b * slots + s]].astype(jnp.float32) * live
            lhs.append(
                jnp.concatenate([src, jnp.full((cols, width), live, jnp.float32)], axis=0).astype(
                    jnp.bfloat16
                )
            )
        out = lax.dot_general(
            jnp.concatenate(lhs, axis=1),
            jnp.concatenate(adjs, axis=1),
            (((1,), (1,)), ((), ())),
            preferred_element_type=jnp.float32,
        )
        deg = out[cols : cols + 1, :]
        nm_ref[r] = (out[:cols, :] / jnp.maximum(deg, 1.0)).astype(nm_ref.dtype)
        deg_ref[r] = deg
        return carry

    lax.fori_loop(0, rows_here, row, 0)


def backward_kernel(ids_ref, cnt_ref, ds_ref, tiles_ref, g_ref):
    step = pl.program_id(0)
    rows_here, slots = tiles_ref.shape[0], tiles_ref.shape[1]
    width = tiles_ref.shape[3]

    @pl.when(step == 0)
    def _():
        g_ref[...] = jnp.zeros_like(g_ref)

    def row(r, carry):
        b = step * rows_here + r
        cnt = cnt_ref[b]
        adjcat = jnp.concatenate([unpack_tile(tiles_ref[r, s]) for s in range(slots)], axis=1)
        res = jnp.dot(ds_ref[r], adjcat, preferred_element_type=jnp.float32)
        for s in range(slots):
            live = jnp.where(s < cnt, 1.0, 0.0)
            t = ids_ref[b * slots + s]
            g_ref[t] = g_ref[t] + res[:, s * width : (s + 1) * width] * live
        return carry

    lax.fori_loop(0, rows_here, row, 0)


def aggregate_forward(ids_flat, counts, feat_t, tiles):
    blocks_here, slots, nwords, width = tiles.shape
    all_blocks, cols, _ = feat_t.shape
    rows = ROWS_PER_STEP
    return pl.pallas_call(
        forward_kernel,
        grid_spec=pltpu.PrefetchScalarGridSpec(
            num_scalar_prefetch=2,
            grid=(blocks_here // rows,),
            in_specs=[
                pl.BlockSpec((all_blocks, cols, width), lambda i, *_: (0, 0, 0)),
                pl.BlockSpec((rows, slots, nwords, width), lambda i, *_: (i, 0, 0, 0)),
            ],
            out_specs=[
                pl.BlockSpec((rows, cols, width), lambda i, *_: (i, 0, 0)),
                pl.BlockSpec((rows, 1, width), lambda i, *_: (i, 0, 0)),
            ],
        ),
        out_shape=[
            jax.ShapeDtypeStruct((blocks_here, cols, width), jnp.bfloat16),
            jax.ShapeDtypeStruct((blocks_here, 1, width), jnp.float32),
        ],
        compiler_params=pltpu.CompilerParams(dimension_semantics=("arbitrary",)),
    )(ids_flat, counts, feat_t, tiles)


def aggregate_backward(ids_flat, counts, ds_blocks, tiles, all_blocks):
    blocks_here, slots, nwords, width = tiles.shape
    cols = ds_blocks.shape[1]
    rows = ROWS_PER_STEP
    return pl.pallas_call(
        backward_kernel,
        grid_spec=pltpu.PrefetchScalarGridSpec(
            num_scalar_prefetch=2,
            grid=(blocks_here // rows,),
            in_specs=[
                pl.BlockSpec((rows, cols, width), lambda i, *_: (i, 0, 0)),
                pl.BlockSpec((rows, slots, nwords, width), lambda i, *_: (i, 0, 0, 0)),
            ],
            out_specs=pl.BlockSpec((all_blocks, cols, width), lambda i, *_: (0, 0, 0)),
        ),
        out_shape=jax.ShapeDtypeStruct((all_blocks, cols, width), jnp.float32),
        compiler_params=pltpu.CompilerParams(dimension_semantics=("arbitrary",)),
    )(ids_flat, counts, ds_blocks, tiles)


def shards(features, w_self, w_neigh, bias, d_out, nbr_ids, nbr_count, tiles):
    node_total, cols = features.shape
    hidden = w_self.shape[1]
    block_size = tiles.shape[3]
    blocks_here = nbr_ids.shape[0]
    all_blocks = node_total // block_size
    node_group = lax.axis_index("node")
    feat_index = lax.axis_index("feat")
    feat_parts = lax.axis_size("feat")
    per = blocks_here // feat_parts
    own_nodes = per * block_size

    feat_t = features.reshape(all_blocks, block_size, cols).transpose(0, 2, 1)
    ids_flat = nbr_ids.reshape(-1)

    nm_t, deg_blocks = aggregate_forward(ids_flat, nbr_count, feat_t, tiles)

    w_both = jnp.concatenate([w_self, w_neigh], axis=1)
    w_all = lax.all_to_all(
        jnp.broadcast_to(w_both[None], (feat_parts,) + w_both.shape), "feat", 0, 0, tiled=True
    ).reshape(feat_parts * cols, 2 * hidden)
    w_self_all = w_all[:, :hidden]
    w_neigh_all = w_all[:, hidden:]

    group_t = lax.dynamic_slice_in_dim(feat_t, node_group * blocks_here, blocks_here, 0)
    sent = jnp.stack([group_t, nm_t], axis=1).reshape(feat_parts, per, 2, cols, block_size)
    got = lax.all_to_all(sent, "feat", 0, 0, tiled=True)
    own = got.transpose(2, 1, 4, 0, 3).reshape(2, own_nodes, feat_parts * cols)
    own_feat = own[0]
    own_nm = own[1]

    pre_act = (
        jnp.dot(own_feat, w_self_all, preferred_element_type=jnp.float32)
        + jnp.dot(own_nm, w_neigh_all, preferred_element_type=jnp.float32)
        + bias
    )
    activated = jax.nn.elu(pre_act).astype(jnp.bfloat16)
    elu_slope = jnp.where(pre_act > 0, 1.0, jnp.exp(jnp.minimum(pre_act, 0.0)))
    dpre = (d_out.astype(jnp.float32) * elu_slope).astype(jnp.bfloat16)

    contract_cols = (((1,), (1,)), ((), ()))
    d_self_t = lax.dot_general(
        w_self_all, dpre, contract_cols, preferred_element_type=jnp.float32
    ).astype(jnp.bfloat16)
    d_neigh_t = lax.dot_general(
        w_neigh_all, dpre, contract_cols, preferred_element_type=jnp.float32
    ).astype(jnp.bfloat16)
    own_deg = lax.dynamic_slice_in_dim(deg_blocks, feat_index * per, per, 0).reshape(1, -1)
    d_scaled_t = (d_neigh_t.astype(jnp.float32) / jnp.maximum(own_deg, 1.0)).astype(jnp.bfloat16)

    contract_rows = (((0,), (0,)), ((), ()))
    part = jnp.concatenate(
        [
            lax.dot_general(own_feat, dpre, contract_rows, preferred_element_type=jnp.float32),
            lax.dot_general(own_nm, dpre, contract_rows, preferred_element_type=jnp.float32),
        ],
        axis=1,
    )
    part_got = lax.all_to_all(part.reshape(feat_parts, cols, 2 * hidden), "feat", 0, 0, tiled=True)
    grads = lax.psum(jnp.sum(part_got, axis=0), "node")
    grad_scale = 1.0 / math.sqrt(node_total)
    grad_self = grads[:, :hidden] * grad_scale
    grad_neigh = grads[:, hidden:] * grad_scale

    back = (
        jnp.stack([d_self_t, d_scaled_t], axis=0)
        .reshape(2, feat_parts, cols, per, block_size)
        .transpose(1, 3, 0, 2, 4)
    )
    got_back = lax.all_to_all(back, "feat", 0, 0, tiled=True).reshape(blocks_here, 2, cols, block_size)
    d_self_blocks = got_back[:, 0]
    d_scaled_blocks = got_back[:, 1]

    grad_all = aggregate_backward(ids_flat, nbr_count, d_scaled_blocks, tiles, all_blocks)
    grad_group = lax.psum_scatter(grad_all, "node", scatter_dimension=0, tiled=True)
    grad_group = grad_group + d_self_blocks.astype(jnp.float32)
    grad_features = grad_group.transpose(0, 2, 1).reshape(-1, cols)
    return (activated, grad_features, grad_self, grad_neigh)


def solution(mesh):
    placed = (
        P(None, "feat"),
        P("feat", None),
        P("feat", None),
        P(),
        P(("node", "feat"), None),
        P("node", None),
        P("node"),
        P("node", None, None, None),
    )
    return jax.shard_map(
        shards,
        mesh=mesh,
        in_specs=placed,
        out_specs=(P(("node", "feat"), None), P("node", "feat"), P("feat", None), P("feat", None)),
        check_vma=False,
    )
```

```python
import functools
import math

import jax
import jax.numpy as jnp
from jax import lax
from jax.experimental import pallas as pl
from jax.experimental.pallas import tpu as pltpu
from jax.sharding import PartitionSpec as P

ROWS_PER_STEP = 8


def unpack_tile(words):
    nwords, width = words.shape
    shifts = lax.broadcasted_iota(jnp.int32, (16, width), 0)
    rows = [
        jnp.bitwise_and(jnp.right_shift(jnp.broadcast_to(words[w : w + 1, :], (16, width)), shifts), 1)
        for w in range(nwords)
    ]
    return jnp.concatenate(rows, axis=0).astype(jnp.float32).astype(jnp.bfloat16)


def forward_kernel(ids_ref, cnt_ref, feat_ref, tiles_ref, nm_ref, deg_ref):
    step = pl.program_id(0)
    rows_here, slots = tiles_ref.shape[0], tiles_ref.shape[1]
    cols, width = feat_ref.shape[1], feat_ref.shape[2]

    def row(r, carry):
        b = step * rows_here + r
        cnt = cnt_ref[b]
        adjs, lhs = [], []
        for s in range(slots):
            live = jnp.where(s < cnt, 1.0, 0.0)
            adjs.append(unpack_tile(tiles_ref[r, s]))
            src = feat_ref[ids_ref[b * slots + s]].astype(jnp.float32) * live
            lhs.append(
                jnp.concatenate([src, jnp.full((cols, width), live, jnp.float32)], axis=0).astype(
                    jnp.bfloat16
                )
            )
        out = lax.dot_general(
            jnp.concatenate(lhs, axis=1),
            jnp.concatenate(adjs, axis=1),
            (((1,), (1,)), ((), ())),
            preferred_element_type=jnp.float32,
        )
        deg = out[cols : cols + 1, :]
        nm_ref[r] = (out[:cols, :] / jnp.maximum(deg, 1.0)).astype(nm_ref.dtype)
        deg_ref[r] = deg
        return carry

    lax.fori_loop(0, rows_here, row, 0)


def backward_kernel(ids_ref, cnt_ref, ds_ref, tiles_ref, g_ref):
    step = pl.program_id(0)
    rows_here, slots = tiles_ref.shape[0], tiles_ref.shape[1]
    width = tiles_ref.shape[3]

    @pl.when(step == 0)
    def _():
        g_ref[...] = jnp.zeros_like(g_ref)

    def row(r, carry):
        b = step * rows_here + r
        cnt = cnt_ref[b]
        adjcat = jnp.concatenate([unpack_tile(tiles_ref[r, s]) for s in range(slots)], axis=1)
        res = jnp.dot(ds_ref[r], adjcat, preferred_element_type=jnp.float32)
        for s in range(slots):
            live = jnp.where(s < cnt, 1.0, 0.0)
            t = ids_ref[b * slots + s]
            g_ref[t] = g_ref[t] + res[:, s * width : (s + 1) * width] * live
        return carry

    lax.fori_loop(0, rows_here, row, 0)


def aggregate_forward(ids_flat, counts, feat_t, tiles):
    blocks_here, slots, nwords, width = tiles.shape
    all_blocks, cols, _ = feat_t.shape
    rows = ROWS_PER_STEP
    return pl.pallas_call(
        forward_kernel,
        grid_spec=pltpu.PrefetchScalarGridSpec(
            num_scalar_prefetch=2,
            grid=(blocks_here // rows,),
            in_specs=[
                pl.BlockSpec((all_blocks, cols, width), lambda i, *_: (0, 0, 0)),
                pl.BlockSpec((rows, slots, nwords, width), lambda i, *_: (i, 0, 0, 0)),
            ],
            out_specs=[
                pl.BlockSpec((rows, cols, width), lambda i, *_: (i, 0, 0)),
                pl.BlockSpec((rows, 1, width), lambda i, *_: (i, 0, 0)),
            ],
        ),
        out_shape=[
            jax.ShapeDtypeStruct((blocks_here, cols, width), jnp.bfloat16),
            jax.ShapeDtypeStruct((blocks_here, 1, width), jnp.float32),
        ],
        compiler_params=pltpu.CompilerParams(dimension_semantics=("arbitrary",)),
    )(ids_flat, counts, feat_t, tiles)


def aggregate_backward(ids_flat, counts, ds_blocks, tiles, all_blocks):
    blocks_here, slots, nwords, width = tiles.shape
    cols = ds_blocks.shape[1]
    rows = ROWS_PER_STEP
    return pl.pallas_call(
        backward_kernel,
        grid_spec=pltpu.PrefetchScalarGridSpec(
            num_scalar_prefetch=2,
            grid=(blocks_here // rows,),
            in_specs=[
                pl.BlockSpec((rows, cols, width), lambda i, *_: (i, 0, 0)),
                pl.BlockSpec((rows, slots, nwords, width), lambda i, *_: (i, 0, 0, 0)),
            ],
            out_specs=pl.BlockSpec((all_blocks, cols, width), lambda i, *_: (0, 0, 0)),
        ),
        out_shape=jax.ShapeDtypeStruct((all_blocks, cols, width), jnp.float32),
        compiler_params=pltpu.CompilerParams(dimension_semantics=("arbitrary",)),
    )(ids_flat, counts, ds_blocks, tiles)


def exchange_kernel(parts, kinds, *refs):
    n_in = len(kinds)
    ins, outs = refs[:n_in], refs[n_in : 2 * n_in]
    send_sems, recv_sems = refs[2 * n_in :]
    me = lax.axis_index("feat")
    mesh_id = pl.DeviceIdType.MESH

    barrier = pltpu.get_barrier_semaphore()

    def greet(k, carry):
        peer = lax.rem(me + k, parts)
        pl.semaphore_signal(barrier, 1, device_id={"feat": peer}, device_id_type=mesh_id)
        return carry

    lax.fori_loop(1, parts, greet, 0)
    pl.semaphore_wait(barrier, parts - 1)

    def copy(i, k):
        peer = lax.rem(me + k, parts)
        src = ins[i] if kinds[i] else ins[i].at[peer]
        return pltpu.make_async_remote_copy(
            src_ref=src,
            dst_ref=outs[i].at[me],
            send_sem=send_sems.at[i, k],
            recv_sem=recv_sems.at[i, k],
            device_id={"feat": peer},
            device_id_type=mesh_id,
        )

    def start(k, carry):
        for i in range(n_in):
            copy(i, k).start()
        return carry

    lax.fori_loop(1, parts, start, 0)
    for i in range(n_in):
        outs[i][me] = ins[i][...] if kinds[i] else ins[i][me]

    def finish(k, carry):
        for i in range(n_in):
            copy(i, k).wait()
        return carry

    lax.fori_loop(1, parts, finish, 0)


def exchange(arrays, kinds, parts, cid):
    out_shapes = [
        jax.ShapeDtypeStruct(((parts,) + x.shape) if kind else x.shape, x.dtype)
        for x, kind in zip(arrays, kinds)
    ]
    vmem = pl.BlockSpec(memory_space=pltpu.VMEM)
    return pl.pallas_call(
        functools.partial(exchange_kernel, parts, tuple(kinds)),
        out_shape=out_shapes,
        in_specs=[vmem] * len(arrays),
        out_specs=[vmem] * len(arrays),
        scratch_shapes=[
            pltpu.SemaphoreType.DMA((len(arrays), parts)),
            pltpu.SemaphoreType.DMA((len(arrays), parts)),
        ],
        compiler_params=pltpu.CompilerParams(collective_id=cid, has_side_effects=True),
    )(*arrays)


def shards(features, w_self, w_neigh, bias, d_out, nbr_ids, nbr_count, tiles):
    node_total, cols = features.shape
    hidden = w_self.shape[1]
    block_size = tiles.shape[3]
    blocks_here = nbr_ids.shape[0]
    all_blocks = node_total // block_size
    node_group = lax.axis_index("node")
    feat_index = lax.axis_index("feat")
    feat_parts = lax.axis_size("feat")
    per = blocks_here // feat_parts
    own_nodes = per * block_size

    feat_t = features.reshape(all_blocks, block_size, cols).transpose(0, 2, 1)
    ids_flat = nbr_ids.reshape(-1)

    nm_t, deg_blocks = aggregate_forward(ids_flat, nbr_count, feat_t, tiles)

    w_both = jnp.concatenate([w_self, w_neigh], axis=1)
    group_t = lax.dynamic_slice_in_dim(feat_t, node_group * blocks_here, blocks_here, 0)
    sent = jnp.stack([group_t, nm_t], axis=1).reshape(feat_parts, per, 2, cols, block_size)
    got, w_all = exchange([sent, w_both], [False, True], feat_parts, 0)
    w_all = w_all.reshape(feat_parts * cols, 2 * hidden)
    w_self_all = w_all[:, :hidden]
    w_neigh_all = w_all[:, hidden:]

    own = got.transpose(2, 1, 4, 0, 3).reshape(2, own_nodes, feat_parts * cols)
    own_feat = own[0]
    own_nm = own[1]

    pre_act = (
        jnp.dot(own_feat, w_self_all, preferred_element_type=jnp.float32)
        + jnp.dot(own_nm, w_neigh_all, preferred_element_type=jnp.float32)
        + bias
    )
    activated = jax.nn.elu(pre_act).astype(jnp.bfloat16)
    elu_slope = jnp.where(pre_act > 0, 1.0, jnp.exp(jnp.minimum(pre_act, 0.0)))
    dpre = (d_out.astype(jnp.float32) * elu_slope).astype(jnp.bfloat16)

    contract_cols = (((1,), (1,)), ((), ()))
    d_self_t = lax.dot_general(
        w_self_all, dpre, contract_cols, preferred_element_type=jnp.float32
    ).astype(jnp.bfloat16)
    d_neigh_t = lax.dot_general(
        w_neigh_all, dpre, contract_cols, preferred_element_type=jnp.float32
    ).astype(jnp.bfloat16)
    own_deg = lax.dynamic_slice_in_dim(deg_blocks, feat_index * per, per, 0).reshape(1, -1)
    d_scaled_t = (d_neigh_t.astype(jnp.float32) / jnp.maximum(own_deg, 1.0)).astype(jnp.bfloat16)

    contract_rows = (((0,), (0,)), ((), ()))
    part = jnp.concatenate(
        [
            lax.dot_general(own_feat, dpre, contract_rows, preferred_element_type=jnp.float32),
            lax.dot_general(own_nm, dpre, contract_rows, preferred_element_type=jnp.float32),
        ],
        axis=1,
    )
    back = (
        jnp.stack([d_self_t, d_scaled_t], axis=0)
        .reshape(2, feat_parts, cols, per, block_size)
        .transpose(1, 3, 0, 2, 4)
    )
    got_back, part_got = exchange(
        [back, part.reshape(feat_parts, cols, 2 * hidden)], [False, False], feat_parts, 1
    )
    got_back = got_back.reshape(blocks_here, 2, cols, block_size)
    d_self_blocks = got_back[:, 0]
    d_scaled_blocks = got_back[:, 1]
    grads = lax.psum(jnp.sum(part_got, axis=0), "node")
    grad_scale = 1.0 / math.sqrt(node_total)
    grad_self = grads[:, :hidden] * grad_scale
    grad_neigh = grads[:, hidden:] * grad_scale

    grad_all = aggregate_backward(ids_flat, nbr_count, d_scaled_blocks, tiles, all_blocks)
    grad_group = lax.psum_scatter(grad_all, "node", scatter_dimension=0, tiled=True)
    grad_group = grad_group + d_self_blocks.astype(jnp.float32)
    grad_features = grad_group.transpose(0, 2, 1).reshape(-1, cols)
    return (activated, grad_features, grad_self, grad_neigh)


def solution(mesh):
    placed = (
        P(None, "feat"),
        P("feat", None),
        P("feat", None),
        P(),
        P(("node", "feat"), None),
        P("node", None),
        P("node"),
        P("node", None, None, None),
    )
    return jax.shard_map(
        shards,
        mesh=mesh,
        in_specs=placed,
        out_specs=(P(("node", "feat"), None), P("node", "feat"), P("feat", None), P("feat", None)),
        check_vma=False,
    )
```

```python
import functools
import math

import jax
import jax.numpy as jnp
from jax import lax
from jax.experimental import pallas as pl
from jax.experimental.pallas import tpu as pltpu
from jax.sharding import PartitionSpec as P

ROWS_PER_STEP = 8


def unpack_tile(words):
    nwords, width = words.shape
    shifts = lax.broadcasted_iota(jnp.int32, (16, width), 0)
    rows = [
        jnp.bitwise_and(jnp.right_shift(jnp.broadcast_to(words[w : w + 1, :], (16, width)), shifts), 1)
        for w in range(nwords)
    ]
    return jnp.concatenate(rows, axis=0).astype(jnp.float32).astype(jnp.bfloat16)


def forward_kernel(ids_ref, cnt_ref, feat_ref, tiles_ref, nm_ref, deg_ref):
    step = pl.program_id(0)
    rows_here, slots = tiles_ref.shape[0], tiles_ref.shape[1]
    cols, width = feat_ref.shape[1], feat_ref.shape[2]

    def row(r, carry):
        b = step * rows_here + r
        cnt = cnt_ref[b]
        adjs, lhs = [], []
        for s in range(slots):
            live = jnp.where(s < cnt, 1.0, 0.0)
            adjs.append(unpack_tile(tiles_ref[r, s]))
            src = feat_ref[ids_ref[b * slots + s]].astype(jnp.float32) * live
            lhs.append(
                jnp.concatenate([src, jnp.full((cols, width), live, jnp.float32)], axis=0).astype(
                    jnp.bfloat16
                )
            )
        out = lax.dot_general(
            jnp.concatenate(lhs, axis=1),
            jnp.concatenate(adjs, axis=1),
            (((1,), (1,)), ((), ())),
            preferred_element_type=jnp.float32,
        )
        deg = out[cols : cols + 1, :]
        nm_ref[r] = (out[:cols, :] / jnp.maximum(deg, 1.0)).astype(nm_ref.dtype)
        deg_ref[r] = deg
        return carry

    lax.fori_loop(0, rows_here, row, 0)


def backward_kernel(ids_ref, cnt_ref, ds_ref, tiles_ref, g_ref):
    step = pl.program_id(0)
    rows_here, slots = tiles_ref.shape[0], tiles_ref.shape[1]
    width = tiles_ref.shape[3]

    @pl.when(step == 0)
    def _():
        g_ref[...] = jnp.zeros_like(g_ref)

    def row(r, carry):
        b = step * rows_here + r
        cnt = cnt_ref[b]
        adjcat = jnp.concatenate([unpack_tile(tiles_ref[r, s]) for s in range(slots)], axis=1)
        res = jnp.dot(ds_ref[r], adjcat, preferred_element_type=jnp.float32)
        for s in range(slots):
            live = jnp.where(s < cnt, 1.0, 0.0)
            t = ids_ref[b * slots + s]
            g_ref[t] = g_ref[t] + res[:, s * width : (s + 1) * width] * live
        return carry

    lax.fori_loop(0, rows_here, row, 0)


def aggregate_forward(ids_flat, counts, feat_t, tiles):
    blocks_here, slots, nwords, width = tiles.shape
    all_blocks, cols, _ = feat_t.shape
    rows = ROWS_PER_STEP
    return pl.pallas_call(
        forward_kernel,
        grid_spec=pltpu.PrefetchScalarGridSpec(
            num_scalar_prefetch=2,
            grid=(blocks_here // rows,),
            in_specs=[
                pl.BlockSpec((all_blocks, cols, width), lambda i, *_: (0, 0, 0)),
                pl.BlockSpec((rows, slots, nwords, width), lambda i, *_: (i, 0, 0, 0)),
            ],
            out_specs=[
                pl.BlockSpec((rows, cols, width), lambda i, *_: (i, 0, 0)),
                pl.BlockSpec((rows, 1, width), lambda i, *_: (i, 0, 0)),
            ],
        ),
        out_shape=[
            jax.ShapeDtypeStruct((blocks_here, cols, width), jnp.bfloat16),
            jax.ShapeDtypeStruct((blocks_here, 1, width), jnp.float32),
        ],
        compiler_params=pltpu.CompilerParams(dimension_semantics=("arbitrary",)),
    )(ids_flat, counts, feat_t, tiles)


def aggregate_backward(ids_flat, counts, ds_blocks, tiles, all_blocks):
    blocks_here, slots, nwords, width = tiles.shape
    cols = ds_blocks.shape[1]
    rows = ROWS_PER_STEP
    return pl.pallas_call(
        backward_kernel,
        grid_spec=pltpu.PrefetchScalarGridSpec(
            num_scalar_prefetch=2,
            grid=(blocks_here // rows,),
            in_specs=[
                pl.BlockSpec((rows, cols, width), lambda i, *_: (i, 0, 0)),
                pl.BlockSpec((rows, slots, nwords, width), lambda i, *_: (i, 0, 0, 0)),
            ],
            out_specs=pl.BlockSpec((all_blocks, cols, width), lambda i, *_: (0, 0, 0)),
        ),
        out_shape=jax.ShapeDtypeStruct((all_blocks, cols, width), jnp.float32),
        compiler_params=pltpu.CompilerParams(dimension_semantics=("arbitrary",)),
    )(ids_flat, counts, ds_blocks, tiles)


def exchange_kernel(parts, kinds, *refs):
    n_in = len(kinds)
    ins, outs = refs[:n_in], refs[n_in : 2 * n_in]
    send_sems, recv_sems = refs[2 * n_in :]
    me = lax.axis_index("feat")
    mesh_id = pl.DeviceIdType.MESH

    barrier = pltpu.get_barrier_semaphore()

    def greet(k, carry):
        peer = lax.rem(me + k, parts)
        pl.semaphore_signal(barrier, 1, device_id={"feat": peer}, device_id_type=mesh_id)
        return carry

    lax.fori_loop(1, parts, greet, 0)
    pl.semaphore_wait(barrier, parts - 1)

    def copy(i, k):
        peer = lax.rem(me + k, parts)
        src = ins[i] if kinds[i] else ins[i].at[peer]
        return pltpu.make_async_remote_copy(
            src_ref=src,
            dst_ref=outs[i].at[me],
            send_sem=send_sems.at[i, k],
            recv_sem=recv_sems.at[i, k],
            device_id={"feat": peer},
            device_id_type=mesh_id,
        )

    def start(k, carry):
        for i in range(n_in):
            copy(i, k).start()
        return carry

    lax.fori_loop(1, parts, start, 0)
    for i in range(n_in):
        outs[i][me] = ins[i][...] if kinds[i] else ins[i][me]

    def finish(k, carry):
        for i in range(n_in):
            copy(i, k).wait()
        return carry

    lax.fori_loop(1, parts, finish, 0)


def exchange(arrays, kinds, parts, cid):
    out_shapes = [
        jax.ShapeDtypeStruct(((parts,) + x.shape) if kind else x.shape, x.dtype)
        for x, kind in zip(arrays, kinds)
    ]
    vmem = pl.BlockSpec(memory_space=pltpu.VMEM)
    return pl.pallas_call(
        functools.partial(exchange_kernel, parts, tuple(kinds)),
        out_shape=out_shapes,
        in_specs=[vmem] * len(arrays),
        out_specs=[vmem] * len(arrays),
        scratch_shapes=[
            pltpu.SemaphoreType.DMA((len(arrays), parts)),
            pltpu.SemaphoreType.DMA((len(arrays), parts)),
        ],
        compiler_params=pltpu.CompilerParams(collective_id=cid, has_side_effects=True),
    )(*arrays)


def shards(features, w_self, w_neigh, bias, d_out, nbr_ids, nbr_count, tiles):
    node_total, cols = features.shape
    hidden = w_self.shape[1]
    block_size = tiles.shape[3]
    blocks_here = nbr_ids.shape[0]
    all_blocks = node_total // block_size
    node_group = lax.axis_index("node")
    feat_index = lax.axis_index("feat")
    feat_parts = lax.axis_size("feat")
    per = blocks_here // feat_parts
    own_nodes = per * block_size

    feat_t = features.reshape(all_blocks, block_size, cols).transpose(0, 2, 1)
    ids_flat = nbr_ids.reshape(-1)

    nm_t, deg_blocks = aggregate_forward(ids_flat, nbr_count, feat_t, tiles)

    w_both = jnp.concatenate([w_self, w_neigh], axis=1)
    group_t = lax.dynamic_slice_in_dim(feat_t, node_group * blocks_here, blocks_here, 0)
    sent = jnp.stack([group_t, nm_t], axis=1).reshape(feat_parts, per, 2, cols, block_size)
    got, w_all = exchange([sent, w_both], [False, True], feat_parts, 0)
    w_all = w_all.reshape(feat_parts * cols, 2 * hidden)
    w_self_all = w_all[:, :hidden]
    w_neigh_all = w_all[:, hidden:]

    own = got.transpose(2, 1, 4, 0, 3).reshape(2, own_nodes, feat_parts * cols)
    own_feat = own[0]
    own_nm = own[1]

    pre_act = (
        jnp.dot(own_feat, w_self_all, preferred_element_type=jnp.float32)
        + jnp.dot(own_nm, w_neigh_all, preferred_element_type=jnp.float32)
        + bias
    )
    activated = jax.nn.elu(pre_act).astype(jnp.bfloat16)
    elu_slope = jnp.where(pre_act > 0, 1.0, jnp.exp(jnp.minimum(pre_act, 0.0)))
    dpre = (d_out.astype(jnp.float32) * elu_slope).astype(jnp.bfloat16)

    contract_cols = (((1,), (1,)), ((), ()))
    d_self_t = lax.dot_general(
        w_self_all, dpre, contract_cols, preferred_element_type=jnp.float32
    ).astype(jnp.bfloat16)
    d_neigh_t = lax.dot_general(
        w_neigh_all, dpre, contract_cols, preferred_element_type=jnp.float32
    ).astype(jnp.bfloat16)
    own_deg = lax.dynamic_slice_in_dim(deg_blocks, feat_index * per, per, 0).reshape(1, -1)
    d_scaled_t = (d_neigh_t.astype(jnp.float32) / jnp.maximum(own_deg, 1.0)).astype(jnp.bfloat16)

    contract_rows = (((0,), (0,)), ((), ()))
    part = jnp.concatenate(
        [
            lax.dot_general(own_feat, dpre, contract_rows, preferred_element_type=jnp.float32),
            lax.dot_general(own_nm, dpre, contract_rows, preferred_element_type=jnp.float32),
        ],
        axis=1,
    )
    part_got = lax.all_to_all(part.reshape(feat_parts, cols, 2 * hidden), "feat", 0, 0, tiled=True)
    grads = lax.psum(jnp.sum(part_got, axis=0), "node")
    grad_scale = 1.0 / math.sqrt(node_total)
    grad_self = grads[:, :hidden] * grad_scale
    grad_neigh = grads[:, hidden:] * grad_scale

    back = (
        jnp.stack([d_self_t, d_scaled_t], axis=0)
        .reshape(2, feat_parts, cols, per, block_size)
        .transpose(1, 3, 0, 2, 4)
    )
    got_back = lax.all_to_all(back, "feat", 0, 0, tiled=True).reshape(blocks_here, 2, cols, block_size)
    d_self_blocks = got_back[:, 0]
    d_scaled_blocks = got_back[:, 1]

    grad_all = aggregate_backward(ids_flat, nbr_count, d_scaled_blocks, tiles, all_blocks)
    grad_group = lax.psum_scatter(grad_all, "node", scatter_dimension=0, tiled=True)
    grad_group = grad_group + d_self_blocks.astype(jnp.float32)
    grad_features = grad_group.transpose(0, 2, 1).reshape(-1, cols)
    return (activated, grad_features, grad_self, grad_neigh)


def solution(mesh):
    placed = (
        P(None, "feat"),
        P("feat", None),
        P("feat", None),
        P(),
        P(("node", "feat"), None),
        P("node", None),
        P("node"),
        P("node", None, None, None),
    )
    return jax.shard_map(
        shards,
        mesh=mesh,
        in_specs=placed,
        out_specs=(P(("node", "feat"), None), P("node", "feat"), P("feat", None), P("feat", None)),
        check_vma=False,
    )
```

```python
import functools
import math

import jax
import jax.numpy as jnp
from jax import lax
from jax.experimental import pallas as pl
from jax.experimental.pallas import tpu as pltpu
from jax.sharding import PartitionSpec as P

ROWS_PER_STEP = 8


def unpack_tile(words):
    nwords, width = words.shape
    shifts = lax.broadcasted_iota(jnp.int32, (16, width), 0)
    rows = [
        jnp.bitwise_and(jnp.right_shift(jnp.broadcast_to(words[w : w + 1, :], (16, width)), shifts), 1)
        for w in range(nwords)
    ]
    return jnp.concatenate(rows, axis=0).astype(jnp.float32).astype(jnp.bfloat16)


def forward_kernel(ids_ref, cnt_ref, feat_ref, tiles_ref, nm_ref, deg_ref):
    step = pl.program_id(0)
    rows_here, slots = tiles_ref.shape[0], tiles_ref.shape[1]
    cols, width = feat_ref.shape[1], feat_ref.shape[2]

    def row(r, carry):
        b = step * rows_here + r
        cnt = cnt_ref[b]
        adjs, lhs = [], []
        for s in range(slots):
            live = jnp.where(s < cnt, 1.0, 0.0)
            adjs.append(unpack_tile(tiles_ref[r, s]))
            src = feat_ref[ids_ref[b * slots + s]].astype(jnp.float32) * live
            lhs.append(
                jnp.concatenate([src, jnp.full((cols, width), live, jnp.float32)], axis=0).astype(
                    jnp.bfloat16
                )
            )
        out = lax.dot_general(
            jnp.concatenate(lhs, axis=1),
            jnp.concatenate(adjs, axis=1),
            (((1,), (1,)), ((), ())),
            preferred_element_type=jnp.float32,
        )
        deg = out[cols : cols + 1, :]
        nm_ref[r] = (out[:cols, :] / jnp.maximum(deg, 1.0)).astype(nm_ref.dtype)
        deg_ref[r] = deg
        return carry

    lax.fori_loop(0, rows_here, row, 0)


def backward_kernel(ids_ref, cnt_ref, ds_ref, tiles_ref, g_ref):
    step = pl.program_id(0)
    rows_here, slots = tiles_ref.shape[0], tiles_ref.shape[1]
    width = tiles_ref.shape[3]

    @pl.when(step == 0)
    def _():
        g_ref[...] = jnp.zeros_like(g_ref)

    def row(r, carry):
        b = step * rows_here + r
        cnt = cnt_ref[b]
        adjcat = jnp.concatenate([unpack_tile(tiles_ref[r, s]) for s in range(slots)], axis=1)
        res = jnp.dot(ds_ref[r], adjcat, preferred_element_type=jnp.float32)
        for s in range(slots):
            live = jnp.where(s < cnt, 1.0, 0.0)
            t = ids_ref[b * slots + s]
            g_ref[t] = g_ref[t] + res[:, s * width : (s + 1) * width] * live
        return carry

    lax.fori_loop(0, rows_here, row, 0)


def aggregate_forward(ids_flat, counts, feat_t, tiles):
    blocks_here, slots, nwords, width = tiles.shape
    all_blocks, cols, _ = feat_t.shape
    rows = ROWS_PER_STEP
    return pl.pallas_call(
        forward_kernel,
        grid_spec=pltpu.PrefetchScalarGridSpec(
            num_scalar_prefetch=2,
            grid=(blocks_here // rows,),
            in_specs=[
                pl.BlockSpec((all_blocks, cols, width), lambda i, *_: (0, 0, 0)),
                pl.BlockSpec((rows, slots, nwords, width), lambda i, *_: (i, 0, 0, 0)),
            ],
            out_specs=[
                pl.BlockSpec((rows, cols, width), lambda i, *_: (i, 0, 0)),
                pl.BlockSpec((rows, 1, width), lambda i, *_: (i, 0, 0)),
            ],
        ),
        out_shape=[
            jax.ShapeDtypeStruct((blocks_here, cols, width), jnp.bfloat16),
            jax.ShapeDtypeStruct((blocks_here, 1, width), jnp.float32),
        ],
        compiler_params=pltpu.CompilerParams(dimension_semantics=("arbitrary",)),
    )(ids_flat, counts, feat_t, tiles)


def aggregate_backward(ids_flat, counts, ds_blocks, tiles, all_blocks):
    blocks_here, slots, nwords, width = tiles.shape
    cols = ds_blocks.shape[1]
    rows = ROWS_PER_STEP
    return pl.pallas_call(
        backward_kernel,
        grid_spec=pltpu.PrefetchScalarGridSpec(
            num_scalar_prefetch=2,
            grid=(blocks_here // rows,),
            in_specs=[
                pl.BlockSpec((rows, cols, width), lambda i, *_: (i, 0, 0)),
                pl.BlockSpec((rows, slots, nwords, width), lambda i, *_: (i, 0, 0, 0)),
            ],
            out_specs=pl.BlockSpec((all_blocks, cols, width), lambda i, *_: (0, 0, 0)),
        ),
        out_shape=jax.ShapeDtypeStruct((all_blocks, cols, width), jnp.float32),
        compiler_params=pltpu.CompilerParams(dimension_semantics=("arbitrary",)),
    )(ids_flat, counts, ds_blocks, tiles)


def exchange_kernel(parts, kinds, *refs):
    n_in = len(kinds)
    ins, outs = refs[:n_in], refs[n_in : 2 * n_in]
    send_sems, recv_sems = refs[2 * n_in :]
    me = lax.axis_index("feat")
    mesh_id = pl.DeviceIdType.MESH

    barrier = pltpu.get_barrier_semaphore()

    def greet(k, carry):
        peer = lax.rem(me + k, parts)
        pl.semaphore_signal(barrier, 1, device_id={"feat": peer}, device_id_type=mesh_id)
        return carry

    lax.fori_loop(1, parts, greet, 0)
    pl.semaphore_wait(barrier, parts - 1)

    def copy(i, k):
        peer = lax.rem(me + k, parts)
        src = ins[i] if kinds[i] else ins[i].at[peer]
        return pltpu.make_async_remote_copy(
            src_ref=src,
            dst_ref=outs[i].at[me],
            send_sem=send_sems.at[i, k],
            recv_sem=recv_sems.at[i, k],
            device_id={"feat": peer},
            device_id_type=mesh_id,
        )

    def start(k, carry):
        for i in range(n_in):
            copy(i, k).start()
        return carry

    lax.fori_loop(1, parts, start, 0)
    for i in range(n_in):
        outs[i][me] = ins[i][...] if kinds[i] else ins[i][me]

    def finish(k, carry):
        for i in range(n_in):
            copy(i, k).wait()
        return carry

    lax.fori_loop(1, parts, finish, 0)


def exchange(arrays, kinds, parts, cid):
    out_shapes = [
        jax.ShapeDtypeStruct(((parts,) + x.shape) if kind else x.shape, x.dtype)
        for x, kind in zip(arrays, kinds)
    ]
    vmem = pl.BlockSpec(memory_space=pltpu.VMEM)
    return pl.pallas_call(
        functools.partial(exchange_kernel, parts, tuple(kinds)),
        out_shape=out_shapes,
        in_specs=[vmem] * len(arrays),
        out_specs=[vmem] * len(arrays),
        scratch_shapes=[
            pltpu.SemaphoreType.DMA((len(arrays), parts)),
            pltpu.SemaphoreType.DMA((len(arrays), parts)),
        ],
        compiler_params=pltpu.CompilerParams(collective_id=cid, has_side_effects=True),
    )(*arrays)


def forward_exchange_kernel(
    parts, ids_ref, cnt_ref, feat_ref, tiles_ref, w_ref,
    feat_out, nm_out, w_out, deg_ref, nm_scr, send_sems, recv_sems,
):
    me = lax.axis_index("feat")
    group = lax.axis_index("node")
    blocks_here, slots = tiles_ref.shape[0], tiles_ref.shape[1]
    cols, width = feat_ref.shape[1], feat_ref.shape[2]
    per = blocks_here // parts
    mesh_id = pl.DeviceIdType.MESH

    barrier = pltpu.get_barrier_semaphore()

    def greet(k, carry):
        peer = lax.rem(me + k, parts)
        pl.semaphore_signal(barrier, 1, device_id={"feat": peer}, device_id_type=mesh_id)
        return carry

    lax.fori_loop(1, parts, greet, 0)
    pl.semaphore_wait(barrier, parts - 1)

    def copy(i, k):
        peer = lax.rem(me + k, parts)
        if i == 0:
            src, dst = w_ref, w_out
        elif i == 1:
            src, dst = feat_ref.at[pl.ds(group * blocks_here + peer * per, per)], feat_out
        else:
            src, dst = nm_scr.at[pl.ds(peer * per, per)], nm_out
        return pltpu.make_async_remote_copy(
            src_ref=src,
            dst_ref=dst.at[me],
            send_sem=send_sems.at[i, k],
            recv_sem=recv_sems.at[i, k],
            device_id={"feat": peer},
            device_id_type=mesh_id,
        )

    def start_inputs(k, carry):
        copy(0, k).start()
        copy(1, k).start()
        return carry

    lax.fori_loop(1, parts, start_inputs, 0)
    w_out[me] = w_ref[...]
    feat_out[me] = feat_ref[pl.ds(group * blocks_here + me * per, per)]

    def row(b, carry):
        cnt = cnt_ref[b]
        adjs, lhs = [], []
        for s in range(slots):
            live = jnp.where(s < cnt, 1.0, 0.0)
            adjs.append(unpack_tile(tiles_ref[b, s]))
            src = feat_ref[ids_ref[b * slots + s]].astype(jnp.float32) * live
            lhs.append(
                jnp.concatenate([src, jnp.full((cols, width), live, jnp.float32)], axis=0).astype(
                    jnp.bfloat16
                )
            )
        out = lax.dot_general(
            jnp.concatenate(lhs, axis=1),
            jnp.concatenate(adjs, axis=1),
            (((1,), (1,)), ((), ())),
            preferred_element_type=jnp.float32,
        )
        deg = out[cols : cols + 1, :]
        nm_scr[b] = (out[:cols, :] / jnp.maximum(deg, 1.0)).astype(nm_scr.dtype)
        deg_ref[b] = deg
        return carry

    lax.fori_loop(0, blocks_here, row, 0)

    def start_result(k, carry):
        copy(2, k).start()
        return carry

    lax.fori_loop(1, parts, start_result, 0)
    nm_out[me] = nm_scr[pl.ds(me * per, per)]

    def finish(k, carry):
        for i in range(3):
            copy(i, k).wait()
        return carry

    lax.fori_loop(1, parts, finish, 0)


def forward_exchange(ids_flat, counts, feat_t, tiles, w_both, parts):
    blocks_here, slots, nwords, width = tiles.shape
    all_blocks, cols, _ = feat_t.shape
    per = blocks_here // parts
    vmem = pl.BlockSpec(memory_space=pltpu.VMEM)
    smem = pl.BlockSpec(memory_space=pltpu.SMEM)
    return pl.pallas_call(
        functools.partial(forward_exchange_kernel, parts),
        out_shape=[
            jax.ShapeDtypeStruct((parts, per, cols, width), jnp.bfloat16),
            jax.ShapeDtypeStruct((parts, per, cols, width), jnp.bfloat16),
            jax.ShapeDtypeStruct((parts,) + w_both.shape, w_both.dtype),
            jax.ShapeDtypeStruct((blocks_here, 1, width), jnp.float32),
        ],
        in_specs=[smem, smem, vmem, vmem, vmem],
        out_specs=[vmem] * 4,
        scratch_shapes=[
            pltpu.VMEM((blocks_here, cols, width), jnp.bfloat16),
            pltpu.SemaphoreType.DMA((3, parts)),
            pltpu.SemaphoreType.DMA((3, parts)),
        ],
        compiler_params=pltpu.CompilerParams(collective_id=0, has_side_effects=True),
    )(ids_flat, counts, feat_t, tiles, w_both)


def shards(features, w_self, w_neigh, bias, d_out, nbr_ids, nbr_count, tiles):
    node_total, cols = features.shape
    hidden = w_self.shape[1]
    block_size = tiles.shape[3]
    blocks_here = nbr_ids.shape[0]
    all_blocks = node_total // block_size
    node_group = lax.axis_index("node")
    feat_index = lax.axis_index("feat")
    feat_parts = lax.axis_size("feat")
    per = blocks_here // feat_parts
    own_nodes = per * block_size

    feat_t = features.reshape(all_blocks, block_size, cols).transpose(0, 2, 1)
    ids_flat = nbr_ids.reshape(-1)

    w_both = jnp.concatenate([w_self, w_neigh], axis=1)
    feat_got, nm_got, w_all, deg_blocks = forward_exchange(
        ids_flat, nbr_count, feat_t, tiles, w_both, feat_parts
    )
    w_all = w_all.reshape(feat_parts * cols, 2 * hidden)
    w_self_all = w_all[:, :hidden]
    w_neigh_all = w_all[:, hidden:]
    own_feat = feat_got.transpose(1, 3, 0, 2).reshape(own_nodes, feat_parts * cols)
    own_nm = nm_got.transpose(1, 3, 0, 2).reshape(own_nodes, feat_parts * cols)

    pre_act = (
        jnp.dot(own_feat, w_self_all, preferred_element_type=jnp.float32)
        + jnp.dot(own_nm, w_neigh_all, preferred_element_type=jnp.float32)
        + bias
    )
    activated = jax.nn.elu(pre_act).astype(jnp.bfloat16)
    elu_slope = jnp.where(pre_act > 0, 1.0, jnp.exp(jnp.minimum(pre_act, 0.0)))
    dpre = (d_out.astype(jnp.float32) * elu_slope).astype(jnp.bfloat16)

    contract_cols = (((1,), (1,)), ((), ()))
    d_self_t = lax.dot_general(
        w_self_all, dpre, contract_cols, preferred_element_type=jnp.float32
    ).astype(jnp.bfloat16)
    d_neigh_t = lax.dot_general(
        w_neigh_all, dpre, contract_cols, preferred_element_type=jnp.float32
    ).astype(jnp.bfloat16)
    own_deg = lax.dynamic_slice_in_dim(deg_blocks, feat_index * per, per, 0).reshape(1, -1)
    d_scaled_t = (d_neigh_t.astype(jnp.float32) / jnp.maximum(own_deg, 1.0)).astype(jnp.bfloat16)

    contract_rows = (((0,), (0,)), ((), ()))
    part = jnp.concatenate(
        [
            lax.dot_general(own_feat, dpre, contract_rows, preferred_element_type=jnp.float32),
            lax.dot_general(own_nm, dpre, contract_rows, preferred_element_type=jnp.float32),
        ],
        axis=1,
    )
    part_got = lax.all_to_all(part.reshape(feat_parts, cols, 2 * hidden), "feat", 0, 0, tiled=True)
    grads = lax.psum(jnp.sum(part_got, axis=0), "node")
    grad_scale = 1.0 / math.sqrt(node_total)
    grad_self = grads[:, :hidden] * grad_scale
    grad_neigh = grads[:, hidden:] * grad_scale

    back = (
        jnp.stack([d_self_t, d_scaled_t], axis=0)
        .reshape(2, feat_parts, cols, per, block_size)
        .transpose(1, 3, 0, 2, 4)
    )
    got_back = lax.all_to_all(back, "feat", 0, 0, tiled=True).reshape(blocks_here, 2, cols, block_size)
    d_self_blocks = got_back[:, 0]
    d_scaled_blocks = got_back[:, 1]

    grad_all = aggregate_backward(ids_flat, nbr_count, d_scaled_blocks, tiles, all_blocks)
    grad_group = lax.psum_scatter(grad_all, "node", scatter_dimension=0, tiled=True)
    grad_group = grad_group + d_self_blocks.astype(jnp.float32)
    grad_features = grad_group.transpose(0, 2, 1).reshape(-1, cols)
    return (activated, grad_features, grad_self, grad_neigh)


def solution(mesh):
    placed = (
        P(None, "feat"),
        P("feat", None),
        P("feat", None),
        P(),
        P(("node", "feat"), None),
        P("node", None),
        P("node"),
        P("node", None, None, None),
    )
    return jax.shard_map(
        shards,
        mesh=mesh,
        in_specs=placed,
        out_specs=(P(("node", "feat"), None), P("node", "feat"), P("feat", None), P("feat", None)),
        check_vma=False,
    )
```

```python
import functools
import math

import jax
import jax.numpy as jnp
from jax import lax
from jax.experimental import pallas as pl
from jax.experimental.pallas import tpu as pltpu
from jax.sharding import PartitionSpec as P

ROWS_PER_STEP = 8


def unpack_tile(words):
    nwords, width = words.shape
    shifts = lax.broadcasted_iota(jnp.int32, (16, width), 0)
    rows = [
        jnp.bitwise_and(jnp.right_shift(jnp.broadcast_to(words[w : w + 1, :], (16, width)), shifts), 1)
        for w in range(nwords)
    ]
    return jnp.concatenate(rows, axis=0).astype(jnp.float32).astype(jnp.bfloat16)


def forward_kernel(ids_ref, cnt_ref, feat_ref, tiles_ref, nm_ref, deg_ref):
    step = pl.program_id(0)
    rows_here, slots = tiles_ref.shape[0], tiles_ref.shape[1]
    cols, width = feat_ref.shape[1], feat_ref.shape[2]

    def row(r, carry):
        b = step * rows_here + r
        cnt = cnt_ref[b]
        adjs, lhs = [], []
        for s in range(slots):
            live = jnp.where(s < cnt, 1.0, 0.0)
            adjs.append(unpack_tile(tiles_ref[r, s]))
            src = feat_ref[ids_ref[b * slots + s]].astype(jnp.float32) * live
            lhs.append(
                jnp.concatenate([src, jnp.full((cols, width), live, jnp.float32)], axis=0).astype(
                    jnp.bfloat16
                )
            )
        out = lax.dot_general(
            jnp.concatenate(lhs, axis=1),
            jnp.concatenate(adjs, axis=1),
            (((1,), (1,)), ((), ())),
            preferred_element_type=jnp.float32,
        )
        deg = out[cols : cols + 1, :]
        nm_ref[r] = (out[:cols, :] / jnp.maximum(deg, 1.0)).astype(nm_ref.dtype)
        deg_ref[r] = deg
        return carry

    lax.fori_loop(0, rows_here, row, 0)


def backward_kernel(ids_ref, cnt_ref, ds_ref, tiles_ref, g_ref):
    step = pl.program_id(0)
    rows_here, slots = tiles_ref.shape[0], tiles_ref.shape[1]
    width = tiles_ref.shape[3]

    @pl.when(step == 0)
    def _():
        g_ref[...] = jnp.zeros_like(g_ref)

    def row(r, carry):
        b = step * rows_here + r
        cnt = cnt_ref[b]
        adjcat = jnp.concatenate([unpack_tile(tiles_ref[r, s]) for s in range(slots)], axis=1)
        res = jnp.dot(ds_ref[r], adjcat, preferred_element_type=jnp.float32)
        for s in range(slots):
            live = jnp.where(s < cnt, 1.0, 0.0)
            t = ids_ref[b * slots + s]
            g_ref[t] = g_ref[t] + res[:, s * width : (s + 1) * width] * live
        return carry

    lax.fori_loop(0, rows_here, row, 0)


def aggregate_forward(ids_flat, counts, feat_t, tiles):
    blocks_here, slots, nwords, width = tiles.shape
    all_blocks, cols, _ = feat_t.shape
    rows = ROWS_PER_STEP
    return pl.pallas_call(
        forward_kernel,
        grid_spec=pltpu.PrefetchScalarGridSpec(
            num_scalar_prefetch=2,
            grid=(blocks_here // rows,),
            in_specs=[
                pl.BlockSpec((all_blocks, cols, width), lambda i, *_: (0, 0, 0)),
                pl.BlockSpec((rows, slots, nwords, width), lambda i, *_: (i, 0, 0, 0)),
            ],
            out_specs=[
                pl.BlockSpec((rows, cols, width), lambda i, *_: (i, 0, 0)),
                pl.BlockSpec((rows, 1, width), lambda i, *_: (i, 0, 0)),
            ],
        ),
        out_shape=[
            jax.ShapeDtypeStruct((blocks_here, cols, width), jnp.bfloat16),
            jax.ShapeDtypeStruct((blocks_here, 1, width), jnp.float32),
        ],
        compiler_params=pltpu.CompilerParams(dimension_semantics=("arbitrary",)),
    )(ids_flat, counts, feat_t, tiles)


def aggregate_backward(ids_flat, counts, ds_blocks, tiles, all_blocks):
    blocks_here, slots, nwords, width = tiles.shape
    cols = ds_blocks.shape[1]
    rows = ROWS_PER_STEP
    return pl.pallas_call(
        backward_kernel,
        grid_spec=pltpu.PrefetchScalarGridSpec(
            num_scalar_prefetch=2,
            grid=(blocks_here // rows,),
            in_specs=[
                pl.BlockSpec((rows, cols, width), lambda i, *_: (i, 0, 0)),
                pl.BlockSpec((rows, slots, nwords, width), lambda i, *_: (i, 0, 0, 0)),
            ],
            out_specs=pl.BlockSpec((all_blocks, cols, width), lambda i, *_: (0, 0, 0)),
        ),
        out_shape=jax.ShapeDtypeStruct((all_blocks, cols, width), jnp.float32),
        compiler_params=pltpu.CompilerParams(dimension_semantics=("arbitrary",)),
    )(ids_flat, counts, ds_blocks, tiles)


def exchange_kernel(parts, kinds, *refs):
    n_in = len(kinds)
    ins, outs = refs[:n_in], refs[n_in : 2 * n_in]
    send_sems, recv_sems = refs[2 * n_in :]
    me = lax.axis_index("feat")
    mesh_id = pl.DeviceIdType.MESH

    barrier = pltpu.get_barrier_semaphore()

    def greet(k, carry):
        peer = lax.rem(me + k, parts)
        pl.semaphore_signal(barrier, 1, device_id={"feat": peer}, device_id_type=mesh_id)
        return carry

    lax.fori_loop(1, parts, greet, 0)
    pl.semaphore_wait(barrier, parts - 1)

    def copy(i, k):
        peer = lax.rem(me + k, parts)
        src = ins[i] if kinds[i] else ins[i].at[peer]
        return pltpu.make_async_remote_copy(
            src_ref=src,
            dst_ref=outs[i].at[me],
            send_sem=send_sems.at[i, k],
            recv_sem=recv_sems.at[i, k],
            device_id={"feat": peer},
            device_id_type=mesh_id,
        )

    def start(k, carry):
        for i in range(n_in):
            copy(i, k).start()
        return carry

    lax.fori_loop(1, parts, start, 0)
    for i in range(n_in):
        outs[i][me] = ins[i][...] if kinds[i] else ins[i][me]

    def finish(k, carry):
        for i in range(n_in):
            copy(i, k).wait()
        return carry

    lax.fori_loop(1, parts, finish, 0)


def exchange(arrays, kinds, parts, cid):
    out_shapes = [
        jax.ShapeDtypeStruct(((parts,) + x.shape) if kind else x.shape, x.dtype)
        for x, kind in zip(arrays, kinds)
    ]
    vmem = pl.BlockSpec(memory_space=pltpu.VMEM)
    return pl.pallas_call(
        functools.partial(exchange_kernel, parts, tuple(kinds)),
        out_shape=out_shapes,
        in_specs=[vmem] * len(arrays),
        out_specs=[vmem] * len(arrays),
        scratch_shapes=[
            pltpu.SemaphoreType.DMA((len(arrays), parts)),
            pltpu.SemaphoreType.DMA((len(arrays), parts)),
        ],
        compiler_params=pltpu.CompilerParams(collective_id=cid, has_side_effects=True),
    )(*arrays)


def forward_exchange_kernel(
    parts, ids_ref, cnt_ref, feat_ref, tiles_ref, w_ref,
    feat_out, nm_out, w_out, deg_ref, nm_scr, send_sems, recv_sems,
):
    me = lax.axis_index("feat")
    group = lax.axis_index("node")
    blocks_here, slots = tiles_ref.shape[0], tiles_ref.shape[1]
    cols, width = feat_ref.shape[1], feat_ref.shape[2]
    per = blocks_here // parts
    mesh_id = pl.DeviceIdType.MESH

    barrier = pltpu.get_barrier_semaphore()

    def greet(k, carry):
        peer = lax.rem(me + k, parts)
        pl.semaphore_signal(barrier, 1, device_id={"feat": peer}, device_id_type=mesh_id)
        return carry

    lax.fori_loop(1, parts, greet, 0)
    pl.semaphore_wait(barrier, parts - 1)

    def copy(i, k):
        peer = lax.rem(me + k, parts)
        if i == 0:
            src, dst = w_ref, w_out
        elif i == 1:
            src, dst = feat_ref.at[pl.ds(group * blocks_here + peer * per, per)], feat_out
        else:
            src, dst = nm_scr.at[pl.ds(peer * per, per)], nm_out
        return pltpu.make_async_remote_copy(
            src_ref=src,
            dst_ref=dst.at[me],
            send_sem=send_sems.at[i, k],
            recv_sem=recv_sems.at[i, k],
            device_id={"feat": peer},
            device_id_type=mesh_id,
        )

    def start_inputs(k, carry):
        copy(0, k).start()
        copy(1, k).start()
        return carry

    lax.fori_loop(1, parts, start_inputs, 0)
    w_out[me] = w_ref[...]
    feat_out[me] = feat_ref[pl.ds(group * blocks_here + me * per, per)]

    def row(b, carry):
        cnt = cnt_ref[b]
        adjs, lhs = [], []
        for s in range(slots):
            live = jnp.where(s < cnt, 1.0, 0.0)
            adjs.append(unpack_tile(tiles_ref[b, s]))
            src = feat_ref[ids_ref[b * slots + s]].astype(jnp.float32) * live
            lhs.append(
                jnp.concatenate([src, jnp.full((cols, width), live, jnp.float32)], axis=0).astype(
                    jnp.bfloat16
                )
            )
        out = lax.dot_general(
            jnp.concatenate(lhs, axis=1),
            jnp.concatenate(adjs, axis=1),
            (((1,), (1,)), ((), ())),
            preferred_element_type=jnp.float32,
        )
        deg = out[cols : cols + 1, :]
        nm_scr[b] = (out[:cols, :] / jnp.maximum(deg, 1.0)).astype(nm_scr.dtype)
        deg_ref[b] = deg
        return carry

    lax.fori_loop(0, blocks_here, row, 0)

    def start_result(k, carry):
        copy(2, k).start()
        return carry

    lax.fori_loop(1, parts, start_result, 0)
    nm_out[me] = nm_scr[pl.ds(me * per, per)]

    def finish(k, carry):
        for i in range(3):
            copy(i, k).wait()
        return carry

    lax.fori_loop(1, parts, finish, 0)


def forward_exchange(ids_flat, counts, feat_t, tiles, w_both, parts):
    blocks_here, slots, nwords, width = tiles.shape
    all_blocks, cols, _ = feat_t.shape
    per = blocks_here // parts
    vmem = pl.BlockSpec(memory_space=pltpu.VMEM)
    smem = pl.BlockSpec(memory_space=pltpu.SMEM)
    return pl.pallas_call(
        functools.partial(forward_exchange_kernel, parts),
        out_shape=[
            jax.ShapeDtypeStruct((parts, per, cols, width), jnp.bfloat16),
            jax.ShapeDtypeStruct((parts, per, cols, width), jnp.bfloat16),
            jax.ShapeDtypeStruct((parts,) + w_both.shape, w_both.dtype),
            jax.ShapeDtypeStruct((blocks_here, 1, width), jnp.float32),
        ],
        in_specs=[smem, smem, vmem, vmem, vmem],
        out_specs=[vmem] * 4,
        scratch_shapes=[
            pltpu.VMEM((blocks_here, cols, width), jnp.bfloat16),
            pltpu.SemaphoreType.DMA((3, parts)),
            pltpu.SemaphoreType.DMA((3, parts)),
        ],
        compiler_params=pltpu.CompilerParams(collective_id=0, has_side_effects=True),
    )(ids_flat, counts, feat_t, tiles, w_both)


def shards(features, w_self, w_neigh, bias, d_out, nbr_ids, nbr_count, tiles):
    node_total, cols = features.shape
    hidden = w_self.shape[1]
    block_size = tiles.shape[3]
    blocks_here = nbr_ids.shape[0]
    all_blocks = node_total // block_size
    node_group = lax.axis_index("node")
    feat_index = lax.axis_index("feat")
    feat_parts = lax.axis_size("feat")
    per = blocks_here // feat_parts
    own_nodes = per * block_size

    feat_t = features.reshape(all_blocks, block_size, cols).transpose(0, 2, 1)
    ids_flat = nbr_ids.reshape(-1)

    w_both = jnp.concatenate([w_self, w_neigh], axis=1)
    feat_got, nm_got, w_all, deg_blocks = forward_exchange(
        ids_flat, nbr_count, feat_t, tiles, w_both, feat_parts
    )
    w_all = w_all.reshape(feat_parts * cols, 2 * hidden)
    w_self_all = w_all[:, :hidden]
    w_neigh_all = w_all[:, hidden:]
    own_feat = feat_got.transpose(1, 3, 0, 2).reshape(own_nodes, feat_parts * cols)
    own_nm = nm_got.transpose(1, 3, 0, 2).reshape(own_nodes, feat_parts * cols)

    pre_act = (
        jnp.dot(own_feat, w_self_all, preferred_element_type=jnp.float32)
        + jnp.dot(own_nm, w_neigh_all, preferred_element_type=jnp.float32)
        + bias
    )
    activated = jax.nn.elu(pre_act).astype(jnp.bfloat16)
    elu_slope = jnp.where(pre_act > 0, 1.0, jnp.exp(jnp.minimum(pre_act, 0.0)))
    dpre = (d_out.astype(jnp.float32) * elu_slope).astype(jnp.bfloat16)

    contract_cols = (((1,), (1,)), ((), ()))
    d_self_t = lax.dot_general(
        w_self_all, dpre, contract_cols, preferred_element_type=jnp.float32
    ).astype(jnp.bfloat16)
    d_neigh_t = lax.dot_general(
        w_neigh_all, dpre, contract_cols, preferred_element_type=jnp.float32
    ).astype(jnp.bfloat16)
    own_deg = lax.dynamic_slice_in_dim(deg_blocks, feat_index * per, per, 0).reshape(1, -1)
    d_scaled_t = (d_neigh_t.astype(jnp.float32) / jnp.maximum(own_deg, 1.0)).astype(jnp.bfloat16)

    contract_rows = (((0,), (0,)), ((), ()))
    part = jnp.concatenate(
        [
            lax.dot_general(own_feat, dpre, contract_rows, preferred_element_type=jnp.float32),
            lax.dot_general(own_nm, dpre, contract_rows, preferred_element_type=jnp.float32),
        ],
        axis=1,
    )
    lanes = part.shape[1] // block_size
    back = (
        jnp.stack([d_self_t, d_scaled_t], axis=0)
        .reshape(2, feat_parts, cols, per, block_size)
        .transpose(1, 3, 0, 2, 4)
        .reshape(feat_parts, per * 2, cols, block_size)
        .astype(jnp.float32)
    )
    part_tiles = part.reshape(feat_parts, cols, lanes, block_size).transpose(0, 2, 1, 3)
    got_back = lax.all_to_all(
        jnp.concatenate([back, part_tiles], axis=1), "feat", 0, 0, tiled=True
    )
    d_blocks = got_back[:, : per * 2].astype(jnp.bfloat16).reshape(blocks_here, 2, cols, block_size)
    d_self_blocks = d_blocks[:, 0]
    d_scaled_blocks = d_blocks[:, 1]
    part_sum = jnp.sum(got_back[:, per * 2 :], axis=0).transpose(1, 0, 2).reshape(cols, lanes * block_size)
    grads = lax.psum(part_sum, "node")
    grad_scale = 1.0 / math.sqrt(node_total)
    grad_self = grads[:, :hidden] * grad_scale
    grad_neigh = grads[:, hidden:] * grad_scale

    grad_all = aggregate_backward(ids_flat, nbr_count, d_scaled_blocks, tiles, all_blocks)
    grad_group = lax.psum_scatter(grad_all, "node", scatter_dimension=0, tiled=True)
    grad_group = grad_group + d_self_blocks.astype(jnp.float32)
    grad_features = grad_group.transpose(0, 2, 1).reshape(-1, cols)
    return (activated, grad_features, grad_self, grad_neigh)


def solution(mesh):
    placed = (
        P(None, "feat"),
        P("feat", None),
        P("feat", None),
        P(),
        P(("node", "feat"), None),
        P("node", None),
        P("node"),
        P("node", None, None, None),
    )
    return jax.shard_map(
        shards,
        mesh=mesh,
        in_specs=placed,
        out_specs=(P(("node", "feat"), None), P("node", "feat"), P("feat", None), P("feat", None)),
        check_vma=False,
    )
```

```python
import functools
import math

import jax
import jax.numpy as jnp
from jax import lax
from jax.experimental import pallas as pl
from jax.experimental.pallas import tpu as pltpu
from jax.sharding import PartitionSpec as P

ROWS_PER_STEP = 8


def unpack_tile(words):
    nwords, width = words.shape
    shifts = lax.broadcasted_iota(jnp.int32, (16, width), 0)
    rows = [
        jnp.bitwise_and(jnp.right_shift(jnp.broadcast_to(words[w : w + 1, :], (16, width)), shifts), 1)
        for w in range(nwords)
    ]
    return jnp.concatenate(rows, axis=0).astype(jnp.float32).astype(jnp.bfloat16)


def forward_kernel(ids_ref, cnt_ref, feat_ref, tiles_ref, nm_ref, deg_ref):
    step = pl.program_id(0)
    rows_here, slots = tiles_ref.shape[0], tiles_ref.shape[1]
    cols, width = feat_ref.shape[1], feat_ref.shape[2]

    def row(r, carry):
        b = step * rows_here + r
        cnt = cnt_ref[b]
        adjs, lhs = [], []
        for s in range(slots):
            live = jnp.where(s < cnt, 1.0, 0.0)
            adjs.append(unpack_tile(tiles_ref[r, s]))
            src = feat_ref[ids_ref[b * slots + s]].astype(jnp.float32) * live
            lhs.append(
                jnp.concatenate([src, jnp.full((cols, width), live, jnp.float32)], axis=0).astype(
                    jnp.bfloat16
                )
            )
        out = lax.dot_general(
            jnp.concatenate(lhs, axis=1),
            jnp.concatenate(adjs, axis=1),
            (((1,), (1,)), ((), ())),
            preferred_element_type=jnp.float32,
        )
        deg = out[cols : cols + 1, :]
        nm_ref[r] = (out[:cols, :] / jnp.maximum(deg, 1.0)).astype(nm_ref.dtype)
        deg_ref[r] = deg
        return carry

    lax.fori_loop(0, rows_here, row, 0)


def backward_kernel(ids_ref, cnt_ref, ds_ref, tiles_ref, g_ref):
    step = pl.program_id(0)
    rows_here, slots = tiles_ref.shape[0], tiles_ref.shape[1]
    width = tiles_ref.shape[3]

    @pl.when(step == 0)
    def _():
        g_ref[...] = jnp.zeros_like(g_ref)

    def row(r, carry):
        b = step * rows_here + r
        cnt = cnt_ref[b]
        adjcat = jnp.concatenate([unpack_tile(tiles_ref[r, s]) for s in range(slots)], axis=1)
        res = jnp.dot(ds_ref[r], adjcat, preferred_element_type=jnp.float32)
        for s in range(slots):
            live = jnp.where(s < cnt, 1.0, 0.0)
            t = ids_ref[b * slots + s]
            g_ref[t] = g_ref[t] + res[:, s * width : (s + 1) * width] * live
        return carry

    lax.fori_loop(0, rows_here, row, 0)


def aggregate_forward(ids_flat, counts, feat_t, tiles):
    blocks_here, slots, nwords, width = tiles.shape
    all_blocks, cols, _ = feat_t.shape
    rows = ROWS_PER_STEP
    return pl.pallas_call(
        forward_kernel,
        grid_spec=pltpu.PrefetchScalarGridSpec(
            num_scalar_prefetch=2,
            grid=(blocks_here // rows,),
            in_specs=[
                pl.BlockSpec((all_blocks, cols, width), lambda i, *_: (0, 0, 0)),
                pl.BlockSpec((rows, slots, nwords, width), lambda i, *_: (i, 0, 0, 0)),
            ],
            out_specs=[
                pl.BlockSpec((rows, cols, width), lambda i, *_: (i, 0, 0)),
                pl.BlockSpec((rows, 1, width), lambda i, *_: (i, 0, 0)),
            ],
        ),
        out_shape=[
            jax.ShapeDtypeStruct((blocks_here, cols, width), jnp.bfloat16),
            jax.ShapeDtypeStruct((blocks_here, 1, width), jnp.float32),
        ],
        compiler_params=pltpu.CompilerParams(dimension_semantics=("arbitrary",)),
    )(ids_flat, counts, feat_t, tiles)


def aggregate_backward(ids_flat, counts, ds_blocks, tiles, all_blocks):
    blocks_here, slots, nwords, width = tiles.shape
    cols = ds_blocks.shape[1]
    rows = ROWS_PER_STEP
    return pl.pallas_call(
        backward_kernel,
        grid_spec=pltpu.PrefetchScalarGridSpec(
            num_scalar_prefetch=2,
            grid=(blocks_here // rows,),
            in_specs=[
                pl.BlockSpec((rows, cols, width), lambda i, *_: (i, 0, 0)),
                pl.BlockSpec((rows, slots, nwords, width), lambda i, *_: (i, 0, 0, 0)),
            ],
            out_specs=pl.BlockSpec((all_blocks, cols, width), lambda i, *_: (0, 0, 0)),
        ),
        out_shape=jax.ShapeDtypeStruct((all_blocks, cols, width), jnp.float32),
        compiler_params=pltpu.CompilerParams(dimension_semantics=("arbitrary",)),
    )(ids_flat, counts, ds_blocks, tiles)


def exchange_kernel(parts, kinds, *refs):
    n_in = len(kinds)
    ins, outs = refs[:n_in], refs[n_in : 2 * n_in]
    send_sems, recv_sems = refs[2 * n_in :]
    me = lax.axis_index("feat")
    mesh_id = pl.DeviceIdType.MESH

    barrier = pltpu.get_barrier_semaphore()

    def greet(k, carry):
        peer = lax.rem(me + k, parts)
        pl.semaphore_signal(barrier, 1, device_id={"feat": peer}, device_id_type=mesh_id)
        return carry

    lax.fori_loop(1, parts, greet, 0)
    pl.semaphore_wait(barrier, parts - 1)

    def copy(i, k):
        peer = lax.rem(me + k, parts)
        src = ins[i] if kinds[i] else ins[i].at[peer]
        return pltpu.make_async_remote_copy(
            src_ref=src,
            dst_ref=outs[i].at[me],
            send_sem=send_sems.at[i, k],
            recv_sem=recv_sems.at[i, k],
            device_id={"feat": peer},
            device_id_type=mesh_id,
        )

    def start(k, carry):
        for i in range(n_in):
            copy(i, k).start()
        return carry

    lax.fori_loop(1, parts, start, 0)
    for i in range(n_in):
        outs[i][me] = ins[i][...] if kinds[i] else ins[i][me]

    def finish(k, carry):
        for i in range(n_in):
            copy(i, k).wait()
        return carry

    lax.fori_loop(1, parts, finish, 0)


def exchange(arrays, kinds, parts, cid):
    out_shapes = [
        jax.ShapeDtypeStruct(((parts,) + x.shape) if kind else x.shape, x.dtype)
        for x, kind in zip(arrays, kinds)
    ]
    vmem = pl.BlockSpec(memory_space=pltpu.VMEM)
    return pl.pallas_call(
        functools.partial(exchange_kernel, parts, tuple(kinds)),
        out_shape=out_shapes,
        in_specs=[vmem] * len(arrays),
        out_specs=[vmem] * len(arrays),
        scratch_shapes=[
            pltpu.SemaphoreType.DMA((len(arrays), parts)),
            pltpu.SemaphoreType.DMA((len(arrays), parts)),
        ],
        compiler_params=pltpu.CompilerParams(collective_id=cid, has_side_effects=True),
    )(*arrays)


def forward_exchange_kernel(
    parts, ids_ref, cnt_ref, feat_ref, tiles_ref, w_ref,
    feat_out, nm_out, w_out, deg_ref, nm_scr, send_sems, recv_sems,
):
    me = lax.axis_index("feat")
    group = lax.axis_index("node")
    blocks_here, slots = tiles_ref.shape[0], tiles_ref.shape[1]
    cols, width = feat_ref.shape[1], feat_ref.shape[2]
    per = blocks_here // parts
    mesh_id = pl.DeviceIdType.MESH

    barrier = pltpu.get_barrier_semaphore()

    def greet(k, carry):
        peer = lax.rem(me + k, parts)
        pl.semaphore_signal(barrier, 1, device_id={"feat": peer}, device_id_type=mesh_id)
        return carry

    lax.fori_loop(1, parts, greet, 0)
    pl.semaphore_wait(barrier, parts - 1)

    half = parts // 2
    par = lax.rem(me, 2)
    sibling = me + 1 - 2 * par

    def copy(i, k):
        if i == 0:
            peer = lax.rem(me + 2 * k, parts)
            src, dst = w_ref, w_out.at[par, me // 2]
        elif i == 1:
            peer = lax.rem(me + k, parts)
            src = feat_ref.at[pl.ds(group * blocks_here + peer * per, per)]
            dst = feat_out.at[me]
        else:
            peer = lax.rem(me + k, parts)
            src, dst = nm_scr.at[pl.ds(peer * per, per)], nm_out.at[me]
        return pltpu.make_async_remote_copy(
            src_ref=src,
            dst_ref=dst,
            send_sem=send_sems.at[i, k],
            recv_sem=recv_sems.at[i, k],
            device_id={"feat": peer},
            device_id_type=mesh_id,
        )

    def start_weights(k, carry):
        copy(0, k).start()
        return carry

    def start_feat(k, carry):
        copy(1, k).start()
        return carry

    lax.fori_loop(1, half, start_weights, 0)
    lax.fori_loop(1, parts, start_feat, 0)
    own_w = pltpu.make_async_copy(w_ref, w_out.at[par, me // 2], send_sems.at[3, 0])
    own_w.start()
    feat_out[me] = feat_ref[pl.ds(group * blocks_here + me * per, per)]

    def row(b, carry):
        cnt = cnt_ref[b]
        adjs, lhs = [], []
        for s in range(slots):
            live = jnp.where(s < cnt, 1.0, 0.0)
            adjs.append(unpack_tile(tiles_ref[b, s]))
            src = feat_ref[ids_ref[b * slots + s]].astype(jnp.float32) * live
            lhs.append(
                jnp.concatenate([src, jnp.full((cols, width), live, jnp.float32)], axis=0).astype(
                    jnp.bfloat16
                )
            )
        out = lax.dot_general(
            jnp.concatenate(lhs, axis=1),
            jnp.concatenate(adjs, axis=1),
            (((1,), (1,)), ((), ())),
            preferred_element_type=jnp.float32,
        )
        deg = out[cols : cols + 1, :]
        nm_scr[b] = (out[:cols, :] / jnp.maximum(deg, 1.0)).astype(nm_scr.dtype)
        deg_ref[b] = deg
        return carry

    lax.fori_loop(0, blocks_here, row, 0)

    def finish_weights(k, carry):
        copy(0, k).wait()
        return carry

    lax.fori_loop(1, half, finish_weights, 0)
    own_w.wait()
    to_sibling = pltpu.make_async_remote_copy(
        src_ref=w_out.at[par],
        dst_ref=w_out.at[par],
        send_sem=send_sems.at[3, 1],
        recv_sem=recv_sems.at[3, 1],
        device_id={"feat": sibling},
        device_id_type=mesh_id,
    )
    to_sibling.start()

    def start_result(k, carry):
        copy(2, k).start()
        return carry

    lax.fori_loop(1, parts, start_result, 0)
    nm_out[me] = nm_scr[pl.ds(me * per, per)]

    def finish(k, carry):
        copy(1, k).wait()
        copy(2, k).wait()
        return carry

    lax.fori_loop(1, parts, finish, 0)
    to_sibling.wait()


def forward_exchange(ids_flat, counts, feat_t, tiles, w_both, parts):
    blocks_here, slots, nwords, width = tiles.shape
    all_blocks, cols, _ = feat_t.shape
    per = blocks_here // parts
    vmem = pl.BlockSpec(memory_space=pltpu.VMEM)
    smem = pl.BlockSpec(memory_space=pltpu.SMEM)
    return pl.pallas_call(
        functools.partial(forward_exchange_kernel, parts),
        out_shape=[
            jax.ShapeDtypeStruct((parts, per, cols, width), jnp.bfloat16),
            jax.ShapeDtypeStruct((parts, per, cols, width), jnp.bfloat16),
            jax.ShapeDtypeStruct((2, parts // 2) + w_both.shape, w_both.dtype),
            jax.ShapeDtypeStruct((blocks_here, 1, width), jnp.float32),
        ],
        in_specs=[smem, smem, vmem, vmem, vmem],
        out_specs=[vmem] * 4,
        scratch_shapes=[
            pltpu.VMEM((blocks_here, cols, width), jnp.bfloat16),
            pltpu.SemaphoreType.DMA((4, parts)),
            pltpu.SemaphoreType.DMA((4, parts)),
        ],
        compiler_params=pltpu.CompilerParams(collective_id=0, has_side_effects=True),
    )(ids_flat, counts, feat_t, tiles, w_both)


def shards(features, w_self, w_neigh, bias, d_out, nbr_ids, nbr_count, tiles):
    node_total, cols = features.shape
    hidden = w_self.shape[1]
    block_size = tiles.shape[3]
    blocks_here = nbr_ids.shape[0]
    all_blocks = node_total // block_size
    node_group = lax.axis_index("node")
    feat_index = lax.axis_index("feat")
    feat_parts = lax.axis_size("feat")
    per = blocks_here // feat_parts
    own_nodes = per * block_size

    feat_t = features.reshape(all_blocks, block_size, cols).transpose(0, 2, 1)
    ids_flat = nbr_ids.reshape(-1)

    w_both = jnp.concatenate([w_self, w_neigh], axis=1)
    feat_got, nm_got, w_all, deg_blocks = forward_exchange(
        ids_flat, nbr_count, feat_t, tiles, w_both, feat_parts
    )
    w_all = w_all.transpose(1, 0, 2, 3).reshape(feat_parts * cols, 2 * hidden)
    w_self_all = w_all[:, :hidden]
    w_neigh_all = w_all[:, hidden:]
    own_feat = feat_got.transpose(1, 3, 0, 2).reshape(own_nodes, feat_parts * cols)
    own_nm = nm_got.transpose(1, 3, 0, 2).reshape(own_nodes, feat_parts * cols)

    pre_act = (
        jnp.dot(own_feat, w_self_all, preferred_element_type=jnp.float32)
        + jnp.dot(own_nm, w_neigh_all, preferred_element_type=jnp.float32)
        + bias
    )
    activated = jax.nn.elu(pre_act).astype(jnp.bfloat16)
    elu_slope = jnp.where(pre_act > 0, 1.0, jnp.exp(jnp.minimum(pre_act, 0.0)))
    dpre = (d_out.astype(jnp.float32) * elu_slope).astype(jnp.bfloat16)

    contract_cols = (((1,), (1,)), ((), ()))
    d_self_t = lax.dot_general(
        w_self_all, dpre, contract_cols, preferred_element_type=jnp.float32
    ).astype(jnp.bfloat16)
    d_neigh_t = lax.dot_general(
        w_neigh_all, dpre, contract_cols, preferred_element_type=jnp.float32
    ).astype(jnp.bfloat16)
    own_deg = lax.dynamic_slice_in_dim(deg_blocks, feat_index * per, per, 0).reshape(1, -1)
    d_scaled_t = (d_neigh_t.astype(jnp.float32) / jnp.maximum(own_deg, 1.0)).astype(jnp.bfloat16)

    contract_rows = (((0,), (0,)), ((), ()))
    part = jnp.concatenate(
        [
            lax.dot_general(own_feat, dpre, contract_rows, preferred_element_type=jnp.float32),
            lax.dot_general(own_nm, dpre, contract_rows, preferred_element_type=jnp.float32),
        ],
        axis=1,
    )
    part_got = lax.all_to_all(part.reshape(feat_parts, cols, 2 * hidden), "feat", 0, 0, tiled=True)
    grads = lax.psum(jnp.sum(part_got, axis=0), "node")
    grad_scale = 1.0 / math.sqrt(node_total)
    grad_self = grads[:, :hidden] * grad_scale
    grad_neigh = grads[:, hidden:] * grad_scale

    back = (
        jnp.stack([d_self_t, d_scaled_t], axis=0)
        .reshape(2, feat_parts, cols, per, block_size)
        .transpose(1, 3, 0, 2, 4)
    )
    got_back = lax.all_to_all(back, "feat", 0, 0, tiled=True).reshape(blocks_here, 2, cols, block_size)
    d_self_blocks = got_back[:, 0]
    d_scaled_blocks = got_back[:, 1]

    grad_all = aggregate_backward(ids_flat, nbr_count, d_scaled_blocks, tiles, all_blocks)
    grad_group = lax.psum_scatter(grad_all, "node", scatter_dimension=0, tiled=True)
    grad_group = grad_group + d_self_blocks.astype(jnp.float32)
    grad_features = grad_group.transpose(0, 2, 1).reshape(-1, cols)
    return (activated, grad_features, grad_self, grad_neigh)


def solution(mesh):
    placed = (
        P(None, "feat"),
        P("feat", None),
        P("feat", None),
        P(),
        P(("node", "feat"), None),
        P("node", None),
        P("node"),
        P("node", None, None, None),
    )
    return jax.shard_map(
        shards,
        mesh=mesh,
        in_specs=placed,
        out_specs=(P(("node", "feat"), None), P("node", "feat"), P("feat", None), P("feat", None)),
        check_vma=False,
    )
```

```python
import functools
import math

import jax
import jax.numpy as jnp
from jax import lax
from jax.experimental import pallas as pl
from jax.experimental.pallas import tpu as pltpu
from jax.sharding import PartitionSpec as P

ROWS_PER_STEP = 8


def unpack_tile(words):
    nwords, width = words.shape
    shifts = lax.broadcasted_iota(jnp.int32, (16, width), 0)
    rows = [
        jnp.bitwise_and(jnp.right_shift(jnp.broadcast_to(words[w : w + 1, :], (16, width)), shifts), 1)
        for w in range(nwords)
    ]
    return jnp.concatenate(rows, axis=0).astype(jnp.float32).astype(jnp.bfloat16)


def forward_kernel(ids_ref, cnt_ref, feat_ref, tiles_ref, nm_ref, deg_ref):
    step = pl.program_id(0)
    rows_here, slots = tiles_ref.shape[0], tiles_ref.shape[1]
    cols, width = feat_ref.shape[1], feat_ref.shape[2]

    def row(r, carry):
        b = step * rows_here + r
        cnt = cnt_ref[b]
        adjs, lhs = [], []
        for s in range(slots):
            live = jnp.where(s < cnt, 1.0, 0.0)
            adjs.append(unpack_tile(tiles_ref[r, s]))
            src = feat_ref[ids_ref[b * slots + s]].astype(jnp.float32) * live
            lhs.append(
                jnp.concatenate([src, jnp.full((cols, width), live, jnp.float32)], axis=0).astype(
                    jnp.bfloat16
                )
            )
        out = lax.dot_general(
            jnp.concatenate(lhs, axis=1),
            jnp.concatenate(adjs, axis=1),
            (((1,), (1,)), ((), ())),
            preferred_element_type=jnp.float32,
        )
        deg = out[cols : cols + 1, :]
        nm_ref[r] = (out[:cols, :] / jnp.maximum(deg, 1.0)).astype(nm_ref.dtype)
        deg_ref[r] = deg
        return carry

    lax.fori_loop(0, rows_here, row, 0)


def backward_kernel(ids_ref, cnt_ref, ds_ref, tiles_ref, g_ref):
    step = pl.program_id(0)
    rows_here, slots = tiles_ref.shape[0], tiles_ref.shape[1]
    width = tiles_ref.shape[3]

    @pl.when(step == 0)
    def _():
        g_ref[...] = jnp.zeros_like(g_ref)

    def row(r, carry):
        b = step * rows_here + r
        cnt = cnt_ref[b]
        adjcat = jnp.concatenate([unpack_tile(tiles_ref[r, s]) for s in range(slots)], axis=1)
        res = jnp.dot(ds_ref[r], adjcat, preferred_element_type=jnp.float32)
        for s in range(slots):
            live = jnp.where(s < cnt, 1.0, 0.0)
            t = ids_ref[b * slots + s]
            g_ref[t] = g_ref[t] + res[:, s * width : (s + 1) * width] * live
        return carry

    lax.fori_loop(0, rows_here, row, 0)


def aggregate_forward(ids_flat, counts, feat_t, tiles):
    blocks_here, slots, nwords, width = tiles.shape
    all_blocks, cols, _ = feat_t.shape
    rows = ROWS_PER_STEP
    return pl.pallas_call(
        forward_kernel,
        grid_spec=pltpu.PrefetchScalarGridSpec(
            num_scalar_prefetch=2,
            grid=(blocks_here // rows,),
            in_specs=[
                pl.BlockSpec((all_blocks, cols, width), lambda i, *_: (0, 0, 0)),
                pl.BlockSpec((rows, slots, nwords, width), lambda i, *_: (i, 0, 0, 0)),
            ],
            out_specs=[
                pl.BlockSpec((rows, cols, width), lambda i, *_: (i, 0, 0)),
                pl.BlockSpec((rows, 1, width), lambda i, *_: (i, 0, 0)),
            ],
        ),
        out_shape=[
            jax.ShapeDtypeStruct((blocks_here, cols, width), jnp.bfloat16),
            jax.ShapeDtypeStruct((blocks_here, 1, width), jnp.float32),
        ],
        compiler_params=pltpu.CompilerParams(dimension_semantics=("arbitrary",)),
    )(ids_flat, counts, feat_t, tiles)


def aggregate_backward(ids_flat, counts, ds_blocks, tiles, all_blocks):
    blocks_here, slots, nwords, width = tiles.shape
    cols = ds_blocks.shape[1]
    rows = ROWS_PER_STEP
    return pl.pallas_call(
        backward_kernel,
        grid_spec=pltpu.PrefetchScalarGridSpec(
            num_scalar_prefetch=2,
            grid=(blocks_here // rows,),
            in_specs=[
                pl.BlockSpec((rows, cols, width), lambda i, *_: (i, 0, 0)),
                pl.BlockSpec((rows, slots, nwords, width), lambda i, *_: (i, 0, 0, 0)),
            ],
            out_specs=pl.BlockSpec((all_blocks, cols, width), lambda i, *_: (0, 0, 0)),
        ),
        out_shape=jax.ShapeDtypeStruct((all_blocks, cols, width), jnp.float32),
        compiler_params=pltpu.CompilerParams(dimension_semantics=("arbitrary",)),
    )(ids_flat, counts, ds_blocks, tiles)


def exchange_kernel(parts, kinds, *refs):
    n_in = len(kinds)
    ins, outs = refs[:n_in], refs[n_in : 2 * n_in]
    send_sems, recv_sems = refs[2 * n_in :]
    me = lax.axis_index("feat")
    mesh_id = pl.DeviceIdType.MESH

    barrier = pltpu.get_barrier_semaphore()

    def greet(k, carry):
        peer = lax.rem(me + k, parts)
        pl.semaphore_signal(barrier, 1, device_id={"feat": peer}, device_id_type=mesh_id)
        return carry

    lax.fori_loop(1, parts, greet, 0)
    pl.semaphore_wait(barrier, parts - 1)

    def copy(i, k):
        peer = lax.rem(me + k, parts)
        src = ins[i] if kinds[i] else ins[i].at[peer]
        return pltpu.make_async_remote_copy(
            src_ref=src,
            dst_ref=outs[i].at[me],
            send_sem=send_sems.at[i, k],
            recv_sem=recv_sems.at[i, k],
            device_id={"feat": peer},
            device_id_type=mesh_id,
        )

    def start(k, carry):
        for i in range(n_in):
            copy(i, k).start()
        return carry

    lax.fori_loop(1, parts, start, 0)
    for i in range(n_in):
        outs[i][me] = ins[i][...] if kinds[i] else ins[i][me]

    def finish(k, carry):
        for i in range(n_in):
            copy(i, k).wait()
        return carry

    lax.fori_loop(1, parts, finish, 0)


def exchange(arrays, kinds, parts, cid):
    out_shapes = [
        jax.ShapeDtypeStruct(((parts,) + x.shape) if kind else x.shape, x.dtype)
        for x, kind in zip(arrays, kinds)
    ]
    vmem = pl.BlockSpec(memory_space=pltpu.VMEM)
    return pl.pallas_call(
        functools.partial(exchange_kernel, parts, tuple(kinds)),
        out_shape=out_shapes,
        in_specs=[vmem] * len(arrays),
        out_specs=[vmem] * len(arrays),
        scratch_shapes=[
            pltpu.SemaphoreType.DMA((len(arrays), parts)),
            pltpu.SemaphoreType.DMA((len(arrays), parts)),
        ],
        compiler_params=pltpu.CompilerParams(collective_id=cid, has_side_effects=True),
    )(*arrays)


def forward_exchange_kernel(
    parts, ids_ref, cnt_ref, feat_ref, tiles_ref, w_ref,
    feat_out, nm_out, w_out, deg_ref, nm_scr, send_sems, recv_sems,
):
    me = lax.axis_index("feat")
    group = lax.axis_index("node")
    blocks_here, slots = tiles_ref.shape[0], tiles_ref.shape[1]
    cols, width = feat_ref.shape[1], feat_ref.shape[2]
    per = blocks_here // parts
    mesh_id = pl.DeviceIdType.MESH

    barrier = pltpu.get_barrier_semaphore()

    def greet(k, carry):
        peer = lax.rem(me + k, parts)
        pl.semaphore_signal(barrier, 1, device_id={"feat": peer}, device_id_type=mesh_id)
        return carry

    lax.fori_loop(1, parts, greet, 0)
    pl.semaphore_wait(barrier, parts - 1)

    half = parts // 2
    par = lax.rem(me, 2)
    sibling = me + 1 - 2 * par

    def copy(i, k):
        if i == 0:
            peer = lax.rem(me + 2 * k, parts)
            src, dst = w_ref, w_out.at[par, me // 2]
        elif i == 1:
            peer = lax.rem(me + k, parts)
            src = feat_ref.at[pl.ds(group * blocks_here + peer * per, per)]
            dst = feat_out.at[me]
        else:
            peer = lax.rem(me + k, parts)
            src, dst = nm_scr.at[pl.ds(peer * per, per)], nm_out.at[me]
        return pltpu.make_async_remote_copy(
            src_ref=src,
            dst_ref=dst,
            send_sem=send_sems.at[i, k],
            recv_sem=recv_sems.at[i, k],
            device_id={"feat": peer},
            device_id_type=mesh_id,
        )

    def start_weights(k, carry):
        copy(0, k).start()
        return carry

    def start_feat(k, carry):
        copy(1, k).start()
        return carry

    lax.fori_loop(1, half, start_weights, 0)
    lax.fori_loop(1, parts, start_feat, 0)
    own_w = pltpu.make_async_copy(w_ref, w_out.at[par, me // 2], send_sems.at[3, 0])
    own_w.start()
    feat_out[me] = feat_ref[pl.ds(group * blocks_here + me * per, per)]

    def row(b, carry):
        cnt = cnt_ref[b]
        adjs, lhs = [], []
        for s in range(slots):
            live = jnp.where(s < cnt, 1.0, 0.0)
            adjs.append(unpack_tile(tiles_ref[b, s]))
            src = feat_ref[ids_ref[b * slots + s]].astype(jnp.float32) * live
            lhs.append(
                jnp.concatenate([src, jnp.full((cols, width), live, jnp.float32)], axis=0).astype(
                    jnp.bfloat16
                )
            )
        out = lax.dot_general(
            jnp.concatenate(lhs, axis=1),
            jnp.concatenate(adjs, axis=1),
            (((1,), (1,)), ((), ())),
            preferred_element_type=jnp.float32,
        )
        deg = out[cols : cols + 1, :]
        nm_scr[b] = (out[:cols, :] / jnp.maximum(deg, 1.0)).astype(nm_scr.dtype)
        deg_ref[b] = deg
        return carry

    lax.fori_loop(0, blocks_here, row, 0)

    def finish_weights(k, carry):
        copy(0, k).wait()
        return carry

    lax.fori_loop(1, half, finish_weights, 0)
    own_w.wait()
    to_sibling = pltpu.make_async_remote_copy(
        src_ref=w_out.at[par],
        dst_ref=w_out.at[par],
        send_sem=send_sems.at[3, 1],
        recv_sem=recv_sems.at[3, 1],
        device_id={"feat": sibling},
        device_id_type=mesh_id,
    )
    to_sibling.start()

    def start_result(k, carry):
        copy(2, k).start()
        return carry

    lax.fori_loop(1, parts, start_result, 0)
    nm_out[me] = nm_scr[pl.ds(me * per, per)]

    def finish(k, carry):
        copy(1, k).wait()
        copy(2, k).wait()
        return carry

    lax.fori_loop(1, parts, finish, 0)
    to_sibling.wait()


def forward_exchange(ids_flat, counts, feat_t, tiles, w_both, parts):
    blocks_here, slots, nwords, width = tiles.shape
    all_blocks, cols, _ = feat_t.shape
    per = blocks_here // parts
    vmem = pl.BlockSpec(memory_space=pltpu.VMEM)
    smem = pl.BlockSpec(memory_space=pltpu.SMEM)
    return pl.pallas_call(
        functools.partial(forward_exchange_kernel, parts),
        out_shape=[
            jax.ShapeDtypeStruct((parts, per, cols, width), jnp.bfloat16),
            jax.ShapeDtypeStruct((parts, per, cols, width), jnp.bfloat16),
            jax.ShapeDtypeStruct((2, parts // 2) + w_both.shape, w_both.dtype),
            jax.ShapeDtypeStruct((blocks_here, 1, width), jnp.float32),
        ],
        in_specs=[smem, smem, vmem, vmem, vmem],
        out_specs=[vmem] * 4,
        scratch_shapes=[
            pltpu.VMEM((blocks_here, cols, width), jnp.bfloat16),
            pltpu.SemaphoreType.DMA((4, parts)),
            pltpu.SemaphoreType.DMA((4, parts)),
        ],
        compiler_params=pltpu.CompilerParams(collective_id=0, has_side_effects=True),
    )(ids_flat, counts, feat_t, tiles, w_both)


def shards(features, w_self, w_neigh, bias, d_out, nbr_ids, nbr_count, tiles):
    node_total, cols = features.shape
    hidden = w_self.shape[1]
    block_size = tiles.shape[3]
    blocks_here = nbr_ids.shape[0]
    all_blocks = node_total // block_size
    node_group = lax.axis_index("node")
    feat_index = lax.axis_index("feat")
    feat_parts = lax.axis_size("feat")
    per = blocks_here // feat_parts
    own_nodes = per * block_size

    feat_t = features.reshape(all_blocks, block_size, cols).transpose(0, 2, 1)
    ids_flat = nbr_ids.reshape(-1)

    w_both = jnp.concatenate([w_self, w_neigh], axis=1)
    feat_got, nm_got, w_all, deg_blocks = forward_exchange(
        ids_flat, nbr_count, feat_t, tiles, w_both, feat_parts
    )
    w_all = w_all.transpose(1, 0, 2, 3).reshape(feat_parts * cols, 2 * hidden)
    w_self_all = w_all[:, :hidden]
    w_neigh_all = w_all[:, hidden:]
    own_feat = feat_got.transpose(1, 3, 0, 2).reshape(own_nodes, feat_parts * cols)
    own_nm = nm_got.transpose(1, 3, 0, 2).reshape(own_nodes, feat_parts * cols)

    pre_act = (
        jnp.dot(own_feat, w_self_all, preferred_element_type=jnp.float32)
        + jnp.dot(own_nm, w_neigh_all, preferred_element_type=jnp.float32)
        + bias
    )
    activated = jax.nn.elu(pre_act).astype(jnp.bfloat16)
    elu_slope = jnp.where(pre_act > 0, 1.0, jnp.exp(jnp.minimum(pre_act, 0.0)))
    dpre = (d_out.astype(jnp.float32) * elu_slope).astype(jnp.bfloat16)

    contract_cols = (((1,), (1,)), ((), ()))
    d_self_t = lax.dot_general(
        w_self_all, dpre, contract_cols, preferred_element_type=jnp.float32
    ).astype(jnp.bfloat16)
    d_neigh_t = lax.dot_general(
        w_neigh_all, dpre, contract_cols, preferred_element_type=jnp.float32
    ).astype(jnp.bfloat16)
    own_deg = lax.dynamic_slice_in_dim(deg_blocks, feat_index * per, per, 0).reshape(1, -1)
    d_scaled_t = (d_neigh_t.astype(jnp.float32) / jnp.maximum(own_deg, 1.0)).astype(jnp.bfloat16)

    contract_rows = (((0,), (0,)), ((), ()))
    part = jnp.concatenate(
        [
            lax.dot_general(own_feat, dpre, contract_rows, preferred_element_type=jnp.float32),
            lax.dot_general(own_nm, dpre, contract_rows, preferred_element_type=jnp.float32),
        ],
        axis=1,
    )
    part_got = lax.all_to_all(part.reshape(feat_parts, cols, 2 * hidden), "feat", 0, 0, tiled=True)
    grads = lax.psum(jnp.sum(part_got, axis=0), "node")
    grad_scale = 1.0 / math.sqrt(node_total)
    grad_self = grads[:, :hidden] * grad_scale
    grad_neigh = grads[:, hidden:] * grad_scale

    back = (
        jnp.stack([d_self_t, d_scaled_t], axis=0)
        .reshape(2, feat_parts, cols, per, block_size)
        .transpose(1, 3, 0, 2, 4)
    )
    (got_back,) = exchange([back], [False], feat_parts, 1)
    got_back = got_back.reshape(blocks_here, 2, cols, block_size)
    d_self_blocks = got_back[:, 0]
    d_scaled_blocks = got_back[:, 1]

    grad_all = aggregate_backward(ids_flat, nbr_count, d_scaled_blocks, tiles, all_blocks)
    grad_group = lax.psum_scatter(grad_all, "node", scatter_dimension=0, tiled=True)
    grad_group = grad_group + d_self_blocks.astype(jnp.float32)
    grad_features = grad_group.transpose(0, 2, 1).reshape(-1, cols)
    return (activated, grad_features, grad_self, grad_neigh)


def solution(mesh):
    placed = (
        P(None, "feat"),
        P("feat", None),
        P("feat", None),
        P(),
        P(("node", "feat"), None),
        P("node", None),
        P("node"),
        P("node", None, None, None),
    )
    return jax.shard_map(
        shards,
        mesh=mesh,
        in_specs=placed,
        out_specs=(P(("node", "feat"), None), P("node", "feat"), P("feat", None), P("feat", None)),
        check_vma=False,
    )
```

```python
import functools
import math

import jax
import jax.numpy as jnp
from jax import lax
from jax.experimental import pallas as pl
from jax.experimental.pallas import tpu as pltpu
from jax.sharding import PartitionSpec as P

ROWS_PER_STEP = 16


def unpack_tile(words):
    nwords, width = words.shape
    shifts = lax.broadcasted_iota(jnp.int32, (16, width), 0)
    rows = [
        jnp.bitwise_and(jnp.right_shift(jnp.broadcast_to(words[w : w + 1, :], (16, width)), shifts), 1)
        for w in range(nwords)
    ]
    return jnp.concatenate(rows, axis=0).astype(jnp.float32).astype(jnp.bfloat16)


def forward_kernel(ids_ref, cnt_ref, feat_ref, tiles_ref, nm_ref, deg_ref):
    step = pl.program_id(0)
    rows_here, slots = tiles_ref.shape[0], tiles_ref.shape[1]
    cols, width = feat_ref.shape[1], feat_ref.shape[2]

    def row(r, carry):
        b = step * rows_here + r
        cnt = cnt_ref[b]
        adjs, lhs = [], []
        for s in range(slots):
            live = jnp.where(s < cnt, 1.0, 0.0)
            adjs.append(unpack_tile(tiles_ref[r, s]))
            src = feat_ref[ids_ref[b * slots + s]].astype(jnp.float32) * live
            lhs.append(
                jnp.concatenate([src, jnp.full((cols, width), live, jnp.float32)], axis=0).astype(
                    jnp.bfloat16
                )
            )
        out = lax.dot_general(
            jnp.concatenate(lhs, axis=1),
            jnp.concatenate(adjs, axis=1),
            (((1,), (1,)), ((), ())),
            preferred_element_type=jnp.float32,
        )
        deg = out[cols : cols + 1, :]
        nm_ref[r] = (out[:cols, :] / jnp.maximum(deg, 1.0)).astype(nm_ref.dtype)
        deg_ref[r] = deg
        return carry

    lax.fori_loop(0, rows_here, row, 0)


def backward_kernel(ids_ref, cnt_ref, ds_ref, tiles_ref, g_ref):
    step = pl.program_id(0)
    rows_here, slots = tiles_ref.shape[0], tiles_ref.shape[1]
    width = tiles_ref.shape[3]

    @pl.when(step == 0)
    def _():
        g_ref[...] = jnp.zeros_like(g_ref)

    def row(r, carry):
        b = step * rows_here + r
        cnt = cnt_ref[b]
        adjcat = jnp.concatenate([unpack_tile(tiles_ref[r, s]) for s in range(slots)], axis=1)
        res = jnp.dot(ds_ref[r], adjcat, preferred_element_type=jnp.float32)
        for s in range(slots):
            live = jnp.where(s < cnt, 1.0, 0.0)
            t = ids_ref[b * slots + s]
            g_ref[t] = g_ref[t] + res[:, s * width : (s + 1) * width] * live
        return carry

    lax.fori_loop(0, rows_here, row, 0)


def aggregate_forward(ids_flat, counts, feat_t, tiles):
    blocks_here, slots, nwords, width = tiles.shape
    all_blocks, cols, _ = feat_t.shape
    rows = ROWS_PER_STEP
    return pl.pallas_call(
        forward_kernel,
        grid_spec=pltpu.PrefetchScalarGridSpec(
            num_scalar_prefetch=2,
            grid=(blocks_here // rows,),
            in_specs=[
                pl.BlockSpec((all_blocks, cols, width), lambda i, *_: (0, 0, 0)),
                pl.BlockSpec((rows, slots, nwords, width), lambda i, *_: (i, 0, 0, 0)),
            ],
            out_specs=[
                pl.BlockSpec((rows, cols, width), lambda i, *_: (i, 0, 0)),
                pl.BlockSpec((rows, 1, width), lambda i, *_: (i, 0, 0)),
            ],
        ),
        out_shape=[
            jax.ShapeDtypeStruct((blocks_here, cols, width), jnp.bfloat16),
            jax.ShapeDtypeStruct((blocks_here, 1, width), jnp.float32),
        ],
        compiler_params=pltpu.CompilerParams(dimension_semantics=("arbitrary",)),
    )(ids_flat, counts, feat_t, tiles)


def aggregate_backward(ids_flat, counts, ds_blocks, tiles, all_blocks):
    blocks_here, slots, nwords, width = tiles.shape
    cols = ds_blocks.shape[1]
    rows = ROWS_PER_STEP
    return pl.pallas_call(
        backward_kernel,
        grid_spec=pltpu.PrefetchScalarGridSpec(
            num_scalar_prefetch=2,
            grid=(blocks_here // rows,),
            in_specs=[
                pl.BlockSpec((rows, cols, width), lambda i, *_: (i, 0, 0)),
                pl.BlockSpec((rows, slots, nwords, width), lambda i, *_: (i, 0, 0, 0)),
            ],
            out_specs=pl.BlockSpec((all_blocks, cols, width), lambda i, *_: (0, 0, 0)),
        ),
        out_shape=jax.ShapeDtypeStruct((all_blocks, cols, width), jnp.float32),
        compiler_params=pltpu.CompilerParams(dimension_semantics=("arbitrary",)),
    )(ids_flat, counts, ds_blocks, tiles)


def exchange_kernel(parts, kinds, *refs):
    n_in = len(kinds)
    ins, outs = refs[:n_in], refs[n_in : 2 * n_in]
    send_sems, recv_sems = refs[2 * n_in :]
    me = lax.axis_index("feat")
    mesh_id = pl.DeviceIdType.MESH

    barrier = pltpu.get_barrier_semaphore()

    def greet(k, carry):
        peer = lax.rem(me + k, parts)
        pl.semaphore_signal(barrier, 1, device_id={"feat": peer}, device_id_type=mesh_id)
        return carry

    lax.fori_loop(1, parts, greet, 0)
    pl.semaphore_wait(barrier, parts - 1)

    def copy(i, k):
        peer = lax.rem(me + k, parts)
        src = ins[i] if kinds[i] else ins[i].at[peer]
        return pltpu.make_async_remote_copy(
            src_ref=src,
            dst_ref=outs[i].at[me],
            send_sem=send_sems.at[i, k],
            recv_sem=recv_sems.at[i, k],
            device_id={"feat": peer},
            device_id_type=mesh_id,
        )

    def start(k, carry):
        for i in range(n_in):
            copy(i, k).start()
        return carry

    lax.fori_loop(1, parts, start, 0)
    for i in range(n_in):
        outs[i][me] = ins[i][...] if kinds[i] else ins[i][me]

    def finish(k, carry):
        for i in range(n_in):
            copy(i, k).wait()
        return carry

    lax.fori_loop(1, parts, finish, 0)


def exchange(arrays, kinds, parts, cid):
    out_shapes = [
        jax.ShapeDtypeStruct(((parts,) + x.shape) if kind else x.shape, x.dtype)
        for x, kind in zip(arrays, kinds)
    ]
    vmem = pl.BlockSpec(memory_space=pltpu.VMEM)
    return pl.pallas_call(
        functools.partial(exchange_kernel, parts, tuple(kinds)),
        out_shape=out_shapes,
        in_specs=[vmem] * len(arrays),
        out_specs=[vmem] * len(arrays),
        scratch_shapes=[
            pltpu.SemaphoreType.DMA((len(arrays), parts)),
            pltpu.SemaphoreType.DMA((len(arrays), parts)),
        ],
        compiler_params=pltpu.CompilerParams(collective_id=cid, has_side_effects=True),
    )(*arrays)


def forward_exchange_kernel(
    parts, ids_ref, cnt_ref, feat_ref, tiles_ref, w_ref,
    feat_out, nm_out, w_out, deg_ref, nm_scr, send_sems, recv_sems,
):
    me = lax.axis_index("feat")
    group = lax.axis_index("node")
    blocks_here, slots = tiles_ref.shape[0], tiles_ref.shape[1]
    cols, width = feat_ref.shape[1], feat_ref.shape[2]
    per = blocks_here // parts
    mesh_id = pl.DeviceIdType.MESH

    barrier = pltpu.get_barrier_semaphore()

    def greet(k, carry):
        peer = lax.rem(me + k, parts)
        pl.semaphore_signal(barrier, 1, device_id={"feat": peer}, device_id_type=mesh_id)
        return carry

    lax.fori_loop(1, parts, greet, 0)
    pl.semaphore_wait(barrier, parts - 1)

    half = parts // 2
    par = lax.rem(me, 2)
    sibling = me + 1 - 2 * par

    def copy(i, k):
        if i == 0:
            peer = lax.rem(me + 2 * k, parts)
            src, dst = w_ref, w_out.at[par, me // 2]
        elif i == 1:
            peer = lax.rem(me + k, parts)
            src = feat_ref.at[pl.ds(group * blocks_here + peer * per, per)]
            dst = feat_out.at[me]
        else:
            peer = lax.rem(me + k, parts)
            src, dst = nm_scr.at[pl.ds(peer * per, per)], nm_out.at[me]
        return pltpu.make_async_remote_copy(
            src_ref=src,
            dst_ref=dst,
            send_sem=send_sems.at[i, k],
            recv_sem=recv_sems.at[i, k],
            device_id={"feat": peer},
            device_id_type=mesh_id,
        )

    def start_weights(k, carry):
        copy(0, k).start()
        return carry

    def start_feat(k, carry):
        copy(1, k).start()
        return carry

    lax.fori_loop(1, half, start_weights, 0)
    lax.fori_loop(1, parts, start_feat, 0)
    own_w = pltpu.make_async_copy(w_ref, w_out.at[par, me // 2], send_sems.at[3, 0])
    own_w.start()
    feat_out[me] = feat_ref[pl.ds(group * blocks_here + me * per, per)]

    def row(b, carry):
        cnt = cnt_ref[b]
        adjs, lhs = [], []
        for s in range(slots):
            live = jnp.where(s < cnt, 1.0, 0.0)
            adjs.append(unpack_tile(tiles_ref[b, s]))
            src = feat_ref[ids_ref[b * slots + s]].astype(jnp.float32) * live
            lhs.append(
                jnp.concatenate([src, jnp.full((cols, width), live, jnp.float32)], axis=0).astype(
                    jnp.bfloat16
                )
            )
        out = lax.dot_general(
            jnp.concatenate(lhs, axis=1),
            jnp.concatenate(adjs, axis=1),
            (((1,), (1,)), ((), ())),
            preferred_element_type=jnp.float32,
        )
        deg = out[cols : cols + 1, :]
        nm_scr[b] = (out[:cols, :] / jnp.maximum(deg, 1.0)).astype(nm_scr.dtype)
        deg_ref[b] = deg
        return carry

    lax.fori_loop(0, blocks_here, row, 0)

    def finish_weights(k, carry):
        copy(0, k).wait()
        return carry

    lax.fori_loop(1, half, finish_weights, 0)
    own_w.wait()
    to_sibling = pltpu.make_async_remote_copy(
        src_ref=w_out.at[par],
        dst_ref=w_out.at[par],
        send_sem=send_sems.at[3, 1],
        recv_sem=recv_sems.at[3, 1],
        device_id={"feat": sibling},
        device_id_type=mesh_id,
    )
    to_sibling.start()

    def start_result(k, carry):
        copy(2, k).start()
        return carry

    lax.fori_loop(1, parts, start_result, 0)
    nm_out[me] = nm_scr[pl.ds(me * per, per)]

    def finish(k, carry):
        copy(1, k).wait()
        copy(2, k).wait()
        return carry

    lax.fori_loop(1, parts, finish, 0)
    to_sibling.wait()


def forward_exchange(ids_flat, counts, feat_t, tiles, w_both, parts):
    blocks_here, slots, nwords, width = tiles.shape
    all_blocks, cols, _ = feat_t.shape
    per = blocks_here // parts
    vmem = pl.BlockSpec(memory_space=pltpu.VMEM)
    smem = pl.BlockSpec(memory_space=pltpu.SMEM)
    return pl.pallas_call(
        functools.partial(forward_exchange_kernel, parts),
        out_shape=[
            jax.ShapeDtypeStruct((parts, per, cols, width), jnp.bfloat16),
            jax.ShapeDtypeStruct((parts, per, cols, width), jnp.bfloat16),
            jax.ShapeDtypeStruct((2, parts // 2) + w_both.shape, w_both.dtype),
            jax.ShapeDtypeStruct((blocks_here, 1, width), jnp.float32),
        ],
        in_specs=[smem, smem, vmem, vmem, vmem],
        out_specs=[vmem] * 4,
        scratch_shapes=[
            pltpu.VMEM((blocks_here, cols, width), jnp.bfloat16),
            pltpu.SemaphoreType.DMA((4, parts)),
            pltpu.SemaphoreType.DMA((4, parts)),
        ],
        compiler_params=pltpu.CompilerParams(collective_id=0, has_side_effects=True),
    )(ids_flat, counts, feat_t, tiles, w_both)


def shards(features, w_self, w_neigh, bias, d_out, nbr_ids, nbr_count, tiles):
    node_total, cols = features.shape
    hidden = w_self.shape[1]
    block_size = tiles.shape[3]
    blocks_here = nbr_ids.shape[0]
    all_blocks = node_total // block_size
    node_group = lax.axis_index("node")
    feat_index = lax.axis_index("feat")
    feat_parts = lax.axis_size("feat")
    per = blocks_here // feat_parts
    own_nodes = per * block_size

    feat_t = features.reshape(all_blocks, block_size, cols).transpose(0, 2, 1)
    ids_flat = nbr_ids.reshape(-1)

    w_both = jnp.concatenate([w_self, w_neigh], axis=1)
    feat_got, nm_got, w_all, deg_blocks = forward_exchange(
        ids_flat, nbr_count, feat_t, tiles, w_both, feat_parts
    )
    w_all = w_all.transpose(1, 0, 2, 3).reshape(feat_parts * cols, 2 * hidden)
    w_self_all = w_all[:, :hidden]
    w_neigh_all = w_all[:, hidden:]
    own_feat = feat_got.transpose(1, 3, 0, 2).reshape(own_nodes, feat_parts * cols)
    own_nm = nm_got.transpose(1, 3, 0, 2).reshape(own_nodes, feat_parts * cols)

    pre_act = (
        jnp.dot(own_feat, w_self_all, preferred_element_type=jnp.float32)
        + jnp.dot(own_nm, w_neigh_all, preferred_element_type=jnp.float32)
        + bias
    )
    activated = jax.nn.elu(pre_act).astype(jnp.bfloat16)
    elu_slope = jnp.where(pre_act > 0, 1.0, jnp.exp(jnp.minimum(pre_act, 0.0)))
    dpre = (d_out.astype(jnp.float32) * elu_slope).astype(jnp.bfloat16)

    contract_cols = (((1,), (1,)), ((), ()))
    d_self_t = lax.dot_general(
        w_self_all, dpre, contract_cols, preferred_element_type=jnp.float32
    ).astype(jnp.bfloat16)
    d_neigh_t = lax.dot_general(
        w_neigh_all, dpre, contract_cols, preferred_element_type=jnp.float32
    ).astype(jnp.bfloat16)
    own_deg = lax.dynamic_slice_in_dim(deg_blocks, feat_index * per, per, 0).reshape(1, -1)
    d_scaled_t = (d_neigh_t.astype(jnp.float32) / jnp.maximum(own_deg, 1.0)).astype(jnp.bfloat16)

    contract_rows = (((0,), (0,)), ((), ()))
    part = jnp.concatenate(
        [
            lax.dot_general(own_feat, dpre, contract_rows, preferred_element_type=jnp.float32),
            lax.dot_general(own_nm, dpre, contract_rows, preferred_element_type=jnp.float32),
        ],
        axis=1,
    )
    part_got = lax.all_to_all(part.reshape(feat_parts, cols, 2 * hidden), "feat", 0, 0, tiled=True)
    grads = lax.psum(jnp.sum(part_got, axis=0), "node")
    grad_scale = 1.0 / math.sqrt(node_total)
    grad_self = grads[:, :hidden] * grad_scale
    grad_neigh = grads[:, hidden:] * grad_scale

    back = (
        jnp.stack([d_self_t, d_scaled_t], axis=0)
        .reshape(2, feat_parts, cols, per, block_size)
        .transpose(1, 3, 0, 2, 4)
    )
    got_back = lax.all_to_all(back, "feat", 0, 0, tiled=True).reshape(blocks_here, 2, cols, block_size)
    d_self_blocks = got_back[:, 0]
    d_scaled_blocks = got_back[:, 1]

    grad_all = aggregate_backward(ids_flat, nbr_count, d_scaled_blocks, tiles, all_blocks)
    grad_group = lax.psum_scatter(grad_all, "node", scatter_dimension=0, tiled=True)
    grad_group = grad_group + d_self_blocks.astype(jnp.float32)
    grad_features = grad_group.transpose(0, 2, 1).reshape(-1, cols)
    return (activated, grad_features, grad_self, grad_neigh)


def solution(mesh):
    placed = (
        P(None, "feat"),
        P("feat", None),
        P("feat", None),
        P(),
        P(("node", "feat"), None),
        P("node", None),
        P("node"),
        P("node", None, None, None),
    )
    return jax.shard_map(
        shards,
        mesh=mesh,
        in_specs=placed,
        out_specs=(P(("node", "feat"), None), P("node", "feat"), P("feat", None), P("feat", None)),
        check_vma=False,
    )
```

```python
import functools
import math

import jax
import jax.numpy as jnp
from jax import lax
from jax.experimental import pallas as pl
from jax.experimental.pallas import tpu as pltpu
from jax.sharding import PartitionSpec as P

ROWS_PER_STEP = 16


def unpack_tile(words):
    nwords, width = words.shape
    shifts = lax.broadcasted_iota(jnp.int32, (16, width), 0)
    rows = [
        jnp.bitwise_and(jnp.right_shift(jnp.broadcast_to(words[w : w + 1, :], (16, width)), shifts), 1)
        for w in range(nwords)
    ]
    return jnp.concatenate(rows, axis=0).astype(jnp.float32).astype(jnp.bfloat16)


def forward_kernel(ids_ref, cnt_ref, feat_ref, tiles_ref, nm_ref, deg_ref):
    step = pl.program_id(0)
    rows_here, slots = tiles_ref.shape[0], tiles_ref.shape[1]
    cols, width = feat_ref.shape[1], feat_ref.shape[2]

    def row(r, carry):
        b = step * rows_here + r
        cnt = cnt_ref[b]
        adjs, lhs = [], []
        for s in range(slots):
            live = jnp.where(s < cnt, 1.0, 0.0)
            adjs.append(unpack_tile(tiles_ref[r, s]))
            src = feat_ref[ids_ref[b * slots + s]].astype(jnp.float32) * live
            lhs.append(
                jnp.concatenate([src, jnp.full((cols, width), live, jnp.float32)], axis=0).astype(
                    jnp.bfloat16
                )
            )
        out = lax.dot_general(
            jnp.concatenate(lhs, axis=1),
            jnp.concatenate(adjs, axis=1),
            (((1,), (1,)), ((), ())),
            preferred_element_type=jnp.float32,
        )
        deg = out[cols : cols + 1, :]
        nm_ref[r] = (out[:cols, :] / jnp.maximum(deg, 1.0)).astype(nm_ref.dtype)
        deg_ref[r] = deg
        return carry

    lax.fori_loop(0, rows_here, row, 0)


def backward_kernel(ids_ref, cnt_ref, ds_ref, tiles_ref, g_ref):
    step = pl.program_id(0)
    rows_here, slots = tiles_ref.shape[0], tiles_ref.shape[1]
    width = tiles_ref.shape[3]

    @pl.when(step == 0)
    def _():
        g_ref[...] = jnp.zeros_like(g_ref)

    def row(r, carry):
        b = step * rows_here + r
        cnt = cnt_ref[b]
        adjcat = jnp.concatenate([unpack_tile(tiles_ref[r, s]) for s in range(slots)], axis=1)
        res = jnp.dot(ds_ref[r], adjcat, preferred_element_type=jnp.float32)
        for s in range(slots):
            live = jnp.where(s < cnt, 1.0, 0.0)
            t = ids_ref[b * slots + s]
            g_ref[t] = g_ref[t] + res[:, s * width : (s + 1) * width] * live
        return carry

    lax.fori_loop(0, rows_here, row, 0)


def aggregate_forward(ids_flat, counts, feat_t, tiles):
    blocks_here, slots, nwords, width = tiles.shape
    all_blocks, cols, _ = feat_t.shape
    rows = ROWS_PER_STEP
    return pl.pallas_call(
        forward_kernel,
        grid_spec=pltpu.PrefetchScalarGridSpec(
            num_scalar_prefetch=2,
            grid=(blocks_here // rows,),
            in_specs=[
                pl.BlockSpec((all_blocks, cols, width), lambda i, *_: (0, 0, 0)),
                pl.BlockSpec((rows, slots, nwords, width), lambda i, *_: (i, 0, 0, 0)),
            ],
            out_specs=[
                pl.BlockSpec((rows, cols, width), lambda i, *_: (i, 0, 0)),
                pl.BlockSpec((rows, 1, width), lambda i, *_: (i, 0, 0)),
            ],
        ),
        out_shape=[
            jax.ShapeDtypeStruct((blocks_here, cols, width), jnp.bfloat16),
            jax.ShapeDtypeStruct((blocks_here, 1, width), jnp.float32),
        ],
        compiler_params=pltpu.CompilerParams(dimension_semantics=("arbitrary",)),
    )(ids_flat, counts, feat_t, tiles)


def aggregate_backward(ids_flat, counts, ds_blocks, tiles, all_blocks):
    blocks_here, slots, nwords, width = tiles.shape
    cols = ds_blocks.shape[1]
    rows = ROWS_PER_STEP
    return pl.pallas_call(
        backward_kernel,
        grid_spec=pltpu.PrefetchScalarGridSpec(
            num_scalar_prefetch=2,
            grid=(blocks_here // rows,),
            in_specs=[
                pl.BlockSpec((rows, cols, width), lambda i, *_: (i, 0, 0)),
                pl.BlockSpec((rows, slots, nwords, width), lambda i, *_: (i, 0, 0, 0)),
            ],
            out_specs=pl.BlockSpec((all_blocks, cols, width), lambda i, *_: (0, 0, 0)),
        ),
        out_shape=jax.ShapeDtypeStruct((all_blocks, cols, width), jnp.float32),
        compiler_params=pltpu.CompilerParams(dimension_semantics=("arbitrary",)),
    )(ids_flat, counts, ds_blocks, tiles)


def exchange_kernel(parts, kinds, *refs):
    n_in = len(kinds)
    ins, outs = refs[:n_in], refs[n_in : 2 * n_in]
    send_sems, recv_sems = refs[2 * n_in :]
    me = lax.axis_index("feat")
    mesh_id = pl.DeviceIdType.MESH

    barrier = pltpu.get_barrier_semaphore()

    def greet(k, carry):
        peer = lax.rem(me + k, parts)
        pl.semaphore_signal(barrier, 1, device_id={"feat": peer}, device_id_type=mesh_id)
        return carry

    lax.fori_loop(1, parts, greet, 0)
    pl.semaphore_wait(barrier, parts - 1)

    def copy(i, k):
        peer = lax.rem(me + k, parts)
        src = ins[i] if kinds[i] else ins[i].at[peer]
        return pltpu.make_async_remote_copy(
            src_ref=src,
            dst_ref=outs[i].at[me],
            send_sem=send_sems.at[i, k],
            recv_sem=recv_sems.at[i, k],
            device_id={"feat": peer},
            device_id_type=mesh_id,
        )

    def start(k, carry):
        for i in range(n_in):
            copy(i, k).start()
        return carry

    lax.fori_loop(1, parts, start, 0)
    for i in range(n_in):
        outs[i][me] = ins[i][...] if kinds[i] else ins[i][me]

    def finish(k, carry):
        for i in range(n_in):
            copy(i, k).wait()
        return carry

    lax.fori_loop(1, parts, finish, 0)


def exchange(arrays, kinds, parts, cid):
    out_shapes = [
        jax.ShapeDtypeStruct(((parts,) + x.shape) if kind else x.shape, x.dtype)
        for x, kind in zip(arrays, kinds)
    ]
    vmem = pl.BlockSpec(memory_space=pltpu.VMEM)
    return pl.pallas_call(
        functools.partial(exchange_kernel, parts, tuple(kinds)),
        out_shape=out_shapes,
        in_specs=[vmem] * len(arrays),
        out_specs=[vmem] * len(arrays),
        scratch_shapes=[
            pltpu.SemaphoreType.DMA((len(arrays), parts)),
            pltpu.SemaphoreType.DMA((len(arrays), parts)),
        ],
        compiler_params=pltpu.CompilerParams(collective_id=cid, has_side_effects=True),
    )(*arrays)


def forward_exchange_kernel(
    parts, ids_ref, cnt_ref, feat_ref, tiles_ref, w_ref,
    feat_out, nm_out, w_out, deg_ref, nm_scr, send_sems, recv_sems,
):
    me = lax.axis_index("feat")
    group = lax.axis_index("node")
    blocks_here, slots = tiles_ref.shape[0], tiles_ref.shape[1]
    cols, width = feat_ref.shape[1], feat_ref.shape[2]
    per = blocks_here // parts
    mesh_id = pl.DeviceIdType.MESH

    barrier = pltpu.get_barrier_semaphore()

    def greet(k, carry):
        peer = lax.rem(me + k, parts)
        pl.semaphore_signal(barrier, 1, device_id={"feat": peer}, device_id_type=mesh_id)
        return carry

    lax.fori_loop(1, parts, greet, 0)
    pl.semaphore_wait(barrier, parts - 1)

    half = parts // 2
    par = lax.rem(me, 2)
    sibling = me + 1 - 2 * par

    def copy(i, k):
        if i == 0:
            peer = lax.rem(me + 2 * k, parts)
            src, dst = w_ref, w_out.at[par, me // 2]
        elif i == 1:
            peer = lax.rem(me + k, parts)
            src = feat_ref.at[pl.ds(group * blocks_here + peer * per, per)]
            dst = feat_out.at[me]
        else:
            peer = lax.rem(me + k, parts)
            src, dst = nm_scr.at[pl.ds(peer * per, per)], nm_out.at[me]
        return pltpu.make_async_remote_copy(
            src_ref=src,
            dst_ref=dst,
            send_sem=send_sems.at[i, k],
            recv_sem=recv_sems.at[i, k],
            device_id={"feat": peer},
            device_id_type=mesh_id,
        )

    def start_weights(k, carry):
        copy(0, k).start()
        return carry

    def start_feat(k, carry):
        copy(1, k).start()
        return carry

    lax.fori_loop(1, half, start_weights, 0)
    lax.fori_loop(1, parts, start_feat, 0)
    own_w = pltpu.make_async_copy(w_ref, w_out.at[par, me // 2], send_sems.at[3, 0])
    own_w.start()
    feat_out[me] = feat_ref[pl.ds(group * blocks_here + me * per, per)]

    def row(b, carry):
        cnt = cnt_ref[b]
        adjs, lhs = [], []
        for s in range(slots):
            live = jnp.where(s < cnt, 1.0, 0.0)
            adjs.append(unpack_tile(tiles_ref[b, s]))
            src = feat_ref[ids_ref[b * slots + s]].astype(jnp.float32) * live
            lhs.append(
                jnp.concatenate([src, jnp.full((cols, width), live, jnp.float32)], axis=0).astype(
                    jnp.bfloat16
                )
            )
        out = lax.dot_general(
            jnp.concatenate(lhs, axis=1),
            jnp.concatenate(adjs, axis=1),
            (((1,), (1,)), ((), ())),
            preferred_element_type=jnp.float32,
        )
        deg = out[cols : cols + 1, :]
        nm_scr[b] = (out[:cols, :] / jnp.maximum(deg, 1.0)).astype(nm_scr.dtype)
        deg_ref[b] = deg
        k = lax.rem(b // per - me + parts, parts)

        @pl.when(jnp.logical_and(k != 0, lax.rem(b + 1, per) == 0))
        def _():
            copy(2, k).start()

        return carry

    lax.fori_loop(0, blocks_here, row, 0)

    def finish_weights(k, carry):
        copy(0, k).wait()
        return carry

    lax.fori_loop(1, half, finish_weights, 0)
    own_w.wait()
    to_sibling = pltpu.make_async_remote_copy(
        src_ref=w_out.at[par],
        dst_ref=w_out.at[par],
        send_sem=send_sems.at[3, 1],
        recv_sem=recv_sems.at[3, 1],
        device_id={"feat": sibling},
        device_id_type=mesh_id,
    )
    to_sibling.start()

    nm_out[me] = nm_scr[pl.ds(me * per, per)]

    def finish(k, carry):
        copy(1, k).wait()
        copy(2, k).wait()
        return carry

    lax.fori_loop(1, parts, finish, 0)
    to_sibling.wait()


def forward_exchange(ids_flat, counts, feat_t, tiles, w_both, parts):
    blocks_here, slots, nwords, width = tiles.shape
    all_blocks, cols, _ = feat_t.shape
    per = blocks_here // parts
    vmem = pl.BlockSpec(memory_space=pltpu.VMEM)
    smem = pl.BlockSpec(memory_space=pltpu.SMEM)
    return pl.pallas_call(
        functools.partial(forward_exchange_kernel, parts),
        out_shape=[
            jax.ShapeDtypeStruct((parts, per, cols, width), jnp.bfloat16),
            jax.ShapeDtypeStruct((parts, per, cols, width), jnp.bfloat16),
            jax.ShapeDtypeStruct((2, parts // 2) + w_both.shape, w_both.dtype),
            jax.ShapeDtypeStruct((blocks_here, 1, width), jnp.float32),
        ],
        in_specs=[smem, smem, vmem, vmem, vmem],
        out_specs=[vmem] * 4,
        scratch_shapes=[
            pltpu.VMEM((blocks_here, cols, width), jnp.bfloat16),
            pltpu.SemaphoreType.DMA((4, parts)),
            pltpu.SemaphoreType.DMA((4, parts)),
        ],
        compiler_params=pltpu.CompilerParams(collective_id=0, has_side_effects=True),
    )(ids_flat, counts, feat_t, tiles, w_both)


def shards(features, w_self, w_neigh, bias, d_out, nbr_ids, nbr_count, tiles):
    node_total, cols = features.shape
    hidden = w_self.shape[1]
    block_size = tiles.shape[3]
    blocks_here = nbr_ids.shape[0]
    all_blocks = node_total // block_size
    node_group = lax.axis_index("node")
    feat_index = lax.axis_index("feat")
    feat_parts = lax.axis_size("feat")
    per = blocks_here // feat_parts
    own_nodes = per * block_size

    feat_t = features.reshape(all_blocks, block_size, cols).transpose(0, 2, 1)
    ids_flat = nbr_ids.reshape(-1)

    w_both = jnp.concatenate([w_self, w_neigh], axis=1)
    feat_got, nm_got, w_all, deg_blocks = forward_exchange(
        ids_flat, nbr_count, feat_t, tiles, w_both, feat_parts
    )
    w_all = w_all.transpose(1, 0, 2, 3).reshape(feat_parts * cols, 2 * hidden)
    w_self_all = w_all[:, :hidden]
    w_neigh_all = w_all[:, hidden:]
    own_feat = feat_got.transpose(1, 3, 0, 2).reshape(own_nodes, feat_parts * cols)
    own_nm = nm_got.transpose(1, 3, 0, 2).reshape(own_nodes, feat_parts * cols)

    pre_act = (
        jnp.dot(own_feat, w_self_all, preferred_element_type=jnp.float32)
        + jnp.dot(own_nm, w_neigh_all, preferred_element_type=jnp.float32)
        + bias
    )
    activated = jax.nn.elu(pre_act).astype(jnp.bfloat16)
    elu_slope = jnp.where(pre_act > 0, 1.0, jnp.exp(jnp.minimum(pre_act, 0.0)))
    dpre = (d_out.astype(jnp.float32) * elu_slope).astype(jnp.bfloat16)

    contract_cols = (((1,), (1,)), ((), ()))
    d_self_t = lax.dot_general(
        w_self_all, dpre, contract_cols, preferred_element_type=jnp.float32
    ).astype(jnp.bfloat16)
    d_neigh_t = lax.dot_general(
        w_neigh_all, dpre, contract_cols, preferred_element_type=jnp.float32
    ).astype(jnp.bfloat16)
    own_deg = lax.dynamic_slice_in_dim(deg_blocks, feat_index * per, per, 0).reshape(1, -1)
    d_scaled_t = (d_neigh_t.astype(jnp.float32) / jnp.maximum(own_deg, 1.0)).astype(jnp.bfloat16)

    contract_rows = (((0,), (0,)), ((), ()))
    part = jnp.concatenate(
        [
            lax.dot_general(own_feat, dpre, contract_rows, preferred_element_type=jnp.float32),
            lax.dot_general(own_nm, dpre, contract_rows, preferred_element_type=jnp.float32),
        ],
        axis=1,
    )
    part_got = lax.all_to_all(part.reshape(feat_parts, cols, 2 * hidden), "feat", 0, 0, tiled=True)
    grads = lax.psum(jnp.sum(part_got, axis=0), "node")
    grad_scale = 1.0 / math.sqrt(node_total)
    grad_self = grads[:, :hidden] * grad_scale
    grad_neigh = grads[:, hidden:] * grad_scale

    back = (
        jnp.stack([d_self_t, d_scaled_t], axis=0)
        .reshape(2, feat_parts, cols, per, block_size)
        .transpose(1, 3, 0, 2, 4)
    )
    got_back = lax.all_to_all(back, "feat", 0, 0, tiled=True).reshape(blocks_here, 2, cols, block_size)
    d_self_blocks = got_back[:, 0]
    d_scaled_blocks = got_back[:, 1]

    grad_all = aggregate_backward(ids_flat, nbr_count, d_scaled_blocks, tiles, all_blocks)
    grad_group = lax.psum_scatter(grad_all, "node", scatter_dimension=0, tiled=True)
    grad_group = grad_group + d_self_blocks.astype(jnp.float32)
    grad_features = grad_group.transpose(0, 2, 1).reshape(-1, cols)
    return (activated, grad_features, grad_self, grad_neigh)


def solution(mesh):
    placed = (
        P(None, "feat"),
        P("feat", None),
        P("feat", None),
        P(),
        P(("node", "feat"), None),
        P("node", None),
        P("node"),
        P("node", None, None, None),
    )
    return jax.shard_map(
        shards,
        mesh=mesh,
        in_specs=placed,
        out_specs=(P(("node", "feat"), None), P("node", "feat"), P("feat", None), P("feat", None)),
        check_vma=False,
    )
```

```python
import functools
import math

import jax
import jax.numpy as jnp
from jax import lax
from jax.experimental import pallas as pl
from jax.experimental.pallas import tpu as pltpu
from jax.sharding import PartitionSpec as P

ROWS_PER_STEP = 16


def unpack_tile(words):
    nwords, width = words.shape
    shifts = lax.broadcasted_iota(jnp.int32, (16, width), 0)
    rows = [
        jnp.bitwise_and(jnp.right_shift(jnp.broadcast_to(words[w : w + 1, :], (16, width)), shifts), 1)
        for w in range(nwords)
    ]
    return jnp.concatenate(rows, axis=0).astype(jnp.float32).astype(jnp.bfloat16)


def forward_kernel(ids_ref, cnt_ref, feat_ref, tiles_ref, nm_ref, deg_ref):
    step = pl.program_id(0)
    rows_here, slots = tiles_ref.shape[0], tiles_ref.shape[1]
    cols, width = feat_ref.shape[1], feat_ref.shape[2]

    def row(r, carry):
        b = step * rows_here + r
        cnt = cnt_ref[b]
        adjs, lhs = [], []
        for s in range(slots):
            live = jnp.where(s < cnt, 1.0, 0.0)
            adjs.append(unpack_tile(tiles_ref[r, s]))
            src = feat_ref[ids_ref[b * slots + s]].astype(jnp.float32) * live
            lhs.append(
                jnp.concatenate([src, jnp.full((cols, width), live, jnp.float32)], axis=0).astype(
                    jnp.bfloat16
                )
            )
        out = lax.dot_general(
            jnp.concatenate(lhs, axis=1),
            jnp.concatenate(adjs, axis=1),
            (((1,), (1,)), ((), ())),
            preferred_element_type=jnp.float32,
        )
        deg = out[cols : cols + 1, :]
        nm_ref[r] = (out[:cols, :] / jnp.maximum(deg, 1.0)).astype(nm_ref.dtype)
        deg_ref[r] = deg
        return carry

    lax.fori_loop(0, rows_here, row, 0)


def backward_kernel(ids_ref, cnt_ref, ds_ref, tiles_ref, g_ref):
    step = pl.program_id(0)
    rows_here, slots = tiles_ref.shape[0], tiles_ref.shape[1]
    width = tiles_ref.shape[3]

    @pl.when(step == 0)
    def _():
        g_ref[...] = jnp.zeros_like(g_ref)

    def row(r, carry):
        b = step * rows_here + r
        cnt = cnt_ref[b]
        adjcat = jnp.concatenate([unpack_tile(tiles_ref[r, s]) for s in range(slots)], axis=1)
        res = jnp.dot(ds_ref[r], adjcat, preferred_element_type=jnp.float32)
        for s in range(slots):
            live = jnp.where(s < cnt, 1.0, 0.0)
            t = ids_ref[b * slots + s]
            g_ref[t] = g_ref[t] + res[:, s * width : (s + 1) * width] * live
        return carry

    lax.fori_loop(0, rows_here, row, 0)


def aggregate_forward(ids_flat, counts, feat_t, tiles):
    blocks_here, slots, nwords, width = tiles.shape
    all_blocks, cols, _ = feat_t.shape
    rows = ROWS_PER_STEP
    return pl.pallas_call(
        forward_kernel,
        grid_spec=pltpu.PrefetchScalarGridSpec(
            num_scalar_prefetch=2,
            grid=(blocks_here // rows,),
            in_specs=[
                pl.BlockSpec((all_blocks, cols, width), lambda i, *_: (0, 0, 0)),
                pl.BlockSpec((rows, slots, nwords, width), lambda i, *_: (i, 0, 0, 0)),
            ],
            out_specs=[
                pl.BlockSpec((rows, cols, width), lambda i, *_: (i, 0, 0)),
                pl.BlockSpec((rows, 1, width), lambda i, *_: (i, 0, 0)),
            ],
        ),
        out_shape=[
            jax.ShapeDtypeStruct((blocks_here, cols, width), jnp.bfloat16),
            jax.ShapeDtypeStruct((blocks_here, 1, width), jnp.float32),
        ],
        compiler_params=pltpu.CompilerParams(dimension_semantics=("arbitrary",)),
    )(ids_flat, counts, feat_t, tiles)


def aggregate_backward(ids_flat, counts, ds_blocks, tiles, all_blocks):
    blocks_here, slots, nwords, width = tiles.shape
    cols = ds_blocks.shape[1]
    rows = ROWS_PER_STEP
    return pl.pallas_call(
        backward_kernel,
        grid_spec=pltpu.PrefetchScalarGridSpec(
            num_scalar_prefetch=2,
            grid=(blocks_here // rows,),
            in_specs=[
                pl.BlockSpec((rows, cols, width), lambda i, *_: (i, 0, 0)),
                pl.BlockSpec((rows, slots, nwords, width), lambda i, *_: (i, 0, 0, 0)),
            ],
            out_specs=pl.BlockSpec((all_blocks, cols, width), lambda i, *_: (0, 0, 0)),
        ),
        out_shape=jax.ShapeDtypeStruct((all_blocks, cols, width), jnp.float32),
        compiler_params=pltpu.CompilerParams(dimension_semantics=("arbitrary",)),
    )(ids_flat, counts, ds_blocks, tiles)


def exchange_kernel(parts, kinds, *refs):
    n_in = len(kinds)
    ins, outs = refs[:n_in], refs[n_in : 2 * n_in]
    send_sems, recv_sems = refs[2 * n_in :]
    me = lax.axis_index("feat")
    mesh_id = pl.DeviceIdType.MESH

    barrier = pltpu.get_barrier_semaphore()

    def greet(k, carry):
        peer = lax.rem(me + k, parts)
        pl.semaphore_signal(barrier, 1, device_id={"feat": peer}, device_id_type=mesh_id)
        return carry

    lax.fori_loop(1, parts, greet, 0)
    pl.semaphore_wait(barrier, parts - 1)

    def copy(i, k):
        peer = lax.rem(me + k, parts)
        src = ins[i] if kinds[i] else ins[i].at[peer]
        return pltpu.make_async_remote_copy(
            src_ref=src,
            dst_ref=outs[i].at[me],
            send_sem=send_sems.at[i, k],
            recv_sem=recv_sems.at[i, k],
            device_id={"feat": peer},
            device_id_type=mesh_id,
        )

    def start(k, carry):
        for i in range(n_in):
            copy(i, k).start()
        return carry

    lax.fori_loop(1, parts, start, 0)
    for i in range(n_in):
        outs[i][me] = ins[i][...] if kinds[i] else ins[i][me]

    def finish(k, carry):
        for i in range(n_in):
            copy(i, k).wait()
        return carry

    lax.fori_loop(1, parts, finish, 0)


def exchange(arrays, kinds, parts, cid):
    out_shapes = [
        jax.ShapeDtypeStruct(((parts,) + x.shape) if kind else x.shape, x.dtype)
        for x, kind in zip(arrays, kinds)
    ]
    vmem = pl.BlockSpec(memory_space=pltpu.VMEM)
    return pl.pallas_call(
        functools.partial(exchange_kernel, parts, tuple(kinds)),
        out_shape=out_shapes,
        in_specs=[vmem] * len(arrays),
        out_specs=[vmem] * len(arrays),
        scratch_shapes=[
            pltpu.SemaphoreType.DMA((len(arrays), parts)),
            pltpu.SemaphoreType.DMA((len(arrays), parts)),
        ],
        compiler_params=pltpu.CompilerParams(collective_id=cid, has_side_effects=True),
    )(*arrays)


def forward_exchange_kernel(
    parts, ids_ref, cnt_ref, feat_ref, tiles_ref, w_ref,
    feat_out, nm_out, w_out, deg_ref, nm_scr, send_sems, recv_sems,
):
    me = lax.axis_index("feat")
    group = lax.axis_index("node")
    blocks_here, slots = tiles_ref.shape[0], tiles_ref.shape[1]
    cols, width = feat_ref.shape[1], feat_ref.shape[2]
    per = blocks_here // parts
    mesh_id = pl.DeviceIdType.MESH

    barrier = pltpu.get_barrier_semaphore()

    def greet(k, carry):
        peer = lax.rem(me + k, parts)
        pl.semaphore_signal(barrier, 1, device_id={"feat": peer}, device_id_type=mesh_id)
        return carry

    lax.fori_loop(1, parts, greet, 0)
    pl.semaphore_wait(barrier, parts - 1)

    half = parts // 2
    par = lax.rem(me, 2)
    sibling = me + 1 - 2 * par

    def copy(i, k):
        if i == 0:
            peer = lax.rem(me + 2 * k, parts)
            src, dst = w_ref, w_out.at[par, me // 2]
        elif i == 1:
            peer = lax.rem(me + k, parts)
            src = feat_ref.at[pl.ds(group * blocks_here + peer * per, per)]
            dst = feat_out.at[me]
        else:
            peer = lax.rem(me + k, parts)
            src, dst = nm_scr.at[pl.ds(peer * per, per)], nm_out.at[me]
        return pltpu.make_async_remote_copy(
            src_ref=src,
            dst_ref=dst,
            send_sem=send_sems.at[i, k],
            recv_sem=recv_sems.at[i, k],
            device_id={"feat": peer},
            device_id_type=mesh_id,
        )

    def start_weights(k, carry):
        copy(0, k).start()
        return carry

    def start_feat(k, carry):
        copy(1, k).start()
        return carry

    lax.fori_loop(1, half, start_weights, 0)
    lax.fori_loop(1, parts, start_feat, 0)
    own_w = pltpu.make_async_copy(w_ref, w_out.at[par, me // 2], send_sems.at[3, 0])
    own_w.start()
    feat_out[me] = feat_ref[pl.ds(group * blocks_here + me * per, per)]

    def row(b, carry):
        cnt = cnt_ref[b]
        adjs, lhs = [], []
        for s in range(slots):
            live = jnp.where(s < cnt, 1.0, 0.0)
            adjs.append(unpack_tile(tiles_ref[b, s]))
            src = feat_ref[ids_ref[b * slots + s]].astype(jnp.float32) * live
            lhs.append(
                jnp.concatenate([src, jnp.full((cols, width), live, jnp.float32)], axis=0).astype(
                    jnp.bfloat16
                )
            )
        out = lax.dot_general(
            jnp.concatenate(lhs, axis=1),
            jnp.concatenate(adjs, axis=1),
            (((1,), (1,)), ((), ())),
            preferred_element_type=jnp.float32,
        )
        deg = out[cols : cols + 1, :]
        nm_scr[b] = (out[:cols, :] / jnp.maximum(deg, 1.0)).astype(nm_scr.dtype)
        deg_ref[b] = deg
        k = lax.rem(b // per - me + parts, parts)

        @pl.when(jnp.logical_and(k != 0, lax.rem(b + 1, per) == 0))
        def _():
            copy(2, k).start()

        return carry

    lax.fori_loop(0, blocks_here, row, 0)

    def finish_weights(k, carry):
        copy(0, k).wait()
        return carry

    lax.fori_loop(1, half, finish_weights, 0)
    own_w.wait()
    to_sibling = pltpu.make_async_remote_copy(
        src_ref=w_out.at[par],
        dst_ref=w_out.at[par],
        send_sem=send_sems.at[3, 1],
        recv_sem=recv_sems.at[3, 1],
        device_id={"feat": sibling},
        device_id_type=mesh_id,
    )
    to_sibling.start()

    nm_out[me] = nm_scr[pl.ds(me * per, per)]

    def finish(k, carry):
        copy(1, k).wait()
        copy(2, k).wait()
        return carry

    lax.fori_loop(1, parts, finish, 0)
    to_sibling.wait()


def forward_exchange(ids_flat, counts, feat_t, tiles, w_both, parts):
    blocks_here, slots, nwords, width = tiles.shape
    all_blocks, cols, _ = feat_t.shape
    per = blocks_here // parts
    vmem = pl.BlockSpec(memory_space=pltpu.VMEM)
    smem = pl.BlockSpec(memory_space=pltpu.SMEM)
    return pl.pallas_call(
        functools.partial(forward_exchange_kernel, parts),
        out_shape=[
            jax.ShapeDtypeStruct((parts, per, cols, width), jnp.bfloat16),
            jax.ShapeDtypeStruct((parts, per, cols, width), jnp.bfloat16),
            jax.ShapeDtypeStruct((2, parts // 2) + w_both.shape, w_both.dtype),
            jax.ShapeDtypeStruct((blocks_here, 1, width), jnp.float32),
        ],
        in_specs=[smem, smem, vmem, vmem, vmem],
        out_specs=[vmem] * 4,
        scratch_shapes=[
            pltpu.VMEM((blocks_here, cols, width), jnp.bfloat16),
            pltpu.SemaphoreType.DMA((4, parts)),
            pltpu.SemaphoreType.DMA((4, parts)),
        ],
        compiler_params=pltpu.CompilerParams(collective_id=0, has_side_effects=True),
    )(ids_flat, counts, feat_t, tiles, w_both)


def shards(features, w_self, w_neigh, bias, d_out, nbr_ids, nbr_count, tiles):
    node_total, cols = features.shape
    hidden = w_self.shape[1]
    block_size = tiles.shape[3]
    blocks_here = nbr_ids.shape[0]
    all_blocks = node_total // block_size
    node_group = lax.axis_index("node")
    feat_index = lax.axis_index("feat")
    feat_parts = lax.axis_size("feat")
    per = blocks_here // feat_parts
    own_nodes = per * block_size

    feat_t = features.reshape(all_blocks, block_size, cols).transpose(0, 2, 1)
    ids_flat = nbr_ids.reshape(-1)

    w_both = jnp.concatenate([w_self, w_neigh], axis=1)
    feat_got, nm_got, w_all, deg_blocks = forward_exchange(
        ids_flat, nbr_count, feat_t, tiles, w_both, feat_parts
    )
    w_all = w_all.transpose(1, 0, 2, 3).reshape(feat_parts * cols, 2 * hidden)
    w_self_all = w_all[:, :hidden]
    w_neigh_all = w_all[:, hidden:]
    own_feat = feat_got.transpose(1, 3, 0, 2).reshape(own_nodes, feat_parts * cols)
    own_nm = nm_got.transpose(1, 3, 0, 2).reshape(own_nodes, feat_parts * cols)

    pre_act = (
        jnp.dot(own_feat, w_self_all, preferred_element_type=jnp.float32)
        + jnp.dot(own_nm, w_neigh_all, preferred_element_type=jnp.float32)
        + bias
    )
    activated = jax.nn.elu(pre_act).astype(jnp.bfloat16)
    elu_slope = jnp.where(pre_act > 0, 1.0, jnp.exp(jnp.minimum(pre_act, 0.0)))
    dpre = (d_out.astype(jnp.float32) * elu_slope).astype(jnp.bfloat16)

    contract_cols = (((1,), (1,)), ((), ()))
    d_self_t = lax.dot_general(
        w_self_all, dpre, contract_cols, preferred_element_type=jnp.float32
    ).astype(jnp.bfloat16)
    d_neigh_t = lax.dot_general(
        w_neigh_all, dpre, contract_cols, preferred_element_type=jnp.float32
    ).astype(jnp.bfloat16)
    own_deg = lax.dynamic_slice_in_dim(deg_blocks, feat_index * per, per, 0).reshape(1, -1)
    d_scaled_t = (d_neigh_t.astype(jnp.float32) / jnp.maximum(own_deg, 1.0)).astype(jnp.bfloat16)

    contract_rows = (((0,), (0,)), ((), ()))
    part = jnp.concatenate(
        [
            lax.dot_general(own_feat, dpre, contract_rows, preferred_element_type=jnp.float32),
            lax.dot_general(own_nm, dpre, contract_rows, preferred_element_type=jnp.float32),
        ],
        axis=1,
    )
    part_got = lax.all_to_all(part.reshape(feat_parts, cols, 2 * hidden), "feat", 0, 0, tiled=True)
    grads = jnp.sum(lax.all_gather(jnp.sum(part_got, axis=0), "node"), axis=0)
    grad_scale = 1.0 / math.sqrt(node_total)
    grad_self = grads[:, :hidden] * grad_scale
    grad_neigh = grads[:, hidden:] * grad_scale

    back = (
        jnp.stack([d_self_t, d_scaled_t], axis=0)
        .reshape(2, feat_parts, cols, per, block_size)
        .transpose(1, 3, 0, 2, 4)
    )
    got_back = lax.all_to_all(back, "feat", 0, 0, tiled=True).reshape(blocks_here, 2, cols, block_size)
    d_self_blocks = got_back[:, 0]
    d_scaled_blocks = got_back[:, 1]

    grad_all = aggregate_backward(ids_flat, nbr_count, d_scaled_blocks, tiles, all_blocks)
    grad_group = lax.psum_scatter(grad_all, "node", scatter_dimension=0, tiled=True)
    grad_group = grad_group + d_self_blocks.astype(jnp.float32)
    grad_features = grad_group.transpose(0, 2, 1).reshape(-1, cols)
    return (activated, grad_features, grad_self, grad_neigh)


def solution(mesh):
    placed = (
        P(None, "feat"),
        P("feat", None),
        P("feat", None),
        P(),
        P(("node", "feat"), None),
        P("node", None),
        P("node"),
        P("node", None, None, None),
    )
    return jax.shard_map(
        shards,
        mesh=mesh,
        in_specs=placed,
        out_specs=(P(("node", "feat"), None), P("node", "feat"), P("feat", None), P("feat", None)),
        check_vma=False,
    )
```

```python
import functools
import math

import jax
import jax.numpy as jnp
from jax import lax
from jax.experimental import pallas as pl
from jax.experimental.pallas import tpu as pltpu
from jax.sharding import PartitionSpec as P

ROWS_PER_STEP = 16


def unpack_tile(words):
    nwords, width = words.shape
    shifts = lax.broadcasted_iota(jnp.int32, (16, width), 0)
    rows = [
        jnp.bitwise_and(jnp.right_shift(jnp.broadcast_to(words[w : w + 1, :], (16, width)), shifts), 1)
        for w in range(nwords)
    ]
    return jnp.concatenate(rows, axis=0).astype(jnp.float32).astype(jnp.bfloat16)


def forward_kernel(ids_ref, cnt_ref, feat_ref, tiles_ref, nm_ref, deg_ref):
    step = pl.program_id(0)
    rows_here, slots = tiles_ref.shape[0], tiles_ref.shape[1]
    cols, width = feat_ref.shape[1], feat_ref.shape[2]

    def row(r, carry):
        b = step * rows_here + r
        cnt = cnt_ref[b]
        adjs, lhs = [], []
        for s in range(slots):
            live = jnp.where(s < cnt, 1.0, 0.0)
            adjs.append(unpack_tile(tiles_ref[r, s]))
            src = feat_ref[ids_ref[b * slots + s]].astype(jnp.float32) * live
            lhs.append(
                jnp.concatenate([src, jnp.full((cols, width), live, jnp.float32)], axis=0).astype(
                    jnp.bfloat16
                )
            )
        out = lax.dot_general(
            jnp.concatenate(lhs, axis=1),
            jnp.concatenate(adjs, axis=1),
            (((1,), (1,)), ((), ())),
            preferred_element_type=jnp.float32,
        )
        deg = out[cols : cols + 1, :]
        nm_ref[r] = (out[:cols, :] / jnp.maximum(deg, 1.0)).astype(nm_ref.dtype)
        deg_ref[r] = deg
        return carry

    lax.fori_loop(0, rows_here, row, 0)


def backward_kernel(ids_ref, cnt_ref, ds_ref, tiles_ref, g_ref):
    step = pl.program_id(0)
    rows_here, slots = tiles_ref.shape[0], tiles_ref.shape[1]
    width = tiles_ref.shape[3]

    @pl.when(step == 0)
    def _():
        g_ref[...] = jnp.zeros_like(g_ref)

    def row(r, carry):
        b = step * rows_here + r
        cnt = cnt_ref[b]
        adjcat = jnp.concatenate([unpack_tile(tiles_ref[r, s]) for s in range(slots)], axis=1)
        res = jnp.dot(ds_ref[r], adjcat, preferred_element_type=jnp.float32)
        for s in range(slots):
            live = jnp.where(s < cnt, 1.0, 0.0)
            t = ids_ref[b * slots + s]
            g_ref[t] = g_ref[t] + res[:, s * width : (s + 1) * width] * live
        return carry

    lax.fori_loop(0, rows_here, row, 0)


def aggregate_forward(ids_flat, counts, feat_t, tiles):
    blocks_here, slots, nwords, width = tiles.shape
    all_blocks, cols, _ = feat_t.shape
    rows = ROWS_PER_STEP
    return pl.pallas_call(
        forward_kernel,
        grid_spec=pltpu.PrefetchScalarGridSpec(
            num_scalar_prefetch=2,
            grid=(blocks_here // rows,),
            in_specs=[
                pl.BlockSpec((all_blocks, cols, width), lambda i, *_: (0, 0, 0)),
                pl.BlockSpec((rows, slots, nwords, width), lambda i, *_: (i, 0, 0, 0)),
            ],
            out_specs=[
                pl.BlockSpec((rows, cols, width), lambda i, *_: (i, 0, 0)),
                pl.BlockSpec((rows, 1, width), lambda i, *_: (i, 0, 0)),
            ],
        ),
        out_shape=[
            jax.ShapeDtypeStruct((blocks_here, cols, width), jnp.bfloat16),
            jax.ShapeDtypeStruct((blocks_here, 1, width), jnp.float32),
        ],
        compiler_params=pltpu.CompilerParams(dimension_semantics=("arbitrary",)),
    )(ids_flat, counts, feat_t, tiles)


def aggregate_backward(ids_flat, counts, ds_blocks, tiles, all_blocks):
    blocks_here, slots, nwords, width = tiles.shape
    cols = ds_blocks.shape[1]
    rows = ROWS_PER_STEP
    return pl.pallas_call(
        backward_kernel,
        grid_spec=pltpu.PrefetchScalarGridSpec(
            num_scalar_prefetch=2,
            grid=(blocks_here // rows,),
            in_specs=[
                pl.BlockSpec((rows, cols, width), lambda i, *_: (i, 0, 0)),
                pl.BlockSpec((rows, slots, nwords, width), lambda i, *_: (i, 0, 0, 0)),
            ],
            out_specs=pl.BlockSpec((all_blocks, cols, width), lambda i, *_: (0, 0, 0)),
        ),
        out_shape=jax.ShapeDtypeStruct((all_blocks, cols, width), jnp.float32),
        compiler_params=pltpu.CompilerParams(dimension_semantics=("arbitrary",)),
    )(ids_flat, counts, ds_blocks, tiles)


def exchange_kernel(parts, kinds, *refs):
    n_in = len(kinds)
    ins, outs = refs[:n_in], refs[n_in : 2 * n_in]
    send_sems, recv_sems = refs[2 * n_in :]
    me = lax.axis_index("feat")
    mesh_id = pl.DeviceIdType.MESH

    barrier = pltpu.get_barrier_semaphore()

    def greet(k, carry):
        peer = lax.rem(me + k, parts)
        pl.semaphore_signal(barrier, 1, device_id={"feat": peer}, device_id_type=mesh_id)
        return carry

    lax.fori_loop(1, parts, greet, 0)
    pl.semaphore_wait(barrier, parts - 1)

    def copy(i, k):
        peer = lax.rem(me + k, parts)
        src = ins[i] if kinds[i] else ins[i].at[peer]
        return pltpu.make_async_remote_copy(
            src_ref=src,
            dst_ref=outs[i].at[me],
            send_sem=send_sems.at[i, k],
            recv_sem=recv_sems.at[i, k],
            device_id={"feat": peer},
            device_id_type=mesh_id,
        )

    def start(k, carry):
        for i in range(n_in):
            copy(i, k).start()
        return carry

    lax.fori_loop(1, parts, start, 0)
    for i in range(n_in):
        outs[i][me] = ins[i][...] if kinds[i] else ins[i][me]

    def finish(k, carry):
        for i in range(n_in):
            copy(i, k).wait()
        return carry

    lax.fori_loop(1, parts, finish, 0)


def exchange(arrays, kinds, parts, cid):
    out_shapes = [
        jax.ShapeDtypeStruct(((parts,) + x.shape) if kind else x.shape, x.dtype)
        for x, kind in zip(arrays, kinds)
    ]
    vmem = pl.BlockSpec(memory_space=pltpu.VMEM)
    return pl.pallas_call(
        functools.partial(exchange_kernel, parts, tuple(kinds)),
        out_shape=out_shapes,
        in_specs=[vmem] * len(arrays),
        out_specs=[vmem] * len(arrays),
        scratch_shapes=[
            pltpu.SemaphoreType.DMA((len(arrays), parts)),
            pltpu.SemaphoreType.DMA((len(arrays), parts)),
        ],
        compiler_params=pltpu.CompilerParams(collective_id=cid, has_side_effects=True),
    )(*arrays)


def forward_exchange_kernel(
    parts, ids_ref, cnt_ref, feat_ref, tiles_ref, w_ref,
    feat_out, nm_out, w_out, deg_ref, nm_scr, send_sems, recv_sems,
):
    me = lax.axis_index("feat")
    group = lax.axis_index("node")
    blocks_here, slots = tiles_ref.shape[0], tiles_ref.shape[1]
    cols, width = feat_ref.shape[1], feat_ref.shape[2]
    per = blocks_here // parts
    mesh_id = pl.DeviceIdType.MESH

    barrier = pltpu.get_barrier_semaphore()

    def greet(k, carry):
        peer = lax.rem(me + k, parts)
        pl.semaphore_signal(barrier, 1, device_id={"feat": peer}, device_id_type=mesh_id)
        return carry

    lax.fori_loop(1, parts, greet, 0)
    pl.semaphore_wait(barrier, parts - 1)

    half = parts // 2
    par = lax.rem(me, 2)
    sibling = me + 1 - 2 * par

    def copy(i, k):
        if i == 0:
            peer = lax.rem(me + 2 * k, parts)
            src, dst = w_ref, w_out.at[par, me // 2]
        elif i == 1:
            peer = lax.rem(me + k, parts)
            src = feat_ref.at[pl.ds(group * blocks_here + peer * per, per)]
            dst = feat_out.at[me]
        else:
            peer = lax.rem(me + k, parts)
            src, dst = nm_scr.at[pl.ds(peer * per, per)], nm_out.at[me]
        return pltpu.make_async_remote_copy(
            src_ref=src,
            dst_ref=dst,
            send_sem=send_sems.at[i, k],
            recv_sem=recv_sems.at[i, k],
            device_id={"feat": peer},
            device_id_type=mesh_id,
        )

    def start_weights(k, carry):
        copy(0, k).start()
        return carry

    def start_feat(k, carry):
        copy(1, k).start()
        return carry

    lax.fori_loop(1, half, start_weights, 0)
    lax.fori_loop(1, parts, start_feat, 0)
    own_w = pltpu.make_async_copy(w_ref, w_out.at[par, me // 2], send_sems.at[3, 0])
    own_w.start()
    feat_out[me] = feat_ref[pl.ds(group * blocks_here + me * per, per)]

    def row(b, carry):
        cnt = cnt_ref[b]
        adjs, lhs = [], []
        for s in range(slots):
            live = jnp.where(s < cnt, 1.0, 0.0)
            adjs.append(unpack_tile(tiles_ref[b, s]))
            src = feat_ref[ids_ref[b * slots + s]].astype(jnp.float32) * live
            lhs.append(
                jnp.concatenate([src, jnp.full((cols, width), live, jnp.float32)], axis=0).astype(
                    jnp.bfloat16
                )
            )
        out = lax.dot_general(
            jnp.concatenate(lhs, axis=1),
            jnp.concatenate(adjs, axis=1),
            (((1,), (1,)), ((), ())),
            preferred_element_type=jnp.float32,
        )
        deg = out[cols : cols + 1, :]
        nm_scr[b] = (out[:cols, :] / jnp.maximum(deg, 1.0)).astype(nm_scr.dtype)
        deg_ref[b] = deg
        k = lax.rem(b // per - me + parts, parts)

        @pl.when(jnp.logical_and(k != 0, lax.rem(b + 1, per) == 0))
        def _():
            copy(2, k).start()

        return carry

    lax.fori_loop(0, blocks_here, row, 0)

    def finish_weights(k, carry):
        copy(0, k).wait()
        return carry

    lax.fori_loop(1, half, finish_weights, 0)
    own_w.wait()
    to_sibling = pltpu.make_async_remote_copy(
        src_ref=w_out.at[par],
        dst_ref=w_out.at[par],
        send_sem=send_sems.at[3, 1],
        recv_sem=recv_sems.at[3, 1],
        device_id={"feat": sibling},
        device_id_type=mesh_id,
    )
    to_sibling.start()

    nm_out[me] = nm_scr[pl.ds(me * per, per)]

    def finish(k, carry):
        copy(1, k).wait()
        copy(2, k).wait()
        return carry

    lax.fori_loop(1, parts, finish, 0)
    to_sibling.wait()


def forward_exchange(ids_flat, counts, feat_t, tiles, w_both, parts):
    blocks_here, slots, nwords, width = tiles.shape
    all_blocks, cols, _ = feat_t.shape
    per = blocks_here // parts
    vmem = pl.BlockSpec(memory_space=pltpu.VMEM)
    smem = pl.BlockSpec(memory_space=pltpu.SMEM)
    return pl.pallas_call(
        functools.partial(forward_exchange_kernel, parts),
        out_shape=[
            jax.ShapeDtypeStruct((parts, per, cols, width), jnp.bfloat16),
            jax.ShapeDtypeStruct((parts, per, cols, width), jnp.bfloat16),
            jax.ShapeDtypeStruct((2, parts // 2) + w_both.shape, w_both.dtype),
            jax.ShapeDtypeStruct((blocks_here, 1, width), jnp.float32),
        ],
        in_specs=[smem, smem, vmem, vmem, vmem],
        out_specs=[vmem] * 4,
        scratch_shapes=[
            pltpu.VMEM((blocks_here, cols, width), jnp.bfloat16),
            pltpu.SemaphoreType.DMA((4, parts)),
            pltpu.SemaphoreType.DMA((4, parts)),
        ],
        compiler_params=pltpu.CompilerParams(collective_id=0, has_side_effects=True),
    )(ids_flat, counts, feat_t, tiles, w_both)


def shards(features, w_self, w_neigh, bias, d_out, nbr_ids, nbr_count, tiles):
    node_total, cols = features.shape
    hidden = w_self.shape[1]
    block_size = tiles.shape[3]
    blocks_here = nbr_ids.shape[0]
    all_blocks = node_total // block_size
    node_group = lax.axis_index("node")
    feat_index = lax.axis_index("feat")
    feat_parts = lax.axis_size("feat")
    per = blocks_here // feat_parts
    own_nodes = per * block_size

    feat_t = features.reshape(all_blocks, block_size, cols).transpose(0, 2, 1)
    ids_flat = nbr_ids.reshape(-1)

    w_both = jnp.concatenate([w_self, w_neigh], axis=1)
    feat_got, nm_got, w_all, deg_blocks = forward_exchange(
        ids_flat, nbr_count, feat_t, tiles, w_both, feat_parts
    )
    w_all = w_all.transpose(1, 0, 2, 3).reshape(feat_parts * cols, 2 * hidden)
    w_self_all = w_all[:, :hidden]
    w_neigh_all = w_all[:, hidden:]
    own_feat = feat_got.transpose(1, 3, 0, 2).reshape(own_nodes, feat_parts * cols)
    own_nm = nm_got.transpose(1, 3, 0, 2).reshape(own_nodes, feat_parts * cols)

    pre_act = (
        jnp.dot(own_feat, w_self_all, preferred_element_type=jnp.float32)
        + jnp.dot(own_nm, w_neigh_all, preferred_element_type=jnp.float32)
        + bias
    )
    activated = jax.nn.elu(pre_act).astype(jnp.bfloat16)
    elu_slope = jnp.where(pre_act > 0, 1.0, jnp.exp(jnp.minimum(pre_act, 0.0)))
    dpre = (d_out.astype(jnp.float32) * elu_slope).astype(jnp.bfloat16)

    contract_cols = (((1,), (1,)), ((), ()))
    d_self_t = lax.dot_general(
        w_self_all, dpre, contract_cols, preferred_element_type=jnp.float32
    ).astype(jnp.bfloat16)
    d_neigh_t = lax.dot_general(
        w_neigh_all, dpre, contract_cols, preferred_element_type=jnp.float32
    ).astype(jnp.bfloat16)
    own_deg = lax.dynamic_slice_in_dim(deg_blocks, feat_index * per, per, 0).reshape(1, -1)
    d_scaled_t = (d_neigh_t.astype(jnp.float32) / jnp.maximum(own_deg, 1.0)).astype(jnp.bfloat16)

    contract_rows = (((0,), (0,)), ((), ()))
    part = jnp.concatenate(
        [
            lax.dot_general(own_feat, dpre, contract_rows, preferred_element_type=jnp.float32),
            lax.dot_general(own_nm, dpre, contract_rows, preferred_element_type=jnp.float32),
        ],
        axis=1,
    )
    part_got = lax.all_to_all(part.reshape(feat_parts, cols, 2 * hidden), "feat", 0, 0, tiled=True)
    grads = jnp.sum(lax.all_gather(jnp.sum(part_got, axis=0), "node"), axis=0)
    grad_scale = 1.0 / math.sqrt(node_total)
    grad_self = grads[:, :hidden] * grad_scale
    grad_neigh = grads[:, hidden:] * grad_scale

    back = (
        jnp.stack([d_self_t, d_scaled_t], axis=0)
        .reshape(2, feat_parts, cols, per, block_size)
        .transpose(1, 3, 0, 2, 4)
    )
    back = back.reshape(feat_parts, per * 2 * cols, block_size)
    got_back = lax.all_to_all(back, "feat", 0, 0, tiled=True).reshape(blocks_here, 2, cols, block_size)
    d_self_blocks = got_back[:, 0]
    d_scaled_blocks = got_back[:, 1]

    grad_all = aggregate_backward(ids_flat, nbr_count, d_scaled_blocks, tiles, all_blocks)
    grad_group = lax.psum_scatter(grad_all, "node", scatter_dimension=0, tiled=True)
    grad_group = grad_group + d_self_blocks.astype(jnp.float32)
    grad_features = grad_group.transpose(0, 2, 1).reshape(-1, cols)
    return (activated, grad_features, grad_self, grad_neigh)


def solution(mesh):
    placed = (
        P(None, "feat"),
        P("feat", None),
        P("feat", None),
        P(),
        P(("node", "feat"), None),
        P("node", None),
        P("node"),
        P("node", None, None, None),
    )
    return jax.shard_map(
        shards,
        mesh=mesh,
        in_specs=placed,
        out_specs=(P(("node", "feat"), None), P("node", "feat"), P("feat", None), P("feat", None)),
        check_vma=False,
    )
```

```python
import functools
import math

import jax
import jax.numpy as jnp
from jax import lax
from jax.experimental import pallas as pl
from jax.experimental.pallas import tpu as pltpu
from jax.sharding import PartitionSpec as P

ROWS_PER_STEP = 16


def unpack_tile(words):
    nwords, width = words.shape
    shifts = lax.broadcasted_iota(jnp.int32, (16, width), 0)
    rows = [
        jnp.bitwise_and(jnp.right_shift(jnp.broadcast_to(words[w : w + 1, :], (16, width)), shifts), 1)
        for w in range(nwords)
    ]
    return jnp.concatenate(rows, axis=0).astype(jnp.float32).astype(jnp.bfloat16)


def forward_kernel(ids_ref, cnt_ref, feat_ref, tiles_ref, nm_ref, deg_ref):
    step = pl.program_id(0)
    rows_here, slots = tiles_ref.shape[0], tiles_ref.shape[1]
    cols, width = feat_ref.shape[1], feat_ref.shape[2]

    def row(r, carry):
        b = step * rows_here + r
        cnt = cnt_ref[b]
        adjs, lhs = [], []
        for s in range(slots):
            live = jnp.where(s < cnt, 1.0, 0.0)
            adjs.append(unpack_tile(tiles_ref[r, s]))
            src = feat_ref[ids_ref[b * slots + s]].astype(jnp.float32) * live
            lhs.append(
                jnp.concatenate([src, jnp.full((cols, width), live, jnp.float32)], axis=0).astype(
                    jnp.bfloat16
                )
            )
        out = lax.dot_general(
            jnp.concatenate(lhs, axis=1),
            jnp.concatenate(adjs, axis=1),
            (((1,), (1,)), ((), ())),
            preferred_element_type=jnp.float32,
        )
        deg = out[cols : cols + 1, :]
        nm_ref[r] = (out[:cols, :] / jnp.maximum(deg, 1.0)).astype(nm_ref.dtype)
        deg_ref[r] = deg
        return carry

    lax.fori_loop(0, rows_here, row, 0)


def backward_kernel(ids_ref, cnt_ref, ds_ref, tiles_ref, g_ref):
    step = pl.program_id(0)
    rows_here, slots = tiles_ref.shape[0], tiles_ref.shape[1]
    width = tiles_ref.shape[3]

    @pl.when(step == 0)
    def _():
        g_ref[...] = jnp.zeros_like(g_ref)

    def row(r, carry):
        b = step * rows_here + r
        cnt = cnt_ref[b]
        adjcat = jnp.concatenate([unpack_tile(tiles_ref[r, s]) for s in range(slots)], axis=1)
        res = jnp.dot(ds_ref[r], adjcat, preferred_element_type=jnp.float32)
        for s in range(slots):
            live = jnp.where(s < cnt, 1.0, 0.0)
            t = ids_ref[b * slots + s]
            g_ref[t] = g_ref[t] + res[:, s * width : (s + 1) * width] * live
        return carry

    lax.fori_loop(0, rows_here, row, 0)


def aggregate_forward(ids_flat, counts, feat_t, tiles):
    blocks_here, slots, nwords, width = tiles.shape
    all_blocks, cols, _ = feat_t.shape
    rows = ROWS_PER_STEP
    return pl.pallas_call(
        forward_kernel,
        grid_spec=pltpu.PrefetchScalarGridSpec(
            num_scalar_prefetch=2,
            grid=(blocks_here // rows,),
            in_specs=[
                pl.BlockSpec((all_blocks, cols, width), lambda i, *_: (0, 0, 0)),
                pl.BlockSpec((rows, slots, nwords, width), lambda i, *_: (i, 0, 0, 0)),
            ],
            out_specs=[
                pl.BlockSpec((rows, cols, width), lambda i, *_: (i, 0, 0)),
                pl.BlockSpec((rows, 1, width), lambda i, *_: (i, 0, 0)),
            ],
        ),
        out_shape=[
            jax.ShapeDtypeStruct((blocks_here, cols, width), jnp.bfloat16),
            jax.ShapeDtypeStruct((blocks_here, 1, width), jnp.float32),
        ],
        compiler_params=pltpu.CompilerParams(dimension_semantics=("arbitrary",)),
    )(ids_flat, counts, feat_t, tiles)


def aggregate_backward(ids_flat, counts, ds_blocks, tiles, all_blocks):
    blocks_here, slots, nwords, width = tiles.shape
    cols = ds_blocks.shape[1]
    rows = ROWS_PER_STEP
    return pl.pallas_call(
        backward_kernel,
        grid_spec=pltpu.PrefetchScalarGridSpec(
            num_scalar_prefetch=2,
            grid=(blocks_here // rows,),
            in_specs=[
                pl.BlockSpec((rows, cols, width), lambda i, *_: (i, 0, 0)),
                pl.BlockSpec((rows, slots, nwords, width), lambda i, *_: (i, 0, 0, 0)),
            ],
            out_specs=pl.BlockSpec((all_blocks, cols, width), lambda i, *_: (0, 0, 0)),
        ),
        out_shape=jax.ShapeDtypeStruct((all_blocks, cols, width), jnp.float32),
        compiler_params=pltpu.CompilerParams(dimension_semantics=("arbitrary",)),
    )(ids_flat, counts, ds_blocks, tiles)


def exchange_kernel(parts, kinds, *refs):
    n_in = len(kinds)
    ins, outs = refs[:n_in], refs[n_in : 2 * n_in]
    send_sems, recv_sems = refs[2 * n_in :]
    me = lax.axis_index("feat")
    mesh_id = pl.DeviceIdType.MESH

    barrier = pltpu.get_barrier_semaphore()

    def greet(k, carry):
        peer = lax.rem(me + k, parts)
        pl.semaphore_signal(barrier, 1, device_id={"feat": peer}, device_id_type=mesh_id)
        return carry

    lax.fori_loop(1, parts, greet, 0)
    pl.semaphore_wait(barrier, parts - 1)

    def copy(i, k):
        peer = lax.rem(me + k, parts)
        src = ins[i] if kinds[i] else ins[i].at[peer]
        return pltpu.make_async_remote_copy(
            src_ref=src,
            dst_ref=outs[i].at[me],
            send_sem=send_sems.at[i, k],
            recv_sem=recv_sems.at[i, k],
            device_id={"feat": peer},
            device_id_type=mesh_id,
        )

    def start(k, carry):
        for i in range(n_in):
            copy(i, k).start()
        return carry

    lax.fori_loop(1, parts, start, 0)
    for i in range(n_in):
        outs[i][me] = ins[i][...] if kinds[i] else ins[i][me]

    def finish(k, carry):
        for i in range(n_in):
            copy(i, k).wait()
        return carry

    lax.fori_loop(1, parts, finish, 0)


def exchange(arrays, kinds, parts, cid):
    out_shapes = [
        jax.ShapeDtypeStruct(((parts,) + x.shape) if kind else x.shape, x.dtype)
        for x, kind in zip(arrays, kinds)
    ]
    vmem = pl.BlockSpec(memory_space=pltpu.VMEM)
    return pl.pallas_call(
        functools.partial(exchange_kernel, parts, tuple(kinds)),
        out_shape=out_shapes,
        in_specs=[vmem] * len(arrays),
        out_specs=[vmem] * len(arrays),
        scratch_shapes=[
            pltpu.SemaphoreType.DMA((len(arrays), parts)),
            pltpu.SemaphoreType.DMA((len(arrays), parts)),
        ],
        compiler_params=pltpu.CompilerParams(collective_id=cid, has_side_effects=True),
    )(*arrays)


def forward_exchange_kernel(
    parts, ids_ref, cnt_ref, feat_ref, tiles_ref, w_ref,
    feat_out, nm_out, w_out, deg_ref, nm_scr, send_sems, recv_sems,
):
    me = lax.axis_index("feat")
    group = lax.axis_index("node")
    blocks_here, slots = tiles_ref.shape[0], tiles_ref.shape[1]
    cols, width = feat_ref.shape[1], feat_ref.shape[2]
    per = blocks_here // parts
    mesh_id = pl.DeviceIdType.MESH

    barrier = pltpu.get_barrier_semaphore()

    def greet(k, carry):
        peer = lax.rem(me + k, parts)
        pl.semaphore_signal(barrier, 1, device_id={"feat": peer}, device_id_type=mesh_id)
        return carry

    lax.fori_loop(1, parts, greet, 0)
    pl.semaphore_wait(barrier, parts - 1)

    half = parts // 2
    par = lax.rem(me, 2)
    sibling = me + 1 - 2 * par

    def copy(i, k):
        if i == 0:
            peer = lax.rem(me + 2 * k, parts)
            src, dst = w_ref, w_out.at[par, me // 2]
        elif i == 1:
            peer = lax.rem(me + k, parts)
            src = feat_ref.at[pl.ds(group * blocks_here + peer * per, per)]
            dst = feat_out.at[me]
        else:
            peer = lax.rem(me + k, parts)
            src, dst = nm_scr.at[pl.ds(peer * per, per)], nm_out.at[me]
        return pltpu.make_async_remote_copy(
            src_ref=src,
            dst_ref=dst,
            send_sem=send_sems.at[i, k],
            recv_sem=recv_sems.at[i, k],
            device_id={"feat": peer},
            device_id_type=mesh_id,
        )

    def start_weights(k, carry):
        copy(0, k).start()
        return carry

    def start_feat(k, carry):
        copy(1, k).start()
        return carry

    lax.fori_loop(1, half, start_weights, 0)
    lax.fori_loop(1, parts, start_feat, 0)
    own_w = pltpu.make_async_copy(w_ref, w_out.at[par, me // 2], send_sems.at[3, 0])
    own_w.start()
    feat_out[me] = feat_ref[pl.ds(group * blocks_here + me * per, per)]

    def row(b, carry):
        cnt = cnt_ref[b]
        adjs, lhs = [], []
        for s in range(slots):
            live = jnp.where(s < cnt, 1.0, 0.0)
            adjs.append(unpack_tile(tiles_ref[b, s]))
            src = feat_ref[ids_ref[b * slots + s]].astype(jnp.float32) * live
            lhs.append(
                jnp.concatenate([src, jnp.full((cols, width), live, jnp.float32)], axis=0).astype(
                    jnp.bfloat16
                )
            )
        out = lax.dot_general(
            jnp.concatenate(lhs, axis=1),
            jnp.concatenate(adjs, axis=1),
            (((1,), (1,)), ((), ())),
            preferred_element_type=jnp.float32,
        )
        deg = out[cols : cols + 1, :]
        nm_scr[b] = (out[:cols, :] / jnp.maximum(deg, 1.0)).astype(nm_scr.dtype)
        deg_ref[b] = deg
        k = lax.rem(b // per - me + parts, parts)

        @pl.when(jnp.logical_and(k != 0, lax.rem(b + 1, per) == 0))
        def _():
            copy(2, k).start()

        return carry

    lax.fori_loop(0, blocks_here, row, 0)

    def finish_weights(k, carry):
        copy(0, k).wait()
        return carry

    lax.fori_loop(1, half, finish_weights, 0)
    own_w.wait()
    to_sibling = pltpu.make_async_remote_copy(
        src_ref=w_out.at[par],
        dst_ref=w_out.at[par],
        send_sem=send_sems.at[3, 1],
        recv_sem=recv_sems.at[3, 1],
        device_id={"feat": sibling},
        device_id_type=mesh_id,
    )
    to_sibling.start()

    nm_out[me] = nm_scr[pl.ds(me * per, per)]

    def finish(k, carry):
        copy(1, k).wait()
        copy(2, k).wait()
        return carry

    lax.fori_loop(1, parts, finish, 0)
    to_sibling.wait()


def forward_exchange(ids_flat, counts, feat_t, tiles, w_both, parts):
    blocks_here, slots, nwords, width = tiles.shape
    all_blocks, cols, _ = feat_t.shape
    per = blocks_here // parts
    vmem = pl.BlockSpec(memory_space=pltpu.VMEM)
    smem = pl.BlockSpec(memory_space=pltpu.SMEM)
    return pl.pallas_call(
        functools.partial(forward_exchange_kernel, parts),
        out_shape=[
            jax.ShapeDtypeStruct((parts, per, cols, width), jnp.bfloat16),
            jax.ShapeDtypeStruct((parts, per, cols, width), jnp.bfloat16),
            jax.ShapeDtypeStruct((2, parts // 2) + w_both.shape, w_both.dtype),
            jax.ShapeDtypeStruct((blocks_here, 1, width), jnp.float32),
        ],
        in_specs=[smem, smem, vmem, vmem, vmem],
        out_specs=[vmem] * 4,
        scratch_shapes=[
            pltpu.VMEM((blocks_here, cols, width), jnp.bfloat16),
            pltpu.SemaphoreType.DMA((4, parts)),
            pltpu.SemaphoreType.DMA((4, parts)),
        ],
        compiler_params=pltpu.CompilerParams(collective_id=0, has_side_effects=True),
    )(ids_flat, counts, feat_t, tiles, w_both)


def shards(features, w_self, w_neigh, bias, d_out, nbr_ids, nbr_count, tiles):
    node_total, cols = features.shape
    hidden = w_self.shape[1]
    block_size = tiles.shape[3]
    blocks_here = nbr_ids.shape[0]
    all_blocks = node_total // block_size
    node_group = lax.axis_index("node")
    feat_index = lax.axis_index("feat")
    feat_parts = lax.axis_size("feat")
    per = blocks_here // feat_parts
    own_nodes = per * block_size

    feat_t = features.reshape(all_blocks, block_size, cols).transpose(0, 2, 1)
    ids_flat = nbr_ids.reshape(-1)

    w_both = jnp.concatenate([w_self, w_neigh], axis=1)
    feat_got, nm_got, w_all, deg_blocks = forward_exchange(
        ids_flat, nbr_count, feat_t, tiles, w_both, feat_parts
    )
    w_all = w_all.transpose(1, 0, 2, 3).reshape(feat_parts * cols, 2 * hidden)
    w_self_all = w_all[:, :hidden]
    w_neigh_all = w_all[:, hidden:]
    own_feat = feat_got.transpose(1, 3, 0, 2).reshape(own_nodes, feat_parts * cols)
    own_nm = nm_got.transpose(1, 3, 0, 2).reshape(own_nodes, feat_parts * cols)

    pre_act = (
        jnp.dot(own_feat, w_self_all, preferred_element_type=jnp.float32)
        + jnp.dot(own_nm, w_neigh_all, preferred_element_type=jnp.float32)
        + bias
    )
    activated = jax.nn.elu(pre_act).astype(jnp.bfloat16)
    elu_slope = jnp.where(pre_act > 0, 1.0, jnp.exp(jnp.minimum(pre_act, 0.0)))
    dpre = (d_out.astype(jnp.float32) * elu_slope).astype(jnp.bfloat16)

    contract_cols = (((1,), (1,)), ((), ()))
    d_self_t = lax.dot_general(
        w_self_all, dpre, contract_cols, preferred_element_type=jnp.float32
    ).astype(jnp.bfloat16)
    d_neigh_t = lax.dot_general(
        w_neigh_all, dpre, contract_cols, preferred_element_type=jnp.float32
    ).astype(jnp.bfloat16)
    own_deg = lax.dynamic_slice_in_dim(deg_blocks, feat_index * per, per, 0).reshape(1, -1)
    d_scaled_t = (d_neigh_t.astype(jnp.float32) / jnp.maximum(own_deg, 1.0)).astype(jnp.bfloat16)

    contract_rows = (((0,), (0,)), ((), ()))
    part = jnp.concatenate(
        [
            lax.dot_general(own_feat, dpre, contract_rows, preferred_element_type=jnp.float32),
            lax.dot_general(own_nm, dpre, contract_rows, preferred_element_type=jnp.float32),
        ],
        axis=1,
    )
    d_self_rows = d_self_t.astype(jnp.float32).reshape(feat_parts, cols, own_nodes)
    late = jnp.concatenate([part.reshape(feat_parts, cols, 2 * hidden), d_self_rows], axis=2)
    late_got = lax.all_to_all(late, "feat", 0, 0, tiled=True)
    part_got = late_got[:, :, : 2 * hidden]
    d_self_blocks = (
        late_got[:, :, 2 * hidden :]
        .astype(jnp.bfloat16)
        .reshape(feat_parts, cols, per, block_size)
        .transpose(0, 2, 1, 3)
        .reshape(blocks_here, cols, block_size)
    )
    grads = jnp.sum(lax.all_gather(jnp.sum(part_got, axis=0), "node"), axis=0)
    grad_scale = 1.0 / math.sqrt(node_total)
    grad_self = grads[:, :hidden] * grad_scale
    grad_neigh = grads[:, hidden:] * grad_scale

    back = d_scaled_t.reshape(feat_parts, cols, per, block_size).transpose(0, 2, 1, 3)
    d_scaled_blocks = lax.all_to_all(back, "feat", 0, 0, tiled=True).reshape(
        blocks_here, cols, block_size
    )

    grad_all = aggregate_backward(ids_flat, nbr_count, d_scaled_blocks, tiles, all_blocks)
    grad_group = lax.psum_scatter(grad_all, "node", scatter_dimension=0, tiled=True)
    grad_group = grad_group + d_self_blocks.astype(jnp.float32)
    grad_features = grad_group.transpose(0, 2, 1).reshape(-1, cols)
    return (activated, grad_features, grad_self, grad_neigh)


def solution(mesh):
    placed = (
        P(None, "feat"),
        P("feat", None),
        P("feat", None),
        P(),
        P(("node", "feat"), None),
        P("node", None),
        P("node"),
        P("node", None, None, None),
    )
    return jax.shard_map(
        shards,
        mesh=mesh,
        in_specs=placed,
        out_specs=(P(("node", "feat"), None), P("node", "feat"), P("feat", None), P("feat", None)),
        check_vma=False,
    )
```
